32 devices in a mesh: seq: 8 (over z, y), head: 4 (over x, core).
Axes of the slice: x: 2, y: 2, z: 4, core: 2. Of those that a mesh axis runs over, the one named last changes fastest.
Arguments:
- hidden_in: bfloat16 [2048, 1024], P('seq'), may hold values from -6 to 6
- seg_ids: int32 [2048], replicated, may hold values from 0 to 3, never falling along the last dimension, each value on 1 to 1024 neighbouring positions
- norm_gain: float32 [2, 1024], replicated, may hold values from 0.5 to 1.5
- w_z: bfloat16 [2, 1024, 2048], P(None, None, 'head'), may hold values from -0.1875 to 0.1875
- w_x: bfloat16 [2, 1024, 2048], P(None, None, 'head'), may hold values from -0.1875 to 0.1875
- w_bc: bfloat16 [2, 1024, 256], replicated, may hold values from -0.1875 to 0.1875
- w_dt: bfloat16 [2, 1024, 32], P(None, None, 'head'), may hold values from -0.1875 to 0.1875
- conv_x_w: float32 [2, 4, 2048], P(None, None, 'head'), may hold values from -3 to 3
- conv_x_b: float32 [2, 2048], P(None, 'head'), may hold values from -3 to 3
- conv_bc_w: float32 [2, 4, 256], replicated, may hold values from -3 to 3
- conv_bc_b: float32 [2, 256], replicated, may hold values from -3 to 3
- dt_bias: float32 [2, 32], P(None, 'head'), may hold values from -4 to -1
- a_log: float32 [2, 32], P(None, 'head'), may hold values from -8 to 1
- d_skip: float32 [2, 32], P(None, 'head'), may hold values from 0.5 to 1.5
- gate_gain: float32 [2, 2048], P(None, 'head'), may hold values from 0.5 to 1.5
- w_out: bfloat16 [2, 2048, 1024], P(None, 'head'), may hold values from -0.125 to 0.125
- out_cot: float32 [2048, 1024], P('seq'), may hold values from -6 to 6
Outputs:
- hidden_out: bfloat16 [2048, 1024], P('seq')
- grad_in: float32 [2048, 1024], P('seq')
- g_norm_gain: float32 [2, 1024], P(None, 'seq')
- g_w_z: float32 [2, 1024, 2048], P(None, 'seq', 'head')
- g_w_x: float32 [2, 1024, 2048], P(None, 'seq', 'head')
- g_w_bc: float32 [2, 1024, 256], P(None, 'seq')
- g_w_dt: float32 [2, 1024, 32], P(None, 'seq', 'head')
- g_conv_x_w: float32 [2, 4, 2048], P(None, None, 'head')
- g_conv_x_b: float32 [2, 2048], P(None, 'head')
- g_conv_bc_w: float32 [2, 4, 256], replicated
- g_conv_bc_b: float32 [2, 256], replicated
- g_dt_bias: float32 [2, 32], P(None, 'head')
- g_a_log: float32 [2, 32], P(None, 'head')
- g_d_skip: float32 [2, 32], P(None, 'head')
- g_gate_gain: float32 [2, 2048], P(None, 'head')
- g_w_out: float32 [2, 2048, 1024], P(None, 'head', 'seq')
The draws below stay inside these ranges and needn't reach their ends.
Inputs may be any that keep to these rules, and one draw needn't show every extreme that they name: seg_ids never falls along the tokens; each document holds at most 1024 tokens and one holds exactly 1024.
All inputs are finite; a program needn't handle non-finite values.
Results may differ from the reference program's by a relative error of at most 0.012.
The reference program's roundings to bfloat16 on the way (of `normed`, `gated_normed` and `cot_b`) count: a program that leaves them out, or rounds other values in their place, can miss the bound.
Values sent between devices are 32-bit elements; how exact they have to be, the bound alone decides.
No kernel may reach another device: no remote copies, remote signals or barrier semaphores. Data moves between devices by JAX's collectives and lax.ppermute only.
A program may use at most 128 MiB of HBM per device.

```python
import math
import jax
import jax.numpy as jnp
import numpy as np
from jax import lax

D = 1024
INNER = 2048
NH = 32
HEADDIM = 64
STATE = 128
CONV = 4
SPAN = 256
LAYERS = 2
SEGMENTS = 4
TOKENS = 2048
MAX_DOC = 1024


def levels(stream_key, dims, split, least, top_value):
    factor_of, own = 1.0, jax.random.fold_in(stream_key, 6)
    for dim, shards_of in split:
        steps = jnp.exp(jax.random.uniform(jax.random.fold_in(own, dim), (shards_of,), jnp.float32, least / len(split), top_value / len(split)))
        factor_of = factor_of * jnp.repeat(steps, dims[dim] // shards_of).reshape([-1 if axis == dim else 1 for axis in range(len(dims))])
    return factor_of


def profile(count, total, bound, lean):
    portions = [(1 << 20) // math.isqrt(rank ** lean) + 1 for rank in range(2, count + 1)]
    surplus, given = total - bound - (count - 1), [1] * (count - 1)
    while surplus > 0:
        candidates = [i for i in range(count - 1) if given[i] < bound]
        mass, left = sum([portions[i] for i in candidates]), surplus
        for i in candidates:
            more = min(bound - given[i], max(1, left * portions[i] // mass), surplus)
            given[i] = given[i] + more
            surplus = surplus - more
    return np.array([bound] + given)


def ragged(own_key, number_of, total, bound, slope):
    if number_of == 2:
        one = jax.random.randint(own_key, (), max(1, total - bound), min(bound, total - 1) + 1)
        return jnp.stack([one, total - one])
    sizes = jnp.asarray(profile(number_of, total, bound, slope), jnp.int32)
    pairs = (number_of - 1) // 2
    source_of, taker = sizes[1:1 + 2 * pairs:2], sizes[2:2 + 2 * pairs:2]
    slack = jnp.minimum(source_of - 1, bound - taker)
    moved = jax.random.randint(jax.random.fold_in(own_key, 1), (pairs,), 0, 1 << 20) % (slack + 1)
    sizes = sizes.at[1:1 + 2 * pairs:2].set(source_of - moved).at[2:2 + 2 * pairs:2].set(taker + moved)
    return sizes[jax.random.permutation(jax.random.fold_in(own_key, 2), number_of)]


def normal_values(stream_key, dims, spread, most, shards=(), kind=jnp.bfloat16):
    values = jax.random.normal(stream_key, dims, jnp.float32) * spread
    if len(shards) > 0:
        values = levels(stream_key, dims, shards, -0.22, 0.18) * values
    return jnp.clip(values, min=-most, max=most).astype(kind)


def setup_inputs(seed: int = 0) -> dict:
    splits = jax.random.split(jax.random.key(seed), 18)
    hidden_in = normal_values(splits[0], (TOKENS, D), 1.0, 6.0, ((0, 8),))
    seg_ids = jnp.searchsorted(jnp.cumsum(ragged(splits[1], SEGMENTS, TOKENS, MAX_DOC, 0)), jnp.arange(TOKENS), side="right").astype(jnp.int32)
    norm_gain = jnp.clip(1.0 + 0.1 * jax.random.normal(splits[2], (LAYERS, D), jnp.float32), 0.5, 1.5)
    w_z = normal_values(splits[3], (LAYERS, D, INNER), D ** -0.5, 0.1875, ((2, 4),))
    w_x = normal_values(splits[4], (LAYERS, D, INNER), D ** -0.5, 0.1875, ((2, 4),))
    w_bc = normal_values(splits[5], (LAYERS, D, 2 * STATE), D ** -0.5, 0.1875)
    w_dt = normal_values(splits[6], (LAYERS, D, NH), D ** -0.5, 0.1875, ((2, 4),))
    conv_x_w = normal_values(splits[7], (LAYERS, CONV, INNER), CONV ** -0.5, 3.0, ((2, 4),), jnp.float32)
    conv_x_b = normal_values(splits[8], (LAYERS, INNER), 0.5, 3.0, ((1, 4),), jnp.float32)
    conv_bc_w = normal_values(splits[9], (LAYERS, CONV, 2 * STATE), CONV ** -0.5, 3.0, (), jnp.float32)
    conv_bc_b = normal_values(splits[10], (LAYERS, 2 * STATE), 0.5, 3.0, (), jnp.float32)
    dt_bias = jnp.clip(-4.0 + 3.0 * jax.random.uniform(splits[11], (LAYERS, NH), jnp.float32) ** levels(splits[11], (LAYERS, NH), ((1, 4),), -0.2, 0.2), -4.0, -1.0)
    a_log = jnp.clip(-8.0 + 9.0 * jax.random.uniform(splits[12], (LAYERS, NH), jnp.float32) ** levels(splits[12], (LAYERS, NH), ((1, 4),), -0.2, 0.2), -8.0, 1.0)
    d_skip = jnp.clip(0.5 + 1.0 * jax.random.uniform(splits[13], (LAYERS, NH), jnp.float32) ** levels(splits[13], (LAYERS, NH), ((1, 4),), -0.2, 0.2), 0.5, 1.5)
    gate_gain = jnp.clip(1.0 + 0.1 * jax.random.normal(splits[14], (LAYERS, INNER), jnp.float32), 0.5, 1.5)
    w_out = normal_values(splits[15], (LAYERS, INNER, D), INNER ** -0.5, 0.125, ((1, 4),))
    out_cot = normal_values(splits[16], (TOKENS, D), 1.0, 6.0, ((0, 8),), jnp.float32)
    return dict(hidden_in=hidden_in, seg_ids=seg_ids, norm_gain=norm_gain, w_z=w_z, w_x=w_x, w_bc=w_bc, w_dt=w_dt, conv_x_w=conv_x_w, conv_x_b=conv_x_b, conv_bc_w=conv_bc_w, conv_bc_b=conv_bc_b, dt_bias=dt_bias, a_log=a_log, d_skip=d_skip, gate_gain=gate_gain, w_out=w_out, out_cot=out_cot)


eps = 1e-05
highest = lax.Precision.HIGHEST

def contract_rows(left, right):
    return lax.dot_general(left, right, (((0,), (0,)), ((), ())), preferred_element_type=jnp.float32)

def contract_cols(left, right):
    return lax.dot_general(left, right, (((1,), (1,)), ((), ())), preferred_element_type=jnp.float32)

def in_norm(resid, gain_row):
    return resid * lax.rsqrt(lax.optimization_barrier(jnp.mean(resid * resid, axis=1)) + eps)[:, None] * gain_row[None, :]

def causal_conv(inputs, edge_rows, weights, biases, seg_ext):
    tok_rows = inputs.shape[0]
    tap_count = weights.shape[0]
    extended = jnp.concatenate([edge_rows, inputs], axis=0)
    own_seg = seg_ext[tap_count - 1:]
    summed = jnp.zeros_like(inputs) + biases[None, :]
    for offset in range(tap_count):
        keep_mask = (seg_ext[offset:offset + tok_rows] == own_seg).astype(jnp.float32)
        summed = summed + weights[offset][None, :] * extended[offset:offset + tok_rows] * keep_mask[:, None]
    return summed

def front_end(x_proj, bc_proj, dt_proj, x_edge, bc_edge, layer_params, seg_ext, head_count):
    conv_xw, conv_xb, conv_bw, conv_bb, dt_shift, log_rate, skip_gain = layer_params
    x_conv = jax.nn.silu(causal_conv(x_proj, x_edge, conv_xw, conv_xb, seg_ext))
    bc_conv = jax.nn.silu(causal_conv(bc_proj, bc_edge, conv_bw, conv_bb, seg_ext))
    state_width = bc_conv.shape[1] // 2
    step_size = jax.nn.softplus(dt_proj + dt_shift[None, :])
    log_decay = -step_size * jnp.exp(log_rate)[None, :]
    x_heads = x_conv.reshape(x_conv.shape[0], head_count, -1)
    return (x_heads, bc_conv[:, :state_width], bc_conv[:, state_width:], step_size, log_decay)

def span_states(x_heads, b_mat, c_mat, step_size, log_decay, own_seg, seg_before, span_len):
    tok_rows, head_count, head_width = x_heads.shape
    state_width = b_mat.shape[1]
    span_count = tok_rows // span_len
    entry_weight = jnp.exp(jnp.cumsum(log_decay, axis=0)) * (own_seg == seg_before).astype(jnp.float32)[:, None]
    earlier_seg = jnp.concatenate([seg_before[None], own_seg[:-1]])
    span_prev = earlier_seg.reshape(span_count, span_len)[:, 0]
    position = jnp.arange(span_len)
    causal = position[:, None] >= position[None, :]

    def advance(carried, pieces):
        x_part, b_part, c_part, dt_part, decay_part, seg_part, prev_seg = pieces
        cumul = jnp.cumsum(decay_part, axis=0)
        same_doc = (seg_part[:, None] == seg_part[None, :]) & causal
        gaps = cumul[:, None, :] - cumul[None, :, :]
        kernel = jnp.exp(jnp.where(same_doc[:, :, None], gaps, -1e+30))
        inner_prod = jnp.dot(c_part, b_part.T, precision=highest)
        scores = inner_prod[:, :, None] * kernel * dt_part[None, :, :]
        y_intra = jnp.einsum('ijh,jhp->ihp', scores, x_part, precision=highest)
        into = jnp.exp(cumul) * (seg_part == prev_seg).astype(jnp.float32)[:, None]
        y_inter = jnp.einsum('is,hps->ihp', c_part, carried, precision=highest) * into[:, :, None]
        to_end = jnp.exp(cumul[-1][None, :] - cumul) * (seg_part == seg_part[-1]).astype(jnp.float32)[:, None] * dt_part
        updated = carried * into[-1][:, None, None] + jnp.einsum('jh,jhp,js->hps', to_end, x_part, b_part, precision=highest)
        return (updated, y_intra + y_inter)
    start_state = jnp.zeros((head_count, head_width, state_width), jnp.float32)
    pieces = (x_heads.reshape(span_count, span_len, head_count, head_width), b_mat.reshape(span_count, span_len, state_width), c_mat.reshape(span_count, span_len, state_width), step_size.reshape(span_count, span_len, head_count), log_decay.reshape(span_count, span_len, head_count), own_seg.reshape(span_count, span_len), span_prev)
    final_state, outputs = lax.scan(advance, start_state, pieces)
    return (outputs.reshape(tok_rows, head_count, head_width), final_state, entry_weight)

def mixer_full(z_proj, x_proj, bc_proj, dt_proj, x_edge, bc_edge, layer_params, incoming, seg_ext, span_len):
    head_count = layer_params[4].shape[0]
    tap_count = layer_params[0].shape[0]
    x_heads, b_mat, c_mat, step_size, log_decay = front_end(x_proj, bc_proj, dt_proj, x_edge, bc_edge, layer_params, seg_ext, head_count)
    own_seg = seg_ext[tap_count - 1:]
    seg_before = seg_ext[tap_count - 2]
    y_local, local_state, entry_weight = span_states(x_heads, b_mat, c_mat, step_size, log_decay, own_seg, seg_before, span_len)
    carried_in = jnp.einsum('ts,hps->thp', c_mat, incoming, precision=highest) * entry_weight[:, :, None]
    mixed = y_local + carried_in + layer_params[6][None, :, None] * x_heads
    gated = mixed.reshape(mixed.shape[0], -1) * jax.nn.silu(z_proj)
    final_state = local_state + entry_weight[-1][:, None, None] * incoming
    return ((gated, final_state), (entry_weight, c_mat))

def gated_block(z_proj, x_proj, bc_proj, dt_proj, layer_params, gamma, seg_ext):
    x_edge = jnp.zeros((CONV - 1, x_proj.shape[1]), jnp.float32)
    bc_edge = jnp.zeros((CONV - 1, bc_proj.shape[1]), jnp.float32)
    incoming = jnp.zeros((NH, HEADDIM, STATE), jnp.float32)
    outputs, extras = mixer_full(z_proj, x_proj, bc_proj, dt_proj, x_edge, bc_edge, layer_params, incoming, seg_ext, SPAN)
    gated = outputs[0]
    scale = lax.rsqrt(lax.optimization_barrier(jnp.mean(gated * gated, axis=1)) + eps)
    return gated * scale[:, None] * gamma[None, :]

def reference(hidden_in, seg_ids, norm_gain, w_z, w_x, w_bc, w_dt, conv_x_w, conv_x_b, conv_bc_w, conv_bc_b, dt_bias, a_log, d_skip, gate_gain, w_out, out_cot):
    seg_ext = jnp.concatenate([jnp.full((CONV - 1,), -1, jnp.int32), seg_ids.astype(jnp.int32)])
    residual = hidden_in.astype(jnp.float32)
    saved = []

    def project(normed, layer_idx):
        return (jnp.dot(normed, w_z[layer_idx], preferred_element_type=jnp.float32), jnp.dot(normed, w_x[layer_idx], preferred_element_type=jnp.float32), jnp.dot(normed, w_bc[layer_idx], preferred_element_type=jnp.float32), jnp.dot(normed, w_dt[layer_idx], preferred_element_type=jnp.float32))

    def params_of(layer_idx):
        return (conv_x_w[layer_idx], conv_x_b[layer_idx], conv_bc_w[layer_idx], conv_bc_b[layer_idx], dt_bias[layer_idx], a_log[layer_idx], d_skip[layer_idx])
    for layer_idx in range(LAYERS):
        saved.append(residual)
        normed = in_norm(residual, norm_gain[layer_idx]).astype(jnp.bfloat16)
        z_proj, x_proj, bc_proj, dt_proj = project(normed, layer_idx)
        gated_normed = gated_block(z_proj, x_proj, bc_proj, dt_proj, params_of(layer_idx), gate_gain[layer_idx], seg_ext).astype(jnp.bfloat16)
        residual = residual + jnp.dot(gated_normed, w_out[layer_idx], preferred_element_type=jnp.float32)
    hidden_out = residual.astype(jnp.bfloat16)
    cotangent = out_cot
    grad_lists = [[None] * LAYERS for index in range(14)]
    for layer_idx in reversed(range(LAYERS)):
        residual = saved[layer_idx]
        normed_f, norm_pull = jax.vjp(in_norm, residual, norm_gain[layer_idx])
        normed = normed_f.astype(jnp.bfloat16)
        z_proj, x_proj, bc_proj, dt_proj = project(normed, layer_idx)

        def block_fn(zp_in, xp_in, bp_in, dp_in, lp_in, gm_in):
            return gated_block(zp_in, xp_in, bp_in, dp_in, lp_in, gm_in, seg_ext)
        gated_f, block_pull = jax.vjp(block_fn, z_proj, x_proj, bc_proj, dt_proj, params_of(layer_idx), gate_gain[layer_idx])
        gated_normed = gated_f.astype(jnp.bfloat16)
        cot_b = cotangent.astype(jnp.bfloat16)
        grad_lists[13][layer_idx] = contract_rows(gated_normed, cot_b)
        d_gated_normed = contract_cols(cot_b, w_out[layer_idx])
        d_z, d_x, d_bc, d_dt, d_params, d_gamma = block_pull(d_gated_normed)
        d_z_b = d_z.astype(jnp.bfloat16)
        d_x_b = d_x.astype(jnp.bfloat16)
        d_bc_b = d_bc.astype(jnp.bfloat16)
        d_dt_b = d_dt.astype(jnp.bfloat16)
        grad_lists[1][layer_idx] = contract_rows(normed, d_z_b)
        grad_lists[2][layer_idx] = contract_rows(normed, d_x_b)
        grad_lists[3][layer_idx] = contract_rows(normed, d_bc_b)
        grad_lists[4][layer_idx] = contract_rows(normed, d_dt_b)
        for slot in range(7):
            grad_lists[5 + slot][layer_idx] = d_params[slot]
        grad_lists[12][layer_idx] = d_gamma
        d_normed = contract_cols(d_z_b, w_z[layer_idx]) + contract_cols(d_x_b, w_x[layer_idx]) + contract_cols(d_bc_b, w_bc[layer_idx]) + contract_cols(d_dt_b, w_dt[layer_idx])
        d_resid, d_gain = norm_pull(d_normed)
        grad_lists[0][layer_idx] = d_gain
        cotangent = cotangent + d_resid
    stacked = [jnp.stack(entries) for entries in grad_lists]
    return (hidden_out, cotangent, stacked[0], stacked[1], stacked[2], stacked[3], stacked[4], stacked[5], stacked[6], stacked[7], stacked[8], stacked[9], stacked[10], stacked[11], stacked[12], stacked[13])
```

```python
import functools

import jax
import jax.numpy as jnp
from jax import lax
from jax.experimental import pallas as pl
from jax.experimental.pallas import tpu as pltpu
from jax.sharding import PartitionSpec as P

eps = 1e-05
F32, BF = jnp.float32, jnp.bfloat16
NN, NT, TN = ((1,), (0,)), ((1,), (1,)), ((0,), (0,))
HALO = 8


def swap(value, axis, mask):
    count = lax.axis_size(axis)
    return lax.ppermute(value, axis, [(i, i ^ mask) for i in range(count)])


def rotate(value, axis, steps):
    count = lax.axis_size(axis)
    return lax.ppermute(value, axis, [(i, (i + steps) % count) for i in range(count)])


def bit_of(axis, bit):
    return (lax.axis_index(axis) >> bit) & 1


def bits_of(axis):
    return lax.axis_size(axis).bit_length() - 1


def halves(value, which, dim):
    half = value.shape[dim] // 2
    keep = lax.dynamic_slice_in_dim(value, which * half, half, dim)
    send = lax.dynamic_slice_in_dim(value, (1 - which) * half, half, dim)
    return keep, send


def scatter_sum(value, axis, dim):
    for bit in range(bits_of(axis)):
        keep, send = halves(value, bit_of(axis, bit), dim)
        value = keep + swap(send, axis, 1 << bit)
    return value


def gather_back(value, axis, dim):
    for bit in reversed(range(bits_of(axis))):
        other = swap(value, axis, 1 << bit)
        first = bit_of(axis, bit) == 0
        value = jnp.where(
            first,
            jnp.concatenate([value, other], dim),
            jnp.concatenate([other, value], dim),
        )
    return value


def own_piece(value, axis, dim):
    for bit in range(bits_of(axis)):
        half = value.shape[dim] // 2
        value = lax.dynamic_slice_in_dim(value, bit_of(axis, bit) * half, half, dim)
    return value


def mask_of(bit):
    return 1 << bit if bit < 2 else 3 << (bit - 1)


def seq_scatter(value, order):
    count = bits_of("seq")
    rows, cols = value.shape
    value = value.reshape((2,) * count + (rows >> count, cols))
    top = list(reversed(range(count)))
    for bit in order:
        dim = top.index(bit)
        keep, send = halves(value, bit_of("seq", bit), dim)
        value = keep + swap(send, "seq", mask_of(bit))
    return value.reshape(rows >> count, cols)


def seq_sum(value):
    for bit in range(bits_of("seq")):
        value = value + swap(value, "seq", mask_of(bit))
    return value


def head_sum(value):
    for bit in range(bits_of("head")):
        value = value + swap(value, "head", 1 << bit)
    return value


def carried(message, heads, reverse):
    cols = message.shape[1]
    rows = message.shape[0] - heads
    state = message[:rows].reshape(heads, rows // heads, cols)
    decay = message[rows:].reshape(heads, 1, cols)
    ahead_s, ahead_d = jnp.zeros_like(state), jnp.ones_like(decay)
    count = bits_of("seq")
    for bit in range(count):
        packed = jnp.concatenate([state.reshape(rows, cols), decay.reshape(heads, cols)], 0)
        got = swap(packed, "seq", mask_of(bit))
        got_s = got[:rows].reshape(heads, rows // heads, cols)
        got_d = got[rows:].reshape(heads, 1, cols)
        upper = bit_of("seq", bit) == 1
        later = jnp.logical_not(upper) if reverse else upper
        ahead_s, ahead_d = (
            jnp.where(later, ahead_d * got_s + ahead_s, ahead_s),
            jnp.where(later, ahead_d * got_d, ahead_d),
        )
        if bit + 1 < count:
            state = jnp.where(later, decay * got_s + state, got_d * state + got_s)
            decay = decay * got_d
    return ahead_s.reshape(rows, cols)


def mm(left, right, dims):
    return lax.dot_general(left, right, (dims, ((), ())), preferred_element_type=F32)


def split2(value):
    high = value.astype(BF)
    return high, (value - high.astype(F32)).astype(BF)


def mm3(left, right, dims):
    lh, ll = split2(left)
    rh, rl = split2(right)
    return mm(lh, rh, dims) + (mm(lh, rl, dims) + mm(ll, rh, dims))


def split3(value):
    high = value.astype(BF)
    rest = value - high.astype(F32)
    mid = rest.astype(BF)
    return high, mid, (rest - mid.astype(F32)).astype(BF)


def sel_right(value, sel, dims):
    return sum(mm(part, sel, dims) for part in split3(value))


def sel_left(sel, value, dims):
    return sum(mm(sel, part, dims) for part in split3(value))


def head_map(heads, inner):
    chan = lax.broadcasted_iota(jnp.int32, (inner, heads), 0)
    head = lax.broadcasted_iota(jnp.int32, (inner, heads), 1)
    return jnp.where(chan // (inner // heads) == head, 1.0, 0.0).astype(BF)


def expand(value, emap):
    return sel_right(value, emap, NT)


def per_head(value, emap):
    return sel_right(value, emap, NN)


def lower(rows):
    row = lax.broadcasted_iota(jnp.int32, (rows, rows), 0)
    col = lax.broadcasted_iota(jnp.int32, (rows, rows), 1)
    return row >= col


def to_column(row_value):
    rows = row_value.shape[1]
    row = lax.broadcasted_iota(jnp.int32, (rows, rows), 0)
    col = lax.broadcasted_iota(jnp.int32, (rows, rows), 1)
    return jnp.sum(jnp.where(row == col, row_value, 0.0), axis=1, keepdims=True)


def row_sums(value):
    ones = jnp.ones((8, value.shape[1]), BF)
    return sel_left(ones, value, NT)[0:1, :]


def sigmoid(value):
    return 1.0 / (1.0 + jnp.exp(-value))


def silu(value):
    return value * sigmoid(value)


def silu_slope(value):
    sig = sigmoid(value)
    return sig * (1.0 + value * (1.0 - sig))


def run(body, outs, *args, blocks=None, scratch=(), flops=2_000_000_000, name=None):
    blocks = blocks or {}

    def whole(shape):
        return pl.BlockSpec(shape, lambda i: (0,) * len(shape))

    in_specs = []
    for place, arg in enumerate(args):
        if place in blocks:
            layer = blocks[place]
            in_specs.append(
                pl.BlockSpec(
                    (pl.Squeezed(),) + arg.shape[1:],
                    functools.partial(lambda l, n, i: (l,) + (0,) * n, layer, arg.ndim - 1),
                )
            )
        else:
            in_specs.append(whole(arg.shape))
    moved = sum(a.size * a.dtype.itemsize for a in args)
    return pl.pallas_call(
        body,
        grid=(1,),
        in_specs=in_specs,
        out_specs=[whole(shape) for shape, kind in outs],
        out_shape=[jax.ShapeDtypeStruct(shape, kind) for shape, kind in outs],
        scratch_shapes=list(scratch),
        cost_estimate=pl.CostEstimate(flops=flops, bytes_accessed=moved, transcendentals=0),
        name=name,
    )(*args)


def k_proj(xn, wz, wx, wbc, wdt, z, x, bc, dt, nb):
    rounded = xn[...].astype(BF)
    nb[...] = rounded
    x[...] = mm(rounded, wx[...], NN)
    bc[...] = mm(rounded, wbc[...], NN)
    dt[...] = mm(rounded, wdt[...], NN)
    z[...] = mm(rounded, wz[...], NN)


def conv_rows(ext, halo_rows, rows, weights, bias, aux):
    total = jnp.broadcast_to(bias, (rows, weights.shape[1]))
    taps = weights.shape[0]
    for tap in range(taps):
        part = ext[pl.ds(halo_rows - taps + 1 + tap, rows), :] * weights[tap : tap + 1, :]
        total = total + (part * aux[:, tap : tap + 1] if tap < taps - 1 else part)
    return total


def k_front(layer, x, bc, dt, edge, aux, cxw, cxb, cbw, cbb, dtb, alog,
            ux, ubc, dts, cum, cumt, msg, ext_x, ext_b):
    rows, inner = x.shape
    heads = dt.shape[1]
    width = bc.shape[1] // 2
    ext_x[0:HALO, :] = edge[:, :inner]
    ext_x[HALO:, :] = x[...]
    ext_b[0:HALO, :] = edge[:, inner:]
    ext_b[HALO:, :] = bc[...]
    masks = aux[...]
    conv_x = conv_rows(ext_x, HALO, rows, cxw[...], cxb[layer : layer + 1, :], masks)
    conv_b = conv_rows(ext_b, HALO, rows, cbw[...], cbb[layer : layer + 1, :], masks)
    ux[...] = conv_x
    ubc[...] = conv_b
    b_mat = silu(conv_b[:, :width])
    raw = dt[...] + dtb[layer : layer + 1, :]
    step = jnp.maximum(raw, 0.0) + jnp.log1p(jnp.exp(-jnp.abs(raw)))
    dts[...] = step
    decay = -step * jnp.exp(alog[layer : layer + 1, :])
    tri = jnp.where(lower(rows), 1.0, 0.0).astype(BF)
    total = sel_left(tri, decay, NN)
    total_t = sum(mm(part, tri, ((0,), (1,))) for part in split3(decay))
    cum[...] = total
    cumt[...] = total_t
    emap = head_map(heads, inner)
    to_end = jnp.exp(total[rows - 1 : rows, :] - total) * masks[:, 3:4] * step
    msg[0:inner, :] = mm3(silu(conv_x) * expand(to_end, emap), b_mat, TN)
    msg[inner:, :] = jnp.broadcast_to(
        jnp.exp(total_t[:, rows - 1 : rows]) * masks[rows - 1 : rows, 4:5], (heads, width)
    )


def head_kernel(cum, cumt, allowed, head):
    gap = cum[:, head : head + 1] - cumt[head : head + 1, :]
    return jnp.exp(jnp.where(allowed, gap, -1e30))


def k_intra(layer, ux, ubc, dts, cum, cumt, segc, segr, dskip, yp):
    rows, inner = ux.shape
    heads = dts.shape[1]
    width = ubc.shape[1] // 2
    per = inner // heads
    emap = head_map(heads, inner)
    x_conv = silu(ux[...])
    bc = silu(ubc[...])
    gram = mm3(bc[:, width:], bc[:, :width], NT)
    allowed = jnp.logical_and(segc[...] == segr[...], lower(rows))
    scaled = x_conv * expand(dts[...], emap)
    skip = x_conv * expand(jnp.broadcast_to(dskip[layer : layer + 1, :], (8, heads)), emap)[0:1, :]
    total, total_t = cum[...], cumt[...]
    group = max(1, 128 // per)
    for first in range(0, heads, group):
        cols = slice(first * per, (first + group) * per)
        sh, sl = split2(scaled[:, cols])
        lane = lax.broadcasted_iota(jnp.int32, (rows, group * per), 1)
        result = skip[:, cols]
        for head in range(first, first + group):
            gh, gl = split2(gram * head_kernel(total, total_t, allowed, head))
            part = mm(gh, sh, NN) + (mm(gh, sl, NN) + mm(gl, sh, NN))
            result = result + jnp.where(lane // per == head - first, part, 0.0)
        yp[:, cols] = result


def k_gate(yp, ubc, cum, aux, z, inc, mixed, gated, ss):
    inner = yp.shape[1]
    heads = cum.shape[1]
    width = ubc.shape[1] // 2
    emap = head_map(heads, inner)
    c_mat = silu(ubc[:, width:])
    into = jnp.exp(cum[...]) * aux[:, 4:5]
    mix = yp[...] + mm3(c_mat, inc[...], NT) * expand(into, emap)
    mixed[...] = mix
    gate = mix * silu(z[...])
    gated[...] = gate
    ss[...] = row_sums(gate * gate)


def k_out(layer, total, gated, ss, gain, wout, gn, part):
    scale = to_column(lax.rsqrt(ss[...] * (1.0 / total) + eps))
    normed = (gated[...] * scale * gain[layer : layer + 1, :]).astype(BF)
    gn[...] = normed
    part[...] = mm(normed, wout[...], NN)


def k_b1(layer, total, cot, wout, gated, ss, gain, cb, dgn, cross, ggain):
    rounded = cot[...].astype(BF)
    cb[...] = rounded
    grad = mm(rounded, wout[...], NT)
    dgn[...] = grad
    scale = to_column(lax.rsqrt(ss[...] * (1.0 / total) + eps))
    both = grad * gated[...]
    cross[...] = row_sums(both * gain[layer : layer + 1, :])
    ggain[...] = jnp.sum(both * scale, axis=0, keepdims=True)


def k_b2(layer, total, dgn, gated, mixed, z, ss, cross, gain, ubc, cum, cumt, aux, dm, dz, msg):
    rows, inner = dgn.shape
    heads = cum.shape[1]
    width = ubc.shape[1] // 2
    emap = head_map(heads, inner)
    scale_row = lax.rsqrt(ss[...] * (1.0 / total) + eps)
    scale = to_column(scale_row)
    pull = to_column(scale_row * scale_row * scale_row * cross[...] * (1.0 / total))
    d_gated = scale * gain[layer : layer + 1, :] * dgn[...] - gated[...] * pull
    zv = z[...]
    grad = d_gated * silu(zv)
    dm[...] = grad
    dz[...] = (d_gated * mixed[...] * silu_slope(zv)).astype(BF)
    masks = aux[...]
    into = jnp.exp(cum[...]) * masks[:, 4:5]
    msg[0:inner, :] = mm3(grad * expand(into, emap), silu(ubc[:, width:]), TN)
    msg[inner:, :] = jnp.broadcast_to(
        jnp.exp(cumt[:, rows - 1 : rows]) * masks[rows - 1 : rows, 4:5], (heads, width)
    )


def k_b3(layer, dm, ux, ubc, dts, cum, cumt, segc, segr, mixed, inc, aux, dskip,
         dx, dbc, dcum, ddt, gskip):
    rows, inner = ux.shape
    heads = dts.shape[1]
    width = ubc.shape[1] // 2
    per = inner // heads
    emap = head_map(heads, inner)
    x_conv = silu(ux[...])
    bc = silu(ubc[...])
    b_mat, c_mat = bc[:, :width], bc[:, width:]
    gram = mm3(c_mat, b_mat, NT)
    allowed = jnp.logical_and(segc[...] == segr[...], lower(rows))
    step = dts[...]
    step_e = expand(step, emap)
    scaled = x_conv * step_e
    grad = dm[...]
    total, total_t = cum[...], cumt[...]
    skip_row = dskip[layer : layer + 1, :]
    skip_e = expand(jnp.broadcast_to(skip_row, (8, heads)), emap)[0:1, :]
    d_gram = jnp.zeros((rows, rows), F32)
    group = max(1, 128 // per)
    plain = []
    for first in range(0, heads, group):
        cols = slice(first * per, (first + group) * per)
        sh, sl = split2(scaled[:, cols])
        lane = lax.broadcasted_iota(jnp.int32, (rows, group * per), 1)
        g_cols = grad[:, cols]
        ch, cl = split2(g_cols)
        result = jnp.zeros((rows, group * per), F32)
        for head in range(first, first + group):
            mine = lane // per == head - first
            fall = head_kernel(total, total_t, allowed, head)
            gh, gl = split2(gram * fall)
            part = mm(gh, ch, TN) + (mm(gh, cl, TN) + mm(gl, ch, TN))
            result = result + jnp.where(mine, part, 0.0)
            mh = jnp.where(mine, ch, jnp.zeros_like(ch))
            ml = jnp.where(mine, cl, jnp.zeros_like(cl))
            outer = mm(mh, sh, NT) + (mm(mh, sl, NT) + mm(ml, sh, NT))
            d_gram = d_gram + outer * fall
        plain.append(result)
    plain = jnp.concatenate(plain, axis=1)
    dx[...] = plain * step_e + grad * skip_e
    into = jnp.exp(total) * aux[:, 4:5]
    dbc[:, :width] = mm3(d_gram, c_mat, TN)
    dbc[:, width:] = mm3(d_gram, b_mat, NN) + mm3(grad * expand(into, emap), inc[...], NN)
    by_col = per_head(x_conv * plain, emap)
    skip_dot = per_head(grad * x_conv, emap)
    ddt[...] = by_col
    dcum[...] = per_head(grad * mixed[...], emap) - skip_row * skip_dot - step * by_col
    gskip[...] = jnp.sum(skip_dot, axis=0, keepdims=True)


def k_b4(layer, ux, ubc, dts, dtp, cum, aux, dx, dbc, dcum, ddt, df, inc, dtb, alog,
         du, dbo, dd, gdtb, galog):
    rows, inner = ux.shape
    heads = dts.shape[1]
    width = ubc.shape[1] // 2
    emap = head_map(heads, inner)
    conv = ux[...]
    x_conv = silu(conv)
    b_mat = silu(ubc[:, :width])
    total, step, masks = cum[...], dts[...], aux[...]
    fin = df[...]
    spread = mm3(b_mat, fin, NT)
    bare = jnp.exp(total[rows - 1 : rows, :] - total) * masks[:, 3:4]
    to_end = bare * step
    to_end_e = expand(to_end, emap)
    dot = per_head(x_conv * spread, emap)
    du[...] = (dx[...] + to_end_e * spread) * silu_slope(conv)
    dbo[:, :width] = dbc[:, :width] + mm3(x_conv * to_end_e, fin, NN)
    dbo[:, width:] = dbc[:, width:]
    used = to_end * dot
    d_cum = dcum[...] - used
    through = per_head(row_sums(fin * inc[...]) + jnp.zeros((8, inner), F32), emap)[0:1, :]
    last = jnp.sum(used, axis=0, keepdims=True) + through * (
        jnp.exp(total[rows - 1 : rows, :]) * masks[rows - 1 : rows, 4:5]
    )
    tri = jnp.where(lower(rows), 1.0, 0.0).astype(BF)
    d_decay = sel_left(tri, d_cum, TN) + last
    rate = jnp.exp(alog[layer : layer + 1, :])
    galog[...] = jnp.sum(-step * rate * d_decay, axis=0, keepdims=True)
    d_raw = (ddt[...] + bare * dot - rate * d_decay) * sigmoid(dtp[...] + dtb[layer : layer + 1, :])
    gdtb[...] = jnp.sum(d_raw, axis=0, keepdims=True)
    dd[...] = d_raw.astype(BF)


def k_conv_back(du, halo, proj, edge, aux, weights, grad, gw, gb, ext_d, ext_p):
    rows = du.shape[0]
    taps = weights.shape[0]
    ext_d[0:rows, :] = du[...]
    ext_d[rows:, :] = halo[...]
    ext_p[0:HALO, :] = edge[...]
    ext_p[HALO:, :] = proj[...]
    masks = aux[...]
    value = du[...]
    total = jnp.zeros_like(value)
    for tap in range(taps):
        back = ext_d[pl.ds(taps - 1 - tap, rows), :] * weights[tap : tap + 1, :]
        seen = ext_p[pl.ds(HALO - taps + 1 + tap, rows), :] * value
        if tap < taps - 1:
            back = back * masks[:, 5 + tap : 6 + tap]
            seen = seen * masks[:, tap : tap + 1]
        total = total + back
        gw[tap : tap + 1, :] = jnp.sum(seen, axis=0, keepdims=True)
    gb[...] = jnp.sum(value, axis=0, keepdims=True)
    grad[...] = total.astype(BF)


def k_dnorm(dz, dxb, dd, dbq, wz, wx, wdt, wbq, own):
    own[...] = (
        mm(dz[...], wz[...], NT)
        + mm(dxb[...], wx[...], NT)
        + mm(dd[...], wdt[...], NT)
        + mm(dbq[...], wbq[...], NT)
    )


def k_round(value, out):
    out[...] = value[...].astype(BF)


def in_norm(resid, gain_row):
    return resid * lax.rsqrt(jnp.mean(resid * resid, axis=1) + eps)[:, None] * gain_row[None, :]


def local(hidden_in, seg_ids, norm_gain, w_z, w_x, w_bc, w_dt, conv_x_w, conv_x_b, conv_bc_w,
          conv_bc_b, dt_bias, a_log, d_skip, gate_gain, w_out, out_cot):
    rows, model = hidden_in.shape
    layers = w_z.shape[0]
    heads = w_dt.shape[2]
    inner = w_z.shape[2]
    state2 = w_bc.shape[2]
    width = state2 // 2
    taps = conv_x_w.shape[1]
    inner_total = inner * lax.axis_size("head")
    seq_bits = bits_of("seq")
    top_down = list(reversed(range(1, seq_bits)))
    orders = ([0] + top_down, top_down + [0], top_down[:1] + [0] + top_down[1:])

    padded = jnp.concatenate(
        [jnp.full((taps - 1,), -1, jnp.int32), seg_ids, jnp.full((taps - 1,), -1, jnp.int32)]
    )
    around = lax.dynamic_slice_in_dim(
        padded, lax.axis_index("seq") * rows, rows + 2 * (taps - 1)
    )
    own = around[taps - 1 : taps - 1 + rows]
    seg_before = around[taps - 2]
    columns = [around[k : k + rows] == own for k in range(taps - 1)]
    columns += [own == own[rows - 1], own == seg_before]
    columns += [around[2 * (taps - 1) - k : 2 * (taps - 1) - k + rows] == own for k in range(taps - 1)]
    aux = jnp.stack(columns, axis=1).astype(F32)
    segc, segr = own[:, None], own[None, :]

    resid = own_piece(hidden_in.astype(F32), "head", 0)
    saved = []
    for l in range(layers):
        if l == 0:
            normed_f = in_norm(hidden_in.astype(F32), norm_gain[l])
        else:
            normed_f = gather_back(in_norm(resid, norm_gain[l]), "head", 0)
        z, x, bc, dtp, nb = run(
            k_proj,
            [((rows, inner), F32), ((rows, inner), F32), ((rows, state2), F32),
             ((rows, heads), F32), ((rows, model), BF)],
            normed_f, w_z, w_x, w_bc, w_dt, blocks={1: l, 2: l, 3: l, 4: l}, name="proj",
        )
        edge = rotate(jnp.concatenate([x[rows - HALO :], bc[rows - HALO :]], 1), "seq", 1)
        ux, ubc, dts, cum, cumt, msg = run(
            functools.partial(k_front, l),
            [((rows, inner), F32), ((rows, state2), F32), ((rows, heads), F32),
             ((rows, heads), F32), ((heads, rows), F32), ((inner + heads, width), F32)],
            x, bc, dtp, edge, aux, conv_x_w, conv_x_b, conv_bc_w, conv_bc_b, dt_bias, a_log,
            blocks={5: l, 7: l},
            scratch=(pltpu.VMEM((rows + HALO, inner), F32), pltpu.VMEM((rows + HALO, state2), F32)),
            name="front",
        )
        inc = carried(msg, heads, False)
        (yp,) = run(
            functools.partial(k_intra, l), [((rows, inner), F32)],
            ux, ubc, dts, cum, cumt, segc, segr, d_skip, name="intra",
        )
        mixed, gated, ss = run(
            k_gate, [((rows, inner), F32), ((rows, inner), F32), ((1, rows), F32)],
            yp, ubc, cum, aux, z, inc, name="gate",
        )
        ss = lax.psum(ss, "head")
        gn, part = run(
            functools.partial(k_out, l, inner_total),
            [((rows, inner), BF), ((rows, model), F32)],
            gated, ss, gate_gain, w_out, blocks={3: l}, name="out",
        )
        branch = scatter_sum(part, "head", 0)
        saved.append((resid, z, x, bc, dtp, nb, edge, ux, ubc, dts, cum, cumt, inc, mixed, gated,
                      ss, gn))
        resid = resid + branch
    (hidden_out,) = run(
        k_round, [((rows, model), BF)], gather_back(resid, "head", 0), flops=1000000, name="round"
    )

    cot_full = out_cot
    cot = own_piece(out_cot, "head", 0)
    wide = [[None] * layers for _ in range(3)]
    narrow = [None] * layers
    small = [None] * layers
    gains = [None] * layers
    for l in reversed(range(layers)):
        (resid, z, x, bc, dtp, nb, edge, ux, ubc, dts, cum, cumt, inc, mixed, gated, ss,
         gn) = saved[l]
        cb, dgn, cross, ggain = run(
            functools.partial(k_b1, l, inner_total),
            [((rows, model), BF), ((rows, inner), F32), ((1, rows), F32), ((1, inner), F32)],
            cot_full, w_out, gated, ss, gate_gain, blocks={1: l}, name="b1",
        )
        cross = lax.psum(cross, "head")
        dm, dz, msg = run(
            functools.partial(k_b2, l, inner_total),
            [((rows, inner), F32), ((rows, inner), BF), ((inner + heads, width), F32)],
            dgn, gated, mixed, z, ss, cross, gate_gain, ubc, cum, cumt, aux, name="b2",
        )
        fin = carried(msg, heads, True)
        dx, dbc, dcum, ddt, gskip = run(
            functools.partial(k_b3, l),
            [((rows, inner), F32), ((rows, state2), F32), ((rows, heads), F32),
             ((rows, heads), F32), ((1, heads), F32)],
            dm, ux, ubc, dts, cum, cumt, segc, segr, mixed, inc, aux, d_skip, name="b3",
        )
        du, dbo, dd, gdtb, galog = run(
            functools.partial(k_b4, l),
            [((rows, inner), F32), ((rows, state2), F32), ((rows, heads), BF),
             ((1, heads), F32), ((1, heads), F32)],
            ux, ubc, dts, dtp, cum, aux, dx, dbc, dcum, ddt, fin, inc, dt_bias, a_log, name="b4",
        )
        halo_x = rotate(du[:HALO], "seq", -1)
        dbq = scatter_sum(dbo, "head", 1)
        dub = dbq * silu_slope(own_piece(ubc, "head", 1))
        halo_b = rotate(dub[:HALO], "seq", -1)
        quarter = dub.shape[1]
        dxb, gcw, gcb = run(
            k_conv_back,
            [((rows, inner), BF), ((taps, inner), F32), ((1, inner), F32)],
            du, halo_x, x, edge[:, :inner], aux, conv_x_w, blocks={5: l},
            scratch=(pltpu.VMEM((rows + HALO, inner), F32), pltpu.VMEM((rows + HALO, inner), F32)),
            name="convx",
        )
        dbb, gbw, gbb = run(
            k_conv_back,
            [((rows, quarter), BF), ((taps, quarter), F32), ((1, quarter), F32)],
            dub, halo_b, own_piece(bc, "head", 1), own_piece(edge[:, inner:], "head", 1), aux,
            own_piece(conv_bc_w[l], "head", 1),
            scratch=(pltpu.VMEM((rows + HALO, quarter), F32),
                     pltpu.VMEM((rows + HALO, quarter), F32)),
            name="convb",
        )
        (part,) = run(
            k_dnorm, [((rows, model), F32)],
            dz, dxb, dd, dbb, w_z, w_x, w_dt, own_piece(w_bc[l], "head", 1),
            blocks={4: l, 5: l, 6: l}, name="dnorm",
        )
        d_normed = scatter_sum(part, "head", 0)
        wide[2][l] = seq_scatter(mm(cb, gn, TN), orders[2])
        wide[0][l] = seq_scatter(mm(nb, dz, TN), orders[0])
        wide[1][l] = seq_scatter(mm(nb, dxb, TN), orders[1])
        narrow[l] = seq_scatter(
            jnp.concatenate([mm(nb, dbb, TN), mm(nb, dd, TN)], axis=1), orders[0]
        )
        _, norm_pull = jax.vjp(in_norm, resid, norm_gain[l])
        d_resid, d_gain = norm_pull(d_normed)
        gains[l] = d_gain
        small[l] = (gcw, gcb, gbw, gbb, gdtb, galog, gskip, ggain)
        cot = cot + d_resid
        cot_full = gather_back(cot, "head", 0)

    flat = [part.reshape(-1) for l in range(layers) for part in small[l]] + gains
    sizes = [part.size for part in flat]
    packed = jnp.concatenate(flat)
    packed = jnp.pad(packed, (0, -packed.size % 1024)).reshape(-1, 128)
    packed = seq_sum(packed).reshape(-1)
    pieces, start = [], 0
    for size in sizes:
        pieces.append(packed[start : start + size])
        start += size
    count = len(small[0])

    def both(slot):
        return jnp.stack([pieces[l * count + slot].reshape(small[l][slot].shape) for l in range(layers)])

    grad_gain = head_sum(jnp.stack(pieces[layers * count :]))
    share = model // lax.axis_size("seq")
    grad_gain = lax.dynamic_slice_in_dim(grad_gain, lax.axis_index("seq") * share, share, 1)
    quarter = state2 // lax.axis_size("head")
    narrow = jnp.stack(narrow)
    bc_parts = jnp.concatenate([narrow[:, :, :quarter], both(2), both(3)], axis=1)
    bc_parts = gather_back(bc_parts, "head", 2)
    return (
        hidden_out,
        cot_full,
        grad_gain,
        jnp.stack(wide[0]),
        jnp.stack(wide[1]),
        bc_parts[:, :share],
        narrow[:, :, quarter:],
        both(0),
        both(1)[:, 0],
        bc_parts[:, share : share + taps],
        bc_parts[:, share + taps],
        both(4)[:, 0],
        both(5)[:, 0],
        both(6)[:, 0],
        both(7)[:, 0],
        jnp.stack([part.T for part in wide[2]]),
    )


def solution(mesh):
    return jax.shard_map(
        local,
        mesh=mesh,
        in_specs=(
            P("seq", None),
            P(),
            P(),
            P(None, None, "head"),
            P(None, None, "head"),
            P(),
            P(None, None, "head"),
            P(None, None, "head"),
            P(None, "head"),
            P(),
            P(),
            P(None, "head"),
            P(None, "head"),
            P(None, "head"),
            P(None, "head"),
            P(None, "head", None),
            P("seq", None),
        ),
        out_specs=(
            P("seq", None),
            P("seq", None),
            P(None, "seq"),
            P(None, "seq", "head"),
            P(None, "seq", "head"),
            P(None, "seq", None),
            P(None, "seq", "head"),
            P(None, None, "head"),
            P(None, "head"),
            P(),
            P(),
            P(None, "head"),
            P(None, "head"),
            P(None, "head"),
            P(None, "head"),
            P(None, "head", "seq"),
        ),
        check_vma=False,
    )
```

```python
import functools

import jax
import jax.numpy as jnp
from jax import lax
from jax.experimental import pallas as pl
from jax.experimental.pallas import tpu as pltpu
from jax.sharding import PartitionSpec as P

eps = 1e-05
F32, BF = jnp.float32, jnp.bfloat16
NN, NT, TN = ((1,), (0,)), ((1,), (1,)), ((0,), (0,))
HALO = 8
GRANT = 24 << 20


def swap(value, axis, mask):
    count = lax.axis_size(axis)
    return lax.ppermute(value, axis, [(i, i ^ mask) for i in range(count)])


def rotate(value, axis, steps):
    count = lax.axis_size(axis)
    return lax.ppermute(value, axis, [(i, (i + steps) % count) for i in range(count)])


def bit_of(axis, bit):
    return (lax.axis_index(axis) >> bit) & 1


def bits_of(axis):
    return lax.axis_size(axis).bit_length() - 1


def reverse_bits(value, count):
    result = 0
    for bit in range(count):
        result = result | (((value >> bit) & 1) << (count - 1 - bit))
    return result


def relative_order(count):
    return [reverse_bits(i, count) for i in range(1 << count)]


def finish_scatter(keep, send, axis):
    for bit in range(bits_of(axis)):
        got = swap(send, axis, 1 << bit)
        half = keep.shape[0] // 2
        if bit + 1 < bits_of(axis):
            send = keep[half:] + got[half:]
            keep = keep[:half] + got[:half]
    return keep, got


def scatter_cols(value, axis):
    for bit in range(bits_of(axis)):
        half = value.shape[1] // 2
        which = bit_of(axis, bit)
        keep = lax.dynamic_slice_in_dim(value, which * half, half, 1)
        send = lax.dynamic_slice_in_dim(value, (1 - which) * half, half, 1)
        value = keep + swap(send, axis, 1 << bit)
    return value


def gather_pieces(mine, axis):
    pieces = [mine]
    for bit in reversed(range(bits_of(axis))):
        pieces = pieces + [swap(piece, axis, 1 << bit) for piece in pieces]
    return pieces


def gather_back(value, axis, dim):
    for bit in reversed(range(bits_of(axis))):
        other = swap(value, axis, 1 << bit)
        first = bit_of(axis, bit) == 0
        value = jnp.where(
            first,
            jnp.concatenate([value, other], dim),
            jnp.concatenate([other, value], dim),
        )
    return value


def own_piece(value, axis, dim):
    for bit in range(bits_of(axis)):
        half = value.shape[dim] // 2
        value = lax.dynamic_slice_in_dim(value, bit_of(axis, bit) * half, half, dim)
    return value


def mask_of(bit):
    return 1 << bit if bit < 2 else 3 << (bit - 1)


def seq_places(order, share):
    count = len(order)
    me = lax.axis_index("seq")
    starts = []
    for piece in range(1 << count):
        mask = 0
        for step, bit in enumerate(order):
            if (piece >> (count - 1 - step)) & 1:
                mask ^= mask_of(bit)
        starts.append((me ^ mask) * share)
    return jnp.stack(starts).astype(jnp.int32)


def seq_step(keep, send, bit, last, after=()):
    got = swap(send, "seq", mask_of(bit))
    rows, cols = keep.shape
    if last:
        return keep + got, None
    half = ((rows // 2, cols), F32)
    return run(k_add, [half, half], keep, got, after=after, flops=rows * cols, name="add")


def seq_sum(value, order):
    for bit in order:
        value = value + swap(value, "seq", mask_of(bit))
    return value


def head_sum(value):
    for bit in range(bits_of("head")):
        value = value + swap(value, "head", 1 << bit)
    return value


def carried(message, heads, reverse):
    count = bits_of("seq")
    shape = [(message.shape, F32)]
    flags = [
        ((1 - bit_of("seq", bit)) if reverse else bit_of("seq", bit)).reshape(1).astype(jnp.int32)
        for bit in range(count)
    ]
    ahead = None
    for bit in range(count - 1):
        got = swap(message, "seq", mask_of(bit))
        if ahead is None:
            ahead, message = run(
                functools.partial(k_scan_first, heads), shape * 2, message, got, small=[flags[bit]],
                flops=1000000, name="scan",
            )
        else:
            ahead, message = run(
                functools.partial(k_scan, heads), shape * 2, message, ahead, got,
                small=[flags[bit]], flops=1000000, name="scan",
            )
    return ahead, swap(message, "seq", mask_of(count - 1)), flags[count - 1]


def mm(left, right, dims):
    return lax.dot_general(left, right, (dims, ((), ())), preferred_element_type=F32)


def split2(value):
    high = value.astype(BF)
    return high, (value - high.astype(F32)).astype(BF)


def mm3(left, right, dims):
    lh, ll = split2(left)
    rh, rl = split2(right)
    return mm(lh, rh, dims) + (mm(lh, rl, dims) + mm(ll, rh, dims))


def split3(value):
    high = value.astype(BF)
    rest = value - high.astype(F32)
    mid = rest.astype(BF)
    return high, mid, (rest - mid.astype(F32)).astype(BF)


def sel_right(value, sel, dims):
    return sum(mm(part, sel, dims) for part in split3(value))


def sel_left(sel, value, dims):
    return sum(mm(sel, part, dims) for part in split3(value))


def head_map(heads, inner):
    chan = lax.broadcasted_iota(jnp.int32, (inner, heads), 0)
    head = lax.broadcasted_iota(jnp.int32, (inner, heads), 1)
    return jnp.where(chan // (inner // heads) == head, 1.0, 0.0).astype(BF)


def expand(value, emap):
    return sel_right(value, emap, NT)


def per_head(value, emap):
    return sel_right(value, emap, NN)


def lower(rows):
    row = lax.broadcasted_iota(jnp.int32, (rows, rows), 0)
    col = lax.broadcasted_iota(jnp.int32, (rows, rows), 1)
    return row >= col


def to_column(row_value):
    rows = row_value.shape[1]
    row = lax.broadcasted_iota(jnp.int32, (rows, rows), 0)
    col = lax.broadcasted_iota(jnp.int32, (rows, rows), 1)
    return jnp.sum(jnp.where(row == col, row_value, 0.0), axis=1, keepdims=True)


def row_sums(value):
    ones = jnp.ones((8, value.shape[1]), BF)
    return sel_left(ones, value, NT)[0:1, :]


def sigmoid(value):
    return 1.0 / (1.0 + jnp.exp(-value))


def silu(value):
    return value * sigmoid(value)


def silu_slope(value):
    sig = sigmoid(value)
    return sig * (1.0 + value * (1.0 - sig))


class Far:
    def __init__(self, value, layer=None):
        self.value, self.layer = value, layer
        self.shape = value.shape if layer is None else value.shape[1:]


def run(body, outs, *args, small=(), after=(), scratch=(), flops=2_000_000_000, name=None):
    held = pl.BlockSpec(memory_space=pltpu.VMEM)
    first, second = len(small), len(small) + len(args)
    far = [i for i, arg in enumerate(args) if isinstance(arg, Far)]
    layers = [arg.layer if isinstance(arg, Far) else None for arg in args]
    values = [arg.value if isinstance(arg, Far) else arg for arg in args]
    buffers = [pltpu.VMEM(args[i].shape, values[i].dtype) for i in far]
    if far:
        buffers = buffers + [pltpu.SemaphoreType.DMA((len(far),))]
    moved = sum(a.size * a.dtype.itemsize for a in values)

    def inner(*refs):
        given = list(refs[:second])
        rest = refs[second + len(after) :]
        if far:
            rest, fetched, sem = rest[: -len(far) - 1], rest[-len(far) - 1 : -1], rest[-1]
            copies = []
            for slot, i in enumerate(far):
                source = given[first + i]
                source = source if layers[i] is None else source.at[layers[i]]
                copies.append(pltpu.make_async_copy(source, fetched[slot], sem.at[slot]))
                given[first + i] = fetched[slot]
            for copy in copies:
                copy.start()
            for copy in copies:
                copy.wait()
        body(*given, *rest)

    return pl.pallas_call(
        inner,
        in_specs=[pl.BlockSpec(memory_space=pltpu.SMEM)] * first
        + [pl.BlockSpec(memory_space=pltpu.HBM) if i in far else held for i in range(len(args))]
        + [pl.BlockSpec(memory_space=pl.ANY)] * len(after),
        out_specs=[held] * len(outs),
        out_shape=[jax.ShapeDtypeStruct(shape, kind) for shape, kind in outs],
        scratch_shapes=list(scratch) + buffers,
        compiler_params=pltpu.CompilerParams(vmem_limit_bytes=GRANT),
        cost_estimate=pl.CostEstimate(flops=flops, bytes_accessed=moved, transcendentals=0),
        name=name,
    )(*small, *values, *after)


def rows_at(place, piece, size):
    return pl.ds(pl.multiple_of(place[piece], size), size)


def norm_rows(value, gain):
    return value * lax.rsqrt(jnp.mean(value * value, axis=1, keepdims=True) + eps) * gain


def k_add(keep, got, first, second):
    half = first.shape[0]
    first[...] = keep[0:half, :] + got[0:half, :]
    second[...] = keep[half:, :] + got[half:, :]


def merge(heads, flag, near, far, state, decay=None):
    rows = near.shape[0] - heads
    per = rows // heads
    use = flag[0] == 1
    for head in range(heads):
        cols = slice(head * per, (head + 1) * per)
        fade = near[rows + head : rows + head + 1, :]
        state[cols, :] = jnp.where(use, fade * far[cols, :] + near[cols, :], near[cols, :])
    if decay is not None:
        fades = near[rows:, :]
        decay[...] = jnp.where(use, fades * far[rows:, :], fades)


def k_scan_first(heads, flag, mine, got, ahead, total):
    rows = mine.shape[0] - heads
    use = flag[0] == 1
    ahead[0:rows, :] = jnp.where(use, got[0:rows, :], 0.0)
    ahead[rows:, :] = jnp.where(use, got[rows:, :], 1.0)
    join(heads, use, mine, got, total)


def join(heads, use, mine, got, total):
    rows = mine.shape[0] - heads
    per = rows // heads
    for head in range(heads):
        cols = slice(head * per, (head + 1) * per)
        own, other = mine[cols, :], got[cols, :]
        own_fade = mine[rows + head : rows + head + 1, :]
        got_fade = got[rows + head : rows + head + 1, :]
        total[cols, :] = jnp.where(use, own_fade * other + own, got_fade * own + other)
    total[rows:, :] = mine[rows:, :] * got[rows:, :]


def k_scan(heads, flag, mine, ahead, got, ahead_out, total):
    rows = mine.shape[0] - heads
    merge(heads, flag, ahead, got, ahead_out, ahead_out.at[pl.ds(rows, heads), :])
    join(heads, flag[0] == 1, mine, got, total)


def k_join(resid, keep, got, gain, total, normed):
    value = resid[...] + (keep[...] + got[...])
    total[...] = value
    normed[...] = norm_rows(value, gain[...])


def k_place(place, *refs):
    out = refs[-1]
    size = refs[0].shape[0]
    for piece, ref in enumerate(refs[:-1]):
        out[rows_at(place, piece, size), :] = ref[:, : out.shape[1]].astype(out.dtype)


def project(rounded, wz, wx, wbc, wdt, z, x, bc, dt):
    x[...] = mm(rounded, wx[...], NN)
    bc[...] = mm(rounded, wbc[...], NN)
    dt[...] = mm(rounded, wdt[...], NN)
    z[...] = mm(rounded, wz[...], NN)


def k_proj_first(hidden, gain, wz, wx, wbc, wdt, z, x, bc, dt, nb):
    rounded = norm_rows(hidden[...].astype(F32), gain[...]).astype(BF)
    nb[...] = rounded
    project(rounded, wz, wx, wbc, wdt, z, x, bc, dt)


def k_proj(place, *refs):
    pieces, (wz, wx, wbc, wdt, z, x, bc, dt, nb) = refs[:-9], refs[-9:]
    k_place(place, *pieces, nb)
    project(nb[...], wz, wx, wbc, wdt, z, x, bc, dt)


def conv_rows(ext, halo_rows, rows, weights, bias, aux):
    total = jnp.broadcast_to(bias, (rows, weights.shape[1]))
    taps = weights.shape[0]
    for tap in range(taps):
        part = ext[pl.ds(halo_rows - taps + 1 + tap, rows), :] * weights[tap : tap + 1, :]
        total = total + (part * aux[:, tap : tap + 1] if tap < taps - 1 else part)
    return total


def k_front(layer, x, bc, dt, edge, aux, cxw, cxb, cbw, cbb, dtb, alog,
            ux, ubc, dts, cum, cumt, msg, ext_x, ext_b):
    rows, inner = x.shape
    heads = dt.shape[1]
    width = bc.shape[1] // 2
    ext_x[0:HALO, :] = edge[:, :inner]
    ext_x[HALO:, :] = x[...]
    ext_b[0:HALO, :] = edge[:, inner:]
    ext_b[HALO:, :] = bc[...]
    masks = aux[...]
    conv_x = conv_rows(ext_x, HALO, rows, cxw[...], cxb[layer : layer + 1, :], masks)
    conv_b = conv_rows(ext_b, HALO, rows, cbw[...], cbb[layer : layer + 1, :], masks)
    ux[...] = conv_x
    ubc[...] = conv_b
    b_mat = silu(conv_b[:, :width])
    raw = dt[...] + dtb[layer : layer + 1, :]
    step = jnp.maximum(raw, 0.0) + jnp.log1p(jnp.exp(-jnp.abs(raw)))
    dts[...] = step
    decay = -step * jnp.exp(alog[layer : layer + 1, :])
    tri = jnp.where(lower(rows), 1.0, 0.0).astype(BF)
    total = sel_left(tri, decay, NN)
    total_t = sum(mm(part, tri, ((0,), (1,))) for part in split3(decay))
    cum[...] = total
    cumt[...] = total_t
    emap = head_map(heads, inner)
    to_end = jnp.exp(total[rows - 1 : rows, :] - total) * masks[:, 3:4] * step
    msg[0:inner, :] = mm3(silu(conv_x) * expand(to_end, emap), b_mat, TN)
    msg[inner:, :] = jnp.broadcast_to(
        jnp.exp(total_t[:, rows - 1 : rows]) * masks[rows - 1 : rows, 4:5], (heads, width)
    )


def head_kernel(cum, cumt, allowed, head):
    gap = cum[:, head : head + 1] - cumt[head : head + 1, :]
    return jnp.exp(jnp.where(allowed, gap, -1e30))


def k_intra(layer, ux, ubc, dts, cum, cumt, segc, segr, dskip, yp):
    rows, inner = ux.shape
    heads = dts.shape[1]
    width = ubc.shape[1] // 2
    per = inner // heads
    emap = head_map(heads, inner)
    x_conv = silu(ux[...])
    bc = silu(ubc[...])
    gram = mm3(bc[:, width:], bc[:, :width], NT)
    allowed = jnp.logical_and(segc[...] == segr[...], lower(rows))
    scaled = x_conv * expand(dts[...], emap)
    skip = x_conv * expand(jnp.broadcast_to(dskip[layer : layer + 1, :], (8, heads)), emap)[0:1, :]
    total, total_t = cum[...], cumt[...]
    group = max(1, 128 // per)
    for first in range(0, heads, group):
        cols = slice(first * per, (first + group) * per)
        sh, sl = split2(scaled[:, cols])
        lane = lax.broadcasted_iota(jnp.int32, (rows, group * per), 1)
        result = skip[:, cols]
        for head in range(first, first + group):
            gh, gl = split2(gram * head_kernel(total, total_t, allowed, head))
            part = mm(gh, sh, NN) + (mm(gh, sl, NN) + mm(gl, sh, NN))
            result = result + jnp.where(lane // per == head - first, part, 0.0)
        yp[:, cols] = result


def k_gate(flag, yp, ubc, cum, aux, z, near, far, mixed, gated, ss, inc):
    inner = yp.shape[1]
    heads = cum.shape[1]
    merge(heads, flag, near, far, inc)
    width = ubc.shape[1] // 2
    emap = head_map(heads, inner)
    c_mat = silu(ubc[:, width:])
    into = jnp.exp(cum[...]) * aux[:, 4:5]
    mix = yp[...] + mm3(c_mat, inc[...], NT) * expand(into, emap)
    mixed[...] = mix
    gate = mix * silu(z[...])
    gated[...] = gate
    ss[...] = row_sums(gate * gate)


def to_relative(place, source, target):
    pieces = place.shape[0]
    size = source.shape[0] // pieces
    for piece in range(pieces):
        target[piece * size : (piece + 1) * size, :] = source[rows_at(place, piece, size), :]


def k_out(layer, total, place, gated, ss, gain, wout, gn, keep, send, moved):
    scale = to_column(lax.rsqrt(ss[...] * (1.0 / total) + eps))
    normed = (gated[...] * scale * gain[layer : layer + 1, :]).astype(BF)
    gn[...] = normed
    to_relative(place, gn, moved)
    half = keep.shape[0]
    part = mm(moved[...], wout[...], NN)
    keep[...] = part[:half, :]
    send[...] = part[half:, :]


def k_b1_top(layer, total, cot, wout, gated, ss, gain, cb, dgn, cross, ggain):
    cb[...] = cot[...].astype(BF)
    back_out(layer, total, wout, gated, ss, gain, cb, dgn, ggain)
    scale_row = lax.rsqrt(ss[...] * (1.0 / total) + eps)
    cross[...] = scale_row * row_sums(dgn[...] * gated[...] * gain[layer : layer + 1, :])


def k_b1(layer, total, place, *refs):
    pieces, (wout, gated, ss, gain, cb, dgn, cross, ggain) = refs[:-8], refs[-8:]
    model = cb.shape[1]
    size = pieces[0].shape[0]
    for piece, ref in enumerate(pieces):
        rows = rows_at(place, piece, size)
        cb[rows, :] = ref[:, :model].astype(BF)
        cross[rows, :] = ref[:, model : model + 1]
    back_out(layer, total, wout, gated, ss, gain, cb, dgn, ggain)


def back_out(layer, total, wout, gated, ss, gain, cb, dgn, ggain):
    grad = mm(cb[...], wout[...], NT)
    dgn[...] = grad
    scale = to_column(lax.rsqrt(ss[...] * (1.0 / total) + eps))
    ggain[...] = jnp.sum(grad * gated[...] * scale, axis=0, keepdims=True)


def k_b2(layer, total, dgn, gated, mixed, z, ss, cross, gain, ubc, cum, cumt, aux, dm, dz, msg):
    rows, inner = dgn.shape
    heads = cum.shape[1]
    width = ubc.shape[1] // 2
    emap = head_map(heads, inner)
    scale_row = lax.rsqrt(ss[...] * (1.0 / total) + eps)
    scale = to_column(scale_row)
    dot = to_column(cross[...]) if cross.shape[0] == 1 else cross[...]
    pull = scale * scale * dot * (1.0 / total)
    d_gated = scale * gain[layer : layer + 1, :] * dgn[...] - gated[...] * pull
    zv = z[...]
    grad = d_gated * silu(zv)
    dm[...] = grad
    dz[...] = (d_gated * mixed[...] * silu_slope(zv)).astype(BF)
    masks = aux[...]
    into = jnp.exp(cum[...]) * masks[:, 4:5]
    msg[0:inner, :] = mm3(grad * expand(into, emap), silu(ubc[:, width:]), TN)
    msg[inner:, :] = jnp.broadcast_to(
        jnp.exp(cumt[:, rows - 1 : rows]) * masks[rows - 1 : rows, 4:5], (heads, width)
    )


def k_b3(layer, dm, ux, ubc, dts, cum, cumt, segc, segr, mixed, inc, aux, dskip,
         dx, dbc, dcum, ddt, gskip):
    rows, inner = ux.shape
    heads = dts.shape[1]
    width = ubc.shape[1] // 2
    per = inner // heads
    emap = head_map(heads, inner)
    x_conv = silu(ux[...])
    bc = silu(ubc[...])
    b_mat, c_mat = bc[:, :width], bc[:, width:]
    gram = mm3(c_mat, b_mat, NT)
    allowed = jnp.logical_and(segc[...] == segr[...], lower(rows))
    step = dts[...]
    step_e = expand(step, emap)
    scaled = x_conv * step_e
    grad = dm[...]
    total, total_t = cum[...], cumt[...]
    skip_row = dskip[layer : layer + 1, :]
    skip_e = expand(jnp.broadcast_to(skip_row, (8, heads)), emap)[0:1, :]
    d_gram = jnp.zeros((rows, rows), F32)
    group = max(1, 128 // per)
    plain = []
    for first in range(0, heads, group):
        cols = slice(first * per, (first + group) * per)
        sh, sl = split2(scaled[:, cols])
        lane = lax.broadcasted_iota(jnp.int32, (rows, group * per), 1)
        g_cols = grad[:, cols]
        ch, cl = split2(g_cols)
        result = jnp.zeros((rows, group * per), F32)
        for head in range(first, first + group):
            mine = lane // per == head - first
            fall = head_kernel(total, total_t, allowed, head)
            gh, gl = split2(gram * fall)
            part = mm(gh, ch, TN) + (mm(gh, cl, TN) + mm(gl, ch, TN))
            result = result + jnp.where(mine, part, 0.0)
            mh = jnp.where(mine, ch, jnp.zeros_like(ch))
            ml = jnp.where(mine, cl, jnp.zeros_like(cl))
            outer = mm(mh, sh, NT) + (mm(mh, sl, NT) + mm(ml, sh, NT))
            d_gram = d_gram + outer * fall
        plain.append(result)
    plain = jnp.concatenate(plain, axis=1)
    dx[...] = plain * step_e + grad * skip_e
    into = jnp.exp(total) * aux[:, 4:5]
    dbc[:, :width] = mm3(d_gram, c_mat, TN)
    dbc[:, width:] = mm3(d_gram, b_mat, NN) + mm3(grad * expand(into, emap), inc[...], NN)
    by_col = per_head(x_conv * plain, emap)
    skip_dot = per_head(grad * x_conv, emap)
    ddt[...] = by_col
    dcum[...] = per_head(grad * mixed[...], emap) - skip_row * skip_dot - step * by_col
    gskip[...] = jnp.sum(skip_dot, axis=0, keepdims=True)


def k_b4(layer, flag, ux, ubc, dts, dtp, cum, aux, dx, dbc, dcum, ddt, near, far, inc, dtb, alog,
         du, dbo, dd, gdtb, galog, edge, df):
    rows, inner = ux.shape
    heads = dts.shape[1]
    width = ubc.shape[1] // 2
    merge(heads, flag, near, far, df)
    emap = head_map(heads, inner)
    conv = ux[...]
    x_conv = silu(conv)
    b_mat = silu(ubc[:, :width])
    total, step, masks = cum[...], dts[...], aux[...]
    fin = df[...]
    spread = mm3(b_mat, fin, NT)
    bare = jnp.exp(total[rows - 1 : rows, :] - total) * masks[:, 3:4]
    to_end = bare * step
    to_end_e = expand(to_end, emap)
    dot = per_head(x_conv * spread, emap)
    du[...] = (dx[...] + to_end_e * spread) * silu_slope(conv)
    slope = silu_slope(ubc[...])
    dbo[:, :width] = (dbc[:, :width] + mm3(x_conv * to_end_e, fin, NN)) * slope[:, :width]
    dbo[:, width:] = dbc[:, width:] * slope[:, width:]
    edge[:, :inner] = du[0:HALO, :]
    edge[:, inner:] = dbo[0:HALO, :]
    used = to_end * dot
    d_cum = dcum[...] - used
    through = per_head(row_sums(fin * inc[...]) + jnp.zeros((8, inner), F32), emap)[0:1, :]
    last = jnp.sum(used, axis=0, keepdims=True) + through * (
        jnp.exp(total[rows - 1 : rows, :]) * masks[rows - 1 : rows, 4:5]
    )
    tri = jnp.where(lower(rows), 1.0, 0.0).astype(BF)
    d_decay = sel_left(tri, d_cum, TN) + last
    rate = jnp.exp(alog[layer : layer + 1, :])
    galog[...] = jnp.sum(-step * rate * d_decay, axis=0, keepdims=True)
    d_raw = (ddt[...] + bare * dot - rate * d_decay) * sigmoid(dtp[...] + dtb[layer : layer + 1, :])
    gdtb[...] = jnp.sum(d_raw, axis=0, keepdims=True)
    dd[...] = d_raw.astype(BF)


def k_conv_back(du, halo, proj, edge, aux, weights, grad, gw, gb, ext_d, ext_p):
    rows = du.shape[0]
    ext_d[0:rows, :] = du[...]
    ext_d[rows:, :] = halo[...]
    conv_back(proj, edge, aux, weights, grad, gw, gb, ext_d, ext_p)


def k_conv_back_b(which, du, proj, edge, aux, weights, grad, gw, gb, part, ext_d, ext_p):
    quarter = du.shape[1]
    for slot in range(ext_d.shape[1] // quarter):
        cols = slice(slot * quarter, (slot + 1) * quarter)
        ext_d[:, cols] = jnp.where(which[0] == slot, du[...], 0.0)
    wide = conv_back(proj, edge, aux, weights, grad, gw, gb, ext_d, ext_p)
    part[...] = sum(
        wide[:, slot * quarter : (slot + 1) * quarter] for slot in range(ext_d.shape[1] // quarter)
    ).astype(BF)


def conv_back(proj, edge, aux, weights, grad, gw, gb, ext_d, ext_p):
    rows = proj.shape[0]
    taps = weights.shape[0]
    ext_p[0:HALO, :] = edge[...]
    ext_p[HALO:, :] = proj[...]
    masks = aux[...]
    value = ext_d[0:rows, :]
    total = jnp.zeros_like(value)
    for tap in range(taps):
        back = ext_d[pl.ds(taps - 1 - tap, rows), :] * weights[tap : tap + 1, :]
        seen = ext_p[pl.ds(HALO - taps + 1 + tap, rows), :] * value
        if tap < taps - 1:
            back = back * masks[:, 5 + tap : 6 + tap]
            seen = seen * masks[:, tap : tap + 1]
        total = total + back
        gw[tap : tap + 1, :] = jnp.sum(seen, axis=0, keepdims=True)
    gb[...] = jnp.sum(value, axis=0, keepdims=True)
    grad[...] = total.astype(BF)
    return total


def k_dnorm(place, dz, dxb, dd, dbq, wz, wx, wdt, wbq, keep, send, own, moved):
    own[...] = (
        mm(dz[...], wz[...], NT)
        + mm(dxb[...], wx[...], NT)
        + mm(dd[...], wdt[...], NT)
        + mm(dbq[...], wbq[...], NT)
    )
    to_relative(place, own, moved)
    half = keep.shape[0]
    keep[...] = moved[0:half, :]
    send[...] = moved[half:, :]


def k_norm_back(resid, keep, got, gain, cot, branch, packed, g_gain):
    grad = keep[...] + got[...]
    value = resid[...]
    inv = lax.rsqrt(jnp.mean(value * value, axis=1, keepdims=True) + eps)
    unit = value * inv
    g_gain[...] = jnp.sum(grad * unit, axis=0, keepdims=True)
    scaled = grad * gain[...]
    mean = jnp.mean(scaled * unit, axis=1, keepdims=True)
    total = cot[...] + inv * (scaled - unit * mean)
    model = value.shape[1]
    packed[:, :model] = total
    if branch is not None:
        rounded = total.astype(BF).astype(F32)
        dot = jnp.sum(rounded * branch[...], axis=1, keepdims=True)
        packed[:, model:] = jnp.broadcast_to(dot, (value.shape[0], packed.shape[1] - model))


def drop_branch(body, *refs):
    body(*refs[:5], None, *refs[5:])


def k_dw(place, left, *refs):
    rights, (keep, send, moved, full) = refs[:-4], refs[-4:]
    pieces = place.shape[0]
    size = left.shape[1] // pieces
    half = keep.shape[0]
    aligned = size % 128 == 0
    if aligned:
        for piece in range(pieces):
            moved[:, piece * size : (piece + 1) * size] = left[:, rows_at(place, piece, size)]
    start = 0
    for right in rights:
        cols = slice(start, start + right.shape[1])
        start += right.shape[1]
        if aligned:
            keep[:, cols] = mm(moved[:, :half], right[...], TN)
            send[:, cols] = mm(moved[:, half:], right[...], TN)
        else:
            full[:, cols] = mm(left[...], right[...], TN)
    if not aligned:
        for piece in range(pieces):
            target, row = (keep, piece) if piece < pieces // 2 else (send, piece - pieces // 2)
            target[row * size : (row + 1) * size, :] = full[rows_at(place, piece, size), :]


def local(hidden_in, seg_ids, norm_gain, w_z, w_x, w_bc, w_dt, conv_x_w, conv_x_b, conv_bc_w,
          conv_bc_b, dt_bias, a_log, d_skip, gate_gain, w_out, out_cot):
    rows, model = hidden_in.shape
    layers = w_z.shape[0]
    heads = w_dt.shape[2]
    inner = w_z.shape[2]
    state2 = w_bc.shape[2]
    width = state2 // 2
    taps = conv_x_w.shape[1]
    inner_total = inner * lax.axis_size("head")
    seq_bits = bits_of("seq")
    spare = list(range(3, seq_bits))
    orders = [
        [bit for bit in base if bit < seq_bits] + spare
        for base in ([0, 1, 2], [1, 2, 0], [2, 0, 1])
    ]
    share = model // lax.axis_size("seq")
    places = [seq_places(order, share) for order in orders]
    head_bits = bits_of("head")
    size = rows // lax.axis_size("head")
    place = jnp.stack(
        [
            reverse_bits(lax.axis_index("head") ^ mask, head_bits) * size
            for mask in relative_order(head_bits)
        ]
    ).astype(jnp.int32)

    padded = jnp.concatenate(
        [jnp.full((taps - 1,), -1, jnp.int32), seg_ids, jnp.full((taps - 1,), -1, jnp.int32)]
    )
    around = lax.dynamic_slice_in_dim(
        padded, lax.axis_index("seq") * rows, rows + 2 * (taps - 1)
    )
    own = around[taps - 1 : taps - 1 + rows]
    seg_before = around[taps - 2]
    columns = [around[k : k + rows] == own for k in range(taps - 1)]
    columns += [own == own[rows - 1], own == seg_before]
    columns += [around[2 * (taps - 1) - k : 2 * (taps - 1) - k + rows] == own for k in range(taps - 1)]
    aux = jnp.stack(columns, axis=1).astype(F32)
    segc, segr = own[:, None], own[None, :]

    own_quarter = reverse_bits(lax.axis_index("head"), head_bits).reshape(1).astype(jnp.int32)
    half_rows = ((rows // 2, model), F32)
    quarter_rows = ((size, model), F32)
    proj_outs = [((rows, inner), F32), ((rows, inner), F32), ((rows, state2), F32),
                 ((rows, heads), F32), ((rows, model), BF)]
    message = ((inner + heads, width), F32)

    resid = own_piece(hidden_in, "head", 0).astype(F32)
    normed = None
    saved = []
    for l in range(layers):
        weights = (Far(w_z, l), Far(w_x, l), Far(w_bc, l), Far(w_dt, l))
        if l == 0:
            z, x, bc, dtp, nb = run(
                k_proj_first, proj_outs, hidden_in, norm_gain[l : l + 1], *weights, name="proj"
            )
        else:
            z, x, bc, dtp, nb = run(
                k_proj, proj_outs, *gather_pieces(normed, "head"), *weights, small=[place],
                name="proj",
            )
        edge = rotate(jnp.concatenate([x[rows - HALO :], bc[rows - HALO :]], 1), "seq", 1)
        ux, ubc, dts, cum, cumt, msg = run(
            functools.partial(k_front, l),
            [((rows, inner), F32), ((rows, state2), F32), ((rows, heads), F32),
             ((rows, heads), F32), ((heads, rows), F32), message],
            x, bc, dtp, edge, aux, conv_x_w[l], conv_x_b, conv_bc_w[l], conv_bc_b, dt_bias, a_log,
            scratch=(pltpu.VMEM((rows + HALO, inner), F32), pltpu.VMEM((rows + HALO, state2), F32)),
            name="front",
        )
        near, far, flag = carried(msg, heads, False)
        (yp,) = run(
            functools.partial(k_intra, l), [((rows, inner), F32)],
            ux, ubc, dts, cum, cumt, segc, segr, d_skip, name="intra",
        )
        mixed, gated, ss, inc = run(
            k_gate,
            [((rows, inner), F32), ((rows, inner), F32), ((1, rows), F32), ((inner, width), F32)],
            yp, ubc, cum, aux, z, near, far, small=[flag], name="gate",
        )
        ss = lax.psum(ss, "head")
        gn, keep, send = run(
            functools.partial(k_out, l, inner_total),
            [((rows, inner), BF), half_rows, half_rows],
            gated, ss, gate_gain, Far(w_out, l), small=[place],
            scratch=(pltpu.VMEM((rows, inner), BF),), name="out",
        )
        keep, got = finish_scatter(keep, send, "head")
        saved.append((resid, z, x, bc, dtp, nb, edge, ux, ubc, dts, cum, cumt, inc, mixed, gated,
                      ss, gn, keep + got))
        last = l + 1 == layers
        resid, normed = run(
            k_join, [quarter_rows, quarter_rows], resid, keep, got,
            norm_gain[0 if last else l + 1][None, :], flops=1000000, name="join",
        )
    (hidden_out,) = run(
        k_place, [((rows, model), BF)], *gather_pieces(resid, "head"), small=[place],
        flops=1000000, name="round",
    )

    def dw_scratch(cols):
        aligned = share % 128 == 0
        return (
            pltpu.VMEM((rows, model if aligned else 128), BF),
            pltpu.VMEM((8 if aligned else model, cols), F32),
        )

    cot = own_piece(out_cot, "head", 0)
    packed = None
    final = [[None] * layers for _ in range(3)]
    narrow_in = [None] * layers
    small = [None] * layers
    gains = [None] * layers
    waiting = []
    block = (model // 2, inner)
    for l in reversed(range(layers)):
        (resid, z, x, bc, dtp, nb, edge, ux, ubc, dts, cum, cumt, inc, mixed, gated, ss, gn,
         branch) = saved[l]
        b1_outs = [((rows, model), BF), ((rows, inner), F32)]
        if packed is None:
            cb, dgn, cross, ggain = run(
                functools.partial(k_b1_top, l, inner_total),
                b1_outs + [((1, rows), F32), ((1, inner), F32)],
                out_cot, Far(w_out, l), Far(gated), ss, gate_gain, name="b1",
            )
            cross = lax.psum(cross, "head")
        else:
            cb, dgn, cross, ggain = run(
                functools.partial(k_b1, l, inner_total),
                b1_outs + [((rows, 1), F32), ((1, inner), F32)],
                *gather_pieces(packed, "head"), Far(w_out, l), Far(gated), ss, gate_gain, small=[place],
                name="b1",
            )
        dm, dz, msg = run(
            functools.partial(k_b2, l, inner_total),
            [((rows, inner), F32), ((rows, inner), BF), message],
            dgn, Far(gated), Far(mixed), Far(z), ss, cross, gate_gain, Far(ubc), Far(cum), Far(cumt), aux,
            after=waiting,
            name="b2",
        )
        near, far, flag = carried(msg, heads, True)
        dx, dbc, dcum, ddt, gskip = run(
            functools.partial(k_b3, l),
            [((rows, inner), F32), ((rows, state2), F32), ((rows, heads), F32),
             ((rows, heads), F32), ((1, heads), F32)],
            dm, Far(ux), Far(ubc), Far(dts), Far(cum), Far(cumt), segc, segr, Far(mixed), Far(inc), aux,
            d_skip, name="b3",
        )
        du, dub, dd, gdtb, galog, first_rows = run(
            functools.partial(k_b4, l),
            [((rows, inner), F32), ((rows, state2), F32), ((rows, heads), BF),
             ((1, heads), F32), ((1, heads), F32), ((HALO, inner + state2), F32)],
            Far(ux), Far(ubc), Far(dts), Far(dtp), Far(cum), aux, dx, dbc, dcum, ddt, near, far,
            Far(inc), dt_bias, a_log,
            small=[flag], scratch=(pltpu.VMEM((inner, width), F32),), name="b4",
        )
        halo = rotate(first_rows, "seq", -1)
        dub = scatter_cols(jnp.concatenate([dub, halo[:, inner:]], 0), "head")
        quarter = dub.shape[1]
        dxb, gcw, gcb = run(
            k_conv_back,
            [((rows, inner), BF), ((taps, inner), F32), ((1, inner), F32)],
            du, halo[:, :inner], Far(x), edge[:, :inner], aux, conv_x_w[l],
            scratch=(pltpu.VMEM((rows + HALO, inner), F32), pltpu.VMEM((rows + HALO, inner), F32)),
            name="convx",
        )
        dbw, gbw, gbb, dbb = run(
            k_conv_back_b,
            [((rows, state2), BF), ((taps, state2), F32), ((1, state2), F32), ((rows, quarter), BF)],
            dub, Far(bc), edge[:, inner:], aux, conv_bc_w[l], small=[own_quarter],
            scratch=(pltpu.VMEM((rows + HALO, state2), F32),
                     pltpu.VMEM((rows + HALO, state2), F32)),
            name="convb",
        )
        keep, send = run(
            k_dnorm, [half_rows, half_rows],
            dz, dxb, dd, dbw, Far(w_z, l), Far(w_x, l), Far(w_dt, l), Far(w_bc, l), small=[place],
            scratch=(pltpu.VMEM((rows, model), F32), pltpu.VMEM((rows, model), F32)), name="dnorm",
        )
        keep, got = finish_scatter(keep, send, "head")
        cols = model + 128 if l > 0 else model
        body = k_norm_back if l > 0 else functools.partial(drop_branch, k_norm_back)
        cot_args = (resid, keep, got, norm_gain[l : l + 1], cot)
        packed, gains[l] = run(
            body, [((size, cols), F32), ((1, model), F32)],
            *(cot_args + ((saved[l - 1][-1],) if l > 0 else ())), flops=1000000, name="normback",
        )
        cot = packed[:, :model]

        def product(slot, left, right, after):
            return run(
                k_dw, [(block, F32), (block, F32)], left, right, small=[places[slot]],
                after=after, scratch=dw_scratch(inner), name="dw",
            )

        steps = [
            product(2, cb, Far(gn), [halo]),
            product(0, Far(nb), dz, [halo]),
            product(1, Far(nb), dxb, []),
        ]
        slots = (2, 0, 1)
        waiting = []
        for slot, (keep, send) in zip(slots, steps):
            for index, bit in enumerate(orders[slot]):
                ended = index + 1 == seq_bits
                keep, send = seq_step(keep, send, bit, ended)
            final[slot][l] = keep
            if slot != 1:
                waiting.append(keep)
        narrow_in[l] = (Far(nb), dbb, dd)
        small[l] = (gcw, gcb, gbw, gbb, gdtb, galog, gskip, ggain)
    (grad_in,) = run(
        k_place, [((rows, model), F32)], *gather_pieces(cot, "head"), small=[place],
        flops=1000000, name="place",
    )

    narrow = [
        run(
            k_dw, [((model // 2, quarter + heads), F32)] * 2, *narrow_in[l], small=[places[0]],
            scratch=dw_scratch(quarter + heads), name="dwn",
        )
        for l in range(layers)
    ]
    keep = jnp.concatenate([pair[0] for pair in narrow], 1)
    send = jnp.concatenate([pair[1] for pair in narrow], 1)
    for index, bit in enumerate(orders[0]):
        keep, send = seq_step(keep, send, bit, index + 1 == seq_bits)
    narrow = jnp.stack(jnp.split(keep, layers, 1))

    def reduced(flat, order):
        sizes = [part.size for part in flat]
        pack = jnp.concatenate([part.reshape(-1) for part in flat])
        pack = jnp.pad(pack, (0, -pack.size % 1024)).reshape(-1, 128)
        pack = seq_sum(pack, order).reshape(-1)
        pieces, start = [], 0
        for count in sizes:
            pieces.append(pack[start : start + count])
            start += count
        return pieces

    pieces = reduced([part for l in range(layers) for part in small[l]], orders[1])
    count = len(small[0])

    def both(slot):
        return jnp.stack([pieces[l * count + slot].reshape(small[l][slot].shape) for l in range(layers)])

    wide = jnp.concatenate(
        [seq_sum(jnp.concatenate(gains, 0), orders[2]).reshape(-1), both(2).reshape(-1),
         both(3).reshape(-1)]
    )
    wide = head_sum(wide.reshape(-1, 128)).reshape(-1)
    stop = layers * model
    grad_gain = wide[:stop].reshape(layers, model)
    grad_gain = lax.dynamic_slice_in_dim(grad_gain, lax.axis_index("seq") * share, share, 1)
    bc_w = wide[stop : stop + layers * taps * state2].reshape(layers, taps, state2)
    bc_b = wide[stop + layers * taps * state2 :].reshape(layers, state2)
    bc_parts = gather_back(narrow[:, :, :quarter], "head", 2)
    return (
        hidden_out,
        grad_in,
        grad_gain,
        jnp.stack(final[0]),
        jnp.stack(final[1]),
        bc_parts,
        narrow[:, :, quarter:],
        both(0),
        both(1)[:, 0],
        bc_w,
        bc_b,
        both(4)[:, 0],
        both(5)[:, 0],
        both(6)[:, 0],
        both(7)[:, 0],
        jnp.stack([part.T for part in final[2]]),
    )


def solution(mesh):
    return jax.shard_map(
        local,
        mesh=mesh,
        in_specs=(
            P("seq", None),
            P(),
            P(),
            P(None, None, "head"),
            P(None, None, "head"),
            P(),
            P(None, None, "head"),
            P(None, None, "head"),
            P(None, "head"),
            P(),
            P(),
            P(None, "head"),
            P(None, "head"),
            P(None, "head"),
            P(None, "head"),
            P(None, "head", None),
            P("seq", None),
        ),
        out_specs=(
            P("seq", None),
            P("seq", None),
            P(None, "seq"),
            P(None, "seq", "head"),
            P(None, "seq", "head"),
            P(None, "seq", None),
            P(None, "seq", "head"),
            P(None, None, "head"),
            P(None, "head"),
            P(),
            P(),
            P(None, "head"),
            P(None, "head"),
            P(None, "head"),
            P(None, "head"),
            P(None, "head", "seq"),
        ),
        check_vma=False,
    )
```

```python
import functools

import jax
import jax.numpy as jnp
from jax import lax
from jax.experimental import pallas as pl
from jax.experimental.pallas import tpu as pltpu
from jax.sharding import PartitionSpec as P

eps = 1e-05
F32, BF = jnp.float32, jnp.bfloat16
NN, NT, TN = ((1,), (0,)), ((1,), (1,)), ((0,), (0,))
HALO = 8
GRANT = 24 << 20


def swap(value, axis, mask):
    count = lax.axis_size(axis)
    return lax.ppermute(value, axis, [(i, i ^ mask) for i in range(count)])


def rotate(value, axis, steps):
    count = lax.axis_size(axis)
    return lax.ppermute(value, axis, [(i, (i + steps) % count) for i in range(count)])


def bit_of(axis, bit):
    return (lax.axis_index(axis) >> bit) & 1


def bits_of(axis):
    return lax.axis_size(axis).bit_length() - 1


def reverse_bits(value, count):
    result = 0
    for bit in range(count):
        result = result | (((value >> bit) & 1) << (count - 1 - bit))
    return result


def relative_order(count):
    return [reverse_bits(i, count) for i in range(1 << count)]


def finish_scatter(keep, send, axis):
    for bit in range(bits_of(axis)):
        got = swap(send, axis, 1 << bit)
        half = keep.shape[0] // 2
        if bit + 1 < bits_of(axis):
            send = keep[half:] + got[half:]
            keep = keep[:half] + got[:half]
    return keep, got


def scatter_cols(value, axis):
    for bit in range(bits_of(axis)):
        half = value.shape[1] // 2
        which = bit_of(axis, bit)
        keep = lax.dynamic_slice_in_dim(value, which * half, half, 1)
        send = lax.dynamic_slice_in_dim(value, (1 - which) * half, half, 1)
        value = keep + swap(send, axis, 1 << bit)
    return value


def gather_pieces(mine, axis):
    pieces = [mine]
    for bit in reversed(range(bits_of(axis))):
        pieces = pieces + [swap(piece, axis, 1 << bit) for piece in pieces]
    return pieces


def gather_back(value, axis, dim):
    for bit in reversed(range(bits_of(axis))):
        other = swap(value, axis, 1 << bit)
        first = bit_of(axis, bit) == 0
        value = jnp.where(
            first,
            jnp.concatenate([value, other], dim),
            jnp.concatenate([other, value], dim),
        )
    return value


def own_piece(value, axis, dim):
    for bit in range(bits_of(axis)):
        half = value.shape[dim] // 2
        value = lax.dynamic_slice_in_dim(value, bit_of(axis, bit) * half, half, dim)
    return value


def mask_of(bit):
    return 1 << bit


def seq_places(order, share):
    count = len(order)
    me = lax.axis_index("seq")
    starts = []
    for piece in range(1 << count):
        mask = 0
        for step, bit in enumerate(order):
            if (piece >> (count - 1 - step)) & 1:
                mask ^= mask_of(bit)
        starts.append((me ^ mask) * share)
    return jnp.stack(starts).astype(jnp.int32)


class SeqScatter:
    def __init__(self, order, keep, send):
        self.order, self.keep, self.step = order, keep, 0
        self.got = swap(send, "seq", mask_of(order[0]))

    def advance(self, after=()):
        self.step += 1
        if self.step == len(self.order):
            self.keep = self.keep + self.got
        elif self.step < len(self.order):
            rows, cols = self.keep.shape
            half = ((rows // 2, cols), F32)
            self.keep, send = run(
                k_add, [half, half], self.keep, self.got, after=after, flops=rows * cols, name="add"
            )
            self.got = swap(send, "seq", mask_of(self.order[self.step]))

    def result(self, after=()):
        while self.step < len(self.order):
            self.advance(after)
        return self.keep


def seq_sum(value, order):
    for bit in order:
        value = value + swap(value, "seq", mask_of(bit))
    return value


def head_sum(value):
    for bit in range(bits_of("head")):
        value = value + swap(value, "head", 1 << bit)
    return value


def carried(message, heads, reverse):
    count = bits_of("seq")
    shape = [(message.shape, F32)]
    flags = [
        ((1 - bit_of("seq", bit)) if reverse else bit_of("seq", bit)).reshape(1).astype(jnp.int32)
        for bit in range(count)
    ]
    ahead = None
    for bit in range(count - 1):
        got = swap(message, "seq", mask_of(bit))
        if ahead is None:
            ahead, message = run(
                functools.partial(k_scan_first, heads), shape * 2, message, got, small=[flags[bit]],
                flops=1000000, name="scan",
            )
        else:
            ahead, message = run(
                functools.partial(k_scan, heads), shape * 2, message, ahead, got,
                small=[flags[bit]], flops=1000000, name="scan",
            )
    return ahead, swap(message, "seq", mask_of(count - 1)), flags[count - 1]


def mm(left, right, dims):
    return lax.dot_general(left, right, (dims, ((), ())), preferred_element_type=F32)


def split2(value):
    high = value.astype(BF)
    return high, (value - high.astype(F32)).astype(BF)


def mm3(left, right, dims):
    lh, ll = split2(left)
    rh, rl = split2(right)
    return mm(lh, rh, dims) + (mm(lh, rl, dims) + mm(ll, rh, dims))


def split3(value):
    high = value.astype(BF)
    rest = value - high.astype(F32)
    mid = rest.astype(BF)
    return high, mid, (rest - mid.astype(F32)).astype(BF)


def sel_right(value, sel, dims):
    return sum(mm(part, sel, dims) for part in split3(value))


def sel_left(sel, value, dims):
    return sum(mm(sel, part, dims) for part in split3(value))


def head_map(heads, inner):
    chan = lax.broadcasted_iota(jnp.int32, (inner, heads), 0)
    head = lax.broadcasted_iota(jnp.int32, (inner, heads), 1)
    return jnp.where(chan // (inner // heads) == head, 1.0, 0.0).astype(BF)


def expand(value, emap):
    return sel_right(value, emap, NT)


def per_head(value, emap):
    return sel_right(value, emap, NN)


def lower(rows):
    row = lax.broadcasted_iota(jnp.int32, (rows, rows), 0)
    col = lax.broadcasted_iota(jnp.int32, (rows, rows), 1)
    return row >= col


def to_column(row_value):
    rows = row_value.shape[1]
    row = lax.broadcasted_iota(jnp.int32, (rows, rows), 0)
    col = lax.broadcasted_iota(jnp.int32, (rows, rows), 1)
    return jnp.sum(jnp.where(row == col, row_value, 0.0), axis=1, keepdims=True)


def row_sums(value):
    ones = jnp.ones((8, value.shape[1]), BF)
    return sel_left(ones, value, NT)[0:1, :]


def sigmoid(value):
    return 1.0 / (1.0 + jnp.exp(-value))


def silu(value):
    return value * sigmoid(value)


def silu_slope(value):
    sig = sigmoid(value)
    return sig * (1.0 + value * (1.0 - sig))


class Far:
    def __init__(self, value, layer=None):
        self.value, self.layer = value, layer
        self.shape = value.shape if layer is None else value.shape[1:]


def run(body, outs, *args, small=(), after=(), scratch=(), flops=2_000_000_000, name=None):
    held = pl.BlockSpec(memory_space=pltpu.VMEM)
    first, second = len(small), len(small) + len(args)
    far = [i for i, arg in enumerate(args) if isinstance(arg, Far)]
    layers = [arg.layer if isinstance(arg, Far) else None for arg in args]
    values = [arg.value if isinstance(arg, Far) else arg for arg in args]
    buffers = [pltpu.VMEM(args[i].shape, values[i].dtype) for i in far]
    if far:
        buffers = buffers + [pltpu.SemaphoreType.DMA((len(far),))]
    moved = sum(a.size * a.dtype.itemsize for a in values)

    def inner(*refs):
        given = list(refs[:second])
        rest = refs[second + len(after) :]
        if far:
            rest, fetched, sem = rest[: -len(far) - 1], rest[-len(far) - 1 : -1], rest[-1]
            copies = []
            for slot, i in enumerate(far):
                source = given[first + i]
                source = source if layers[i] is None else source.at[layers[i]]
                copies.append(pltpu.make_async_copy(source, fetched[slot], sem.at[slot]))
                given[first + i] = fetched[slot]
            for copy in copies:
                copy.start()
            for copy in copies:
                copy.wait()
        body(*given, *rest)

    return pl.pallas_call(
        inner,
        in_specs=[pl.BlockSpec(memory_space=pltpu.SMEM)] * first
        + [pl.BlockSpec(memory_space=pltpu.HBM) if i in far else held for i in range(len(args))]
        + [pl.BlockSpec(memory_space=pl.ANY)] * len(after),
        out_specs=[held] * len(outs),
        out_shape=[jax.ShapeDtypeStruct(shape, kind) for shape, kind in outs],
        scratch_shapes=list(scratch) + buffers,
        compiler_params=pltpu.CompilerParams(vmem_limit_bytes=GRANT),
        cost_estimate=pl.CostEstimate(flops=flops, bytes_accessed=moved, transcendentals=0),
        name=name,
    )(*small, *values, *after)


def rows_at(place, piece, size):
    return pl.ds(pl.multiple_of(place[piece], size), size)


def norm_rows(value, gain):
    return value * lax.rsqrt(jnp.mean(value * value, axis=1, keepdims=True) + eps) * gain


def k_add(keep, got, first, second):
    half = first.shape[0]
    first[...] = keep[0:half, :] + got[0:half, :]
    second[...] = keep[half:, :] + got[half:, :]


def merge(heads, flag, near, far, state, decay=None):
    rows = near.shape[0] - heads
    per = rows // heads
    use = flag[0] == 1
    for head in range(heads):
        cols = slice(head * per, (head + 1) * per)
        fade = near[rows + head : rows + head + 1, :]
        state[cols, :] = jnp.where(use, fade * far[cols, :] + near[cols, :], near[cols, :])
    if decay is not None:
        fades = near[rows:, :]
        decay[...] = jnp.where(use, fades * far[rows:, :], fades)


def k_scan_first(heads, flag, mine, got, ahead, total):
    rows = mine.shape[0] - heads
    use = flag[0] == 1
    ahead[0:rows, :] = jnp.where(use, got[0:rows, :], 0.0)
    ahead[rows:, :] = jnp.where(use, got[rows:, :], 1.0)
    join(heads, use, mine, got, total)


def join(heads, use, mine, got, total):
    rows = mine.shape[0] - heads
    per = rows // heads
    for head in range(heads):
        cols = slice(head * per, (head + 1) * per)
        own, other = mine[cols, :], got[cols, :]
        own_fade = mine[rows + head : rows + head + 1, :]
        got_fade = got[rows + head : rows + head + 1, :]
        total[cols, :] = jnp.where(use, own_fade * other + own, got_fade * own + other)
    total[rows:, :] = mine[rows:, :] * got[rows:, :]


def k_scan(heads, flag, mine, ahead, got, ahead_out, total):
    rows = mine.shape[0] - heads
    merge(heads, flag, ahead, got, ahead_out, ahead_out.at[pl.ds(rows, heads), :])
    join(heads, flag[0] == 1, mine, got, total)


def k_join(resid, keep, got, gain, total, normed):
    value = resid[...] + (keep[...] + got[...])
    total[...] = value
    normed[...] = norm_rows(value, gain[...])


def k_place(place, *refs):
    out = refs[-1]
    size = refs[0].shape[0]
    for piece, ref in enumerate(refs[:-1]):
        out[rows_at(place, piece, size), :] = ref[:, : out.shape[1]].astype(out.dtype)


def project(rounded, wz, wx, wbc, wdt, z, x, bc, dt):
    x[...] = mm(rounded, wx[...], NN)
    bc[...] = mm(rounded, wbc[...], NN)
    dt[...] = mm(rounded, wdt[...], NN)
    z[...] = mm(rounded, wz[...], NN)


def k_proj_first(hidden, gain, wz, wx, wbc, wdt, z, x, bc, dt, nb):
    rounded = norm_rows(hidden[...].astype(F32), gain[...]).astype(BF)
    nb[...] = rounded
    project(rounded, wz, wx, wbc, wdt, z, x, bc, dt)


def k_proj(place, *refs):
    pieces, (wz, wx, wbc, wdt, z, x, bc, dt, nb) = refs[:-9], refs[-9:]
    k_place(place, *pieces, nb)
    project(nb[...], wz, wx, wbc, wdt, z, x, bc, dt)


def conv_rows(ext, halo_rows, rows, weights, bias, aux):
    total = jnp.broadcast_to(bias, (rows, weights.shape[1]))
    taps = weights.shape[0]
    for tap in range(taps):
        part = ext[pl.ds(halo_rows - taps + 1 + tap, rows), :] * weights[tap : tap + 1, :]
        total = total + (part * aux[:, tap : tap + 1] if tap < taps - 1 else part)
    return total


def k_front(layer, x, bc, dt, edge, aux, cxw, cxb, cbw, cbb, dtb, alog,
            ux, ubc, dts, cum, cumt, msg, ext_x, ext_b):
    rows, inner = x.shape
    heads = dt.shape[1]
    width = bc.shape[1] // 2
    ext_x[0:HALO, :] = edge[:, :inner]
    ext_x[HALO:, :] = x[...]
    ext_b[0:HALO, :] = edge[:, inner:]
    ext_b[HALO:, :] = bc[...]
    masks = aux[...]
    conv_x = conv_rows(ext_x, HALO, rows, cxw[...], cxb[layer : layer + 1, :], masks)
    conv_b = conv_rows(ext_b, HALO, rows, cbw[...], cbb[layer : layer + 1, :], masks)
    ux[...] = conv_x
    ubc[...] = conv_b
    b_mat = silu(conv_b[:, :width])
    raw = dt[...] + dtb[layer : layer + 1, :]
    step = jnp.maximum(raw, 0.0) + jnp.log1p(jnp.exp(-jnp.abs(raw)))
    dts[...] = step
    decay = -step * jnp.exp(alog[layer : layer + 1, :])
    tri = jnp.where(lower(rows), 1.0, 0.0).astype(BF)
    total = sel_left(tri, decay, NN)
    total_t = sum(mm(part, tri, ((0,), (1,))) for part in split3(decay))
    cum[...] = total
    cumt[...] = total_t
    emap = head_map(heads, inner)
    to_end = jnp.exp(total[rows - 1 : rows, :] - total) * masks[:, 3:4] * step
    msg[0:inner, :] = mm3(silu(conv_x) * expand(to_end, emap), b_mat, TN)
    msg[inner:, :] = jnp.broadcast_to(
        jnp.exp(total_t[:, rows - 1 : rows]) * masks[rows - 1 : rows, 4:5], (heads, width)
    )


def head_kernel(cum, cumt, allowed, head):
    gap = cum[:, head : head + 1] - cumt[head : head + 1, :]
    return jnp.exp(jnp.where(allowed, gap, -1e30))


def k_intra(layer, ux, ubc, dts, cum, cumt, segc, segr, dskip, yp):
    rows, inner = ux.shape
    heads = dts.shape[1]
    width = ubc.shape[1] // 2
    per = inner // heads
    emap = head_map(heads, inner)
    x_conv = silu(ux[...])
    bc = silu(ubc[...])
    gram = mm3(bc[:, width:], bc[:, :width], NT)
    allowed = jnp.logical_and(segc[...] == segr[...], lower(rows))
    scaled = x_conv * expand(dts[...], emap)
    skip = x_conv * expand(jnp.broadcast_to(dskip[layer : layer + 1, :], (8, heads)), emap)[0:1, :]
    total, total_t = cum[...], cumt[...]
    group = max(1, 128 // per)
    for first in range(0, heads, group):
        cols = slice(first * per, (first + group) * per)
        sh, sl = split2(scaled[:, cols])
        lane = lax.broadcasted_iota(jnp.int32, (rows, group * per), 1)
        result = skip[:, cols]
        for head in range(first, first + group):
            gh, gl = split2(gram * head_kernel(total, total_t, allowed, head))
            part = mm(gh, sh, NN) + (mm(gh, sl, NN) + mm(gl, sh, NN))
            result = result + jnp.where(lane // per == head - first, part, 0.0)
        yp[:, cols] = result


def k_gate(flag, yp, ubc, cum, aux, z, near, far, mixed, gated, ss, inc):
    inner = yp.shape[1]
    heads = cum.shape[1]
    merge(heads, flag, near, far, inc)
    width = ubc.shape[1] // 2
    emap = head_map(heads, inner)
    c_mat = silu(ubc[:, width:])
    into = jnp.exp(cum[...]) * aux[:, 4:5]
    mix = yp[...] + mm3(c_mat, inc[...], NT) * expand(into, emap)
    mixed[...] = mix
    gate = mix * silu(z[...])
    gated[...] = gate
    ss[...] = row_sums(gate * gate)


def to_relative(place, source, target):
    pieces = place.shape[0]
    size = source.shape[0] // pieces
    for piece in range(pieces):
        target[piece * size : (piece + 1) * size, :] = source[rows_at(place, piece, size), :]


def k_out(layer, total, place, gated, ss, gain, wout, gn, keep, send, moved):
    scale = to_column(lax.rsqrt(ss[...] * (1.0 / total) + eps))
    normed = (gated[...] * scale * gain[layer : layer + 1, :]).astype(BF)
    gn[...] = normed
    to_relative(place, gn, moved)
    half = keep.shape[0]
    part = mm(moved[...], wout[...], NN)
    keep[...] = part[:half, :]
    send[...] = part[half:, :]


def k_b1_top(layer, total, cot, wout, gated, ss, gain, cb, dgn, cross, ggain):
    cb[...] = cot[...].astype(BF)
    back_out(layer, total, wout, gated, ss, gain, cb, dgn, cross, ggain)


def k_b1(layer, total, place, *refs):
    pieces, (wout, gated, ss, gain, cb, dgn, cross, ggain) = refs[:-8], refs[-8:]
    k_place(place, *pieces, cb)
    back_out(layer, total, wout, gated, ss, gain, cb, dgn, cross, ggain)


def back_out(layer, total, wout, gated, ss, gain, cb, dgn, cross, ggain):
    grad = mm(cb[...], wout[...], NT)
    dgn[...] = grad
    scale = to_column(lax.rsqrt(ss[...] * (1.0 / total) + eps))
    both = grad * gated[...]
    cross[...] = row_sums(both * gain[layer : layer + 1, :])
    ggain[...] = jnp.sum(both * scale, axis=0, keepdims=True)


def k_b2(layer, total, dgn, gated, mixed, z, ss, cross, gain, ubc, cum, cumt, aux, dm, dz, msg):
    rows, inner = dgn.shape
    heads = cum.shape[1]
    width = ubc.shape[1] // 2
    emap = head_map(heads, inner)
    scale_row = lax.rsqrt(ss[...] * (1.0 / total) + eps)
    scale = to_column(scale_row)
    pull = to_column(scale_row * scale_row * scale_row * cross[...] * (1.0 / total))
    d_gated = scale * gain[layer : layer + 1, :] * dgn[...] - gated[...] * pull
    zv = z[...]
    grad = d_gated * silu(zv)
    dm[...] = grad
    dz[...] = (d_gated * mixed[...] * silu_slope(zv)).astype(BF)
    masks = aux[...]
    into = jnp.exp(cum[...]) * masks[:, 4:5]
    msg[0:inner, :] = mm3(grad * expand(into, emap), silu(ubc[:, width:]), TN)
    msg[inner:, :] = jnp.broadcast_to(
        jnp.exp(cumt[:, rows - 1 : rows]) * masks[rows - 1 : rows, 4:5], (heads, width)
    )


def k_b3(layer, dm, ux, ubc, dts, cum, cumt, segc, segr, mixed, inc, aux, dskip,
         dx, dbc, dcum, ddt, gskip):
    rows, inner = ux.shape
    heads = dts.shape[1]
    width = ubc.shape[1] // 2
    per = inner // heads
    emap = head_map(heads, inner)
    x_conv = silu(ux[...])
    bc = silu(ubc[...])
    b_mat, c_mat = bc[:, :width], bc[:, width:]
    gram = mm3(c_mat, b_mat, NT)
    allowed = jnp.logical_and(segc[...] == segr[...], lower(rows))
    step = dts[...]
    step_e = expand(step, emap)
    scaled = x_conv * step_e
    grad = dm[...]
    total, total_t = cum[...], cumt[...]
    skip_row = dskip[layer : layer + 1, :]
    skip_e = expand(jnp.broadcast_to(skip_row, (8, heads)), emap)[0:1, :]
    d_gram = jnp.zeros((rows, rows), F32)
    group = max(1, 128 // per)
    plain = []
    for first in range(0, heads, group):
        cols = slice(first * per, (first + group) * per)
        sh, sl = split2(scaled[:, cols])
        lane = lax.broadcasted_iota(jnp.int32, (rows, group * per), 1)
        g_cols = grad[:, cols]
        ch, cl = split2(g_cols)
        result = jnp.zeros((rows, group * per), F32)
        for head in range(first, first + group):
            mine = lane // per == head - first
            fall = head_kernel(total, total_t, allowed, head)
            gh, gl = split2(gram * fall)
            part = mm(gh, ch, TN) + (mm(gh, cl, TN) + mm(gl, ch, TN))
            result = result + jnp.where(mine, part, 0.0)
            mh = jnp.where(mine, ch, jnp.zeros_like(ch))
            ml = jnp.where(mine, cl, jnp.zeros_like(cl))
            outer = mm(mh, sh, NT) + (mm(mh, sl, NT) + mm(ml, sh, NT))
            d_gram = d_gram + outer * fall
        plain.append(result)
    plain = jnp.concatenate(plain, axis=1)
    dx[...] = plain * step_e + grad * skip_e
    into = jnp.exp(total) * aux[:, 4:5]
    dbc[:, :width] = mm3(d_gram, c_mat, TN)
    dbc[:, width:] = mm3(d_gram, b_mat, NN) + mm3(grad * expand(into, emap), inc[...], NN)
    by_col = per_head(x_conv * plain, emap)
    skip_dot = per_head(grad * x_conv, emap)
    ddt[...] = by_col
    dcum[...] = per_head(grad * mixed[...], emap) - skip_row * skip_dot - step * by_col
    gskip[...] = jnp.sum(skip_dot, axis=0, keepdims=True)


def k_b4(layer, flag, ux, ubc, dts, dtp, cum, aux, dx, dbc, dcum, ddt, near, far, inc, dtb, alog,
         du, dbo, dd, gdtb, galog, edge, df):
    rows, inner = ux.shape
    heads = dts.shape[1]
    width = ubc.shape[1] // 2
    merge(heads, flag, near, far, df)
    emap = head_map(heads, inner)
    conv = ux[...]
    x_conv = silu(conv)
    b_mat = silu(ubc[:, :width])
    total, step, masks = cum[...], dts[...], aux[...]
    fin = df[...]
    spread = mm3(b_mat, fin, NT)
    bare = jnp.exp(total[rows - 1 : rows, :] - total) * masks[:, 3:4]
    to_end = bare * step
    to_end_e = expand(to_end, emap)
    dot = per_head(x_conv * spread, emap)
    du[...] = (dx[...] + to_end_e * spread) * silu_slope(conv)
    slope = silu_slope(ubc[...])
    dbo[:, :width] = (dbc[:, :width] + mm3(x_conv * to_end_e, fin, NN)) * slope[:, :width]
    dbo[:, width:] = dbc[:, width:] * slope[:, width:]
    edge[:, :inner] = du[0:HALO, :]
    edge[:, inner:] = dbo[0:HALO, :]
    used = to_end * dot
    d_cum = dcum[...] - used
    through = per_head(row_sums(fin * inc[...]) + jnp.zeros((8, inner), F32), emap)[0:1, :]
    last = jnp.sum(used, axis=0, keepdims=True) + through * (
        jnp.exp(total[rows - 1 : rows, :]) * masks[rows - 1 : rows, 4:5]
    )
    tri = jnp.where(lower(rows), 1.0, 0.0).astype(BF)
    d_decay = sel_left(tri, d_cum, TN) + last
    rate = jnp.exp(alog[layer : layer + 1, :])
    galog[...] = jnp.sum(-step * rate * d_decay, axis=0, keepdims=True)
    d_raw = (ddt[...] + bare * dot - rate * d_decay) * sigmoid(dtp[...] + dtb[layer : layer + 1, :])
    gdtb[...] = jnp.sum(d_raw, axis=0, keepdims=True)
    dd[...] = d_raw.astype(BF)


def k_conv_back(du, halo, proj, edge, aux, weights, grad, gw, gb, ext_d, ext_p):
    rows = du.shape[0]
    ext_d[0:rows, :] = du[...]
    ext_d[rows:, :] = halo[...]
    conv_back(proj, edge, aux, weights, grad, gw, gb, ext_d, ext_p)


def k_conv_back_b(which, du, proj, edge, aux, weights, grad, gw, gb, part, ext_d, ext_p):
    quarter = du.shape[1]
    for slot in range(ext_d.shape[1] // quarter):
        cols = slice(slot * quarter, (slot + 1) * quarter)
        ext_d[:, cols] = jnp.where(which[0] == slot, du[...], 0.0)
    wide = conv_back(proj, edge, aux, weights, grad, gw, gb, ext_d, ext_p)
    part[...] = sum(
        wide[:, slot * quarter : (slot + 1) * quarter] for slot in range(ext_d.shape[1] // quarter)
    ).astype(BF)


def conv_back(proj, edge, aux, weights, grad, gw, gb, ext_d, ext_p):
    rows = proj.shape[0]
    taps = weights.shape[0]
    ext_p[0:HALO, :] = edge[...]
    ext_p[HALO:, :] = proj[...]
    masks = aux[...]
    value = ext_d[0:rows, :]
    total = jnp.zeros_like(value)
    for tap in range(taps):
        back = ext_d[pl.ds(taps - 1 - tap, rows), :] * weights[tap : tap + 1, :]
        seen = ext_p[pl.ds(HALO - taps + 1 + tap, rows), :] * value
        if tap < taps - 1:
            back = back * masks[:, 5 + tap : 6 + tap]
            seen = seen * masks[:, tap : tap + 1]
        total = total + back
        gw[tap : tap + 1, :] = jnp.sum(seen, axis=0, keepdims=True)
    gb[...] = jnp.sum(value, axis=0, keepdims=True)
    grad[...] = total.astype(BF)
    return total


def k_dnorm(place, dz, dxb, dd, dbq, wz, wx, wdt, wbq, keep, send, own, moved):
    own[...] = (
        mm(dz[...], wz[...], NT)
        + mm(dxb[...], wx[...], NT)
        + mm(dd[...], wdt[...], NT)
        + mm(dbq[...], wbq[...], NT)
    )
    to_relative(place, own, moved)
    half = keep.shape[0]
    keep[...] = moved[0:half, :]
    send[...] = moved[half:, :]


def k_norm_back(resid, keep, got, gain, cot, out, g_gain):
    grad = keep[...] + got[...]
    value = resid[...]
    inv = lax.rsqrt(jnp.mean(value * value, axis=1, keepdims=True) + eps)
    unit = value * inv
    g_gain[...] = jnp.sum(grad * unit, axis=0, keepdims=True)
    scaled = grad * gain[...]
    mean = jnp.mean(scaled * unit, axis=1, keepdims=True)
    out[...] = cot[...] + inv * (scaled - unit * mean)


def k_dw(place, left, *refs):
    rights, (keep, send, moved, full) = refs[:-4], refs[-4:]
    pieces = place.shape[0]
    size = left.shape[1] // pieces
    half = keep.shape[0]
    aligned = size % 128 == 0
    if aligned:
        for piece in range(pieces):
            moved[:, piece * size : (piece + 1) * size] = left[:, rows_at(place, piece, size)]
    start = 0
    for right in rights:
        cols = slice(start, start + right.shape[1])
        start += right.shape[1]
        if aligned:
            keep[:, cols] = mm(moved[:, :half], right[...], TN)
            send[:, cols] = mm(moved[:, half:], right[...], TN)
        else:
            full[:, cols] = mm(left[...], right[...], TN)
    if not aligned:
        for piece in range(pieces):
            target, row = (keep, piece) if piece < pieces // 2 else (send, piece - pieces // 2)
            target[row * size : (row + 1) * size, :] = full[rows_at(place, piece, size), :]


def local(hidden_in, seg_ids, norm_gain, w_z, w_x, w_bc, w_dt, conv_x_w, conv_x_b, conv_bc_w,
          conv_bc_b, dt_bias, a_log, d_skip, gate_gain, w_out, out_cot):
    rows, model = hidden_in.shape
    layers = w_z.shape[0]
    heads = w_dt.shape[2]
    inner = w_z.shape[2]
    state2 = w_bc.shape[2]
    width = state2 // 2
    taps = conv_x_w.shape[1]
    inner_total = inner * lax.axis_size("head")
    seq_bits = bits_of("seq")
    spare = list(range(3, seq_bits))
    orders = [
        [bit for bit in base if bit < seq_bits] + spare
        for base in ([0, 1, 2], [1, 0, 2])
    ]
    share = model // lax.axis_size("seq")
    head_bits = bits_of("head")
    size = rows // lax.axis_size("head")
    place = jnp.stack(
        [
            reverse_bits(lax.axis_index("head") ^ mask, head_bits) * size
            for mask in relative_order(head_bits)
        ]
    ).astype(jnp.int32)

    padded = jnp.concatenate(
        [jnp.full((taps - 1,), -1, jnp.int32), seg_ids, jnp.full((taps - 1,), -1, jnp.int32)]
    )
    around = lax.dynamic_slice_in_dim(
        padded, lax.axis_index("seq") * rows, rows + 2 * (taps - 1)
    )
    own = around[taps - 1 : taps - 1 + rows]
    seg_before = around[taps - 2]
    columns = [around[k : k + rows] == own for k in range(taps - 1)]
    columns += [own == own[rows - 1], own == seg_before]
    columns += [around[2 * (taps - 1) - k : 2 * (taps - 1) - k + rows] == own for k in range(taps - 1)]
    aux = jnp.stack(columns, axis=1).astype(F32)
    segc, segr = own[:, None], own[None, :]

    own_quarter = reverse_bits(lax.axis_index("head"), head_bits).reshape(1).astype(jnp.int32)
    half_rows = ((rows // 2, model), F32)
    quarter_rows = ((size, model), F32)
    proj_outs = [((rows, inner), F32), ((rows, inner), F32), ((rows, state2), F32),
                 ((rows, heads), F32), ((rows, model), BF)]
    message = ((inner + heads, width), F32)

    resid = own_piece(hidden_in, "head", 0).astype(F32)
    normed = None
    saved = []
    for l in range(layers):
        weights = (Far(w_z, l), Far(w_x, l), Far(w_bc, l), Far(w_dt, l))
        if l == 0:
            z, x, bc, dtp, nb = run(
                k_proj_first, proj_outs, hidden_in, norm_gain[l : l + 1], *weights, name="proj"
            )
        else:
            z, x, bc, dtp, nb = run(
                k_proj, proj_outs, *gather_pieces(normed, "head"), *weights, small=[place],
                name="proj",
            )
        edge = rotate(jnp.concatenate([x[rows - HALO :], bc[rows - HALO :]], 1), "seq", 1)
        ux, ubc, dts, cum, cumt, msg = run(
            functools.partial(k_front, l),
            [((rows, inner), F32), ((rows, state2), F32), ((rows, heads), F32),
             ((rows, heads), F32), ((heads, rows), F32), message],
            x, bc, dtp, edge, aux, conv_x_w[l], conv_x_b, conv_bc_w[l], conv_bc_b, dt_bias, a_log,
            scratch=(pltpu.VMEM((rows + HALO, inner), F32), pltpu.VMEM((rows + HALO, state2), F32)),
            name="front",
        )
        near, far, flag = carried(msg, heads, False)
        (yp,) = run(
            functools.partial(k_intra, l), [((rows, inner), F32)],
            ux, ubc, dts, cum, cumt, segc, segr, d_skip, name="intra",
        )
        mixed, gated, ss, inc = run(
            k_gate,
            [((rows, inner), F32), ((rows, inner), F32), ((1, rows), F32), ((inner, width), F32)],
            yp, ubc, cum, aux, z, near, far, small=[flag], name="gate",
        )
        ss = lax.psum(ss, "head")
        gn, keep, send = run(
            functools.partial(k_out, l, inner_total),
            [((rows, inner), BF), half_rows, half_rows],
            gated, ss, gate_gain, Far(w_out, l), small=[place],
            scratch=(pltpu.VMEM((rows, inner), BF),), name="out",
        )
        keep, got = finish_scatter(keep, send, "head")
        saved.append((resid, z, x, bc, dtp, nb, edge, ux, ubc, dts, cum, cumt, inc, mixed, gated,
                      ss, gn))
        last = l + 1 == layers
        resid, normed = run(
            k_join, [quarter_rows, quarter_rows], resid, keep, got,
            norm_gain[0 if last else l + 1][None, :], flops=1000000, name="join",
        )
    (hidden_out,) = run(
        k_place, [((rows, model), BF)], *gather_pieces(resid, "head"), small=[place],
        flops=1000000, name="round",
    )

    def dw_scratch(cols):
        aligned = share % 128 == 0
        return (
            pltpu.VMEM((rows, model if aligned else 128), BF),
            pltpu.VMEM((8 if aligned else model, cols), F32),
        )

    cot = own_piece(out_cot, "head", 0)
    final = [[None] * layers for _ in range(4)]

    def product(order, left, rights, after, name="dw"):
        cols = sum(right.shape[1] for right in rights)
        keep, send = run(
            k_dw, [((model // 2, cols), F32)] * 2, left, *rights, small=[seq_places(order, share)],
            after=after, scratch=dw_scratch(cols), name=name,
        )
        return SeqScatter(order, keep, send)

    narrow_in = [None] * layers
    small = [None] * layers
    gains = [None] * layers
    waiting = []
    for l in reversed(range(layers)):
        (resid, z, x, bc, dtp, nb, edge, ux, ubc, dts, cum, cumt, inc, mixed, gated, ss,
         gn) = saved[l]
        b1_outs = [((rows, model), BF), ((rows, inner), F32), ((1, rows), F32), ((1, inner), F32)]
        if l + 1 == layers:
            cb, dgn, cross, ggain = run(
                functools.partial(k_b1_top, l, inner_total), b1_outs,
                out_cot, Far(w_out, l), Far(gated), ss, gate_gain, name="b1",
            )
        else:
            cb, dgn, cross, ggain = run(
                functools.partial(k_b1, l, inner_total), b1_outs,
                *gather_pieces(cot, "head"), Far(w_out, l), Far(gated), ss, gate_gain,
                small=[place], name="b1",
            )
        cross = lax.psum(cross, "head")
        dm, dz, msg = run(
            functools.partial(k_b2, l, inner_total),
            [((rows, inner), F32), ((rows, inner), BF), message],
            dgn, Far(gated), Far(mixed), Far(z), ss, cross, gate_gain, Far(ubc), Far(cum), Far(cumt), aux,
            name="b2",
        )
        if waiting:
            waiting[0].advance([dm])
        near, far, flag = carried(msg, heads, True)
        dx, dbc, dcum, ddt, gskip = run(
            functools.partial(k_b3, l),
            [((rows, inner), F32), ((rows, state2), F32), ((rows, heads), F32),
             ((rows, heads), F32), ((1, heads), F32)],
            dm, Far(ux), Far(ubc), Far(dts), Far(cum), Far(cumt), segc, segr, Far(mixed), Far(inc), aux,
            d_skip, name="b3",
        )
        du, dub, dd, gdtb, galog, first_rows = run(
            functools.partial(k_b4, l),
            [((rows, inner), F32), ((rows, state2), F32), ((rows, heads), BF),
             ((1, heads), F32), ((1, heads), F32), ((HALO, inner + state2), F32)],
            Far(ux), Far(ubc), Far(dts), Far(dtp), Far(cum), aux, dx, dbc, dcum, ddt, near, far,
            Far(inc), dt_bias, a_log,
            small=[flag], scratch=(pltpu.VMEM((inner, width), F32),), name="b4",
        )
        halo = rotate(first_rows, "seq", -1)
        for pending in waiting:
            pending.advance([halo])
        fresh = [
            product(orders[0], cb, [Far(gn)], [halo]),
            product(orders[1], Far(nb), [dz], [halo]),
        ]
        dub = scatter_cols(jnp.concatenate([dub, halo[:, inner:]], 0), "head")
        quarter = dub.shape[1]
        dxb, gcw, gcb = run(
            k_conv_back,
            [((rows, inner), BF), ((taps, inner), F32), ((1, inner), F32)],
            du, halo[:, :inner], Far(x), edge[:, :inner], aux, conv_x_w[l],
            scratch=(pltpu.VMEM((rows + HALO, inner), F32), pltpu.VMEM((rows + HALO, inner), F32)),
            name="convx",
        )
        dbw, gbw, gbb, dbb = run(
            k_conv_back_b,
            [((rows, state2), BF), ((taps, state2), F32), ((1, state2), F32), ((rows, quarter), BF)],
            dub, Far(bc), edge[:, inner:], aux, conv_bc_w[l], small=[own_quarter],
            scratch=(pltpu.VMEM((rows + HALO, state2), F32),
                     pltpu.VMEM((rows + HALO, state2), F32)),
            name="convb",
        )
        keep, send = run(
            k_dnorm, [half_rows, half_rows],
            dz, dxb, dd, dbw, Far(w_z, l), Far(w_x, l), Far(w_dt, l), Far(w_bc, l), small=[place],
            scratch=(pltpu.VMEM((rows, model), F32), pltpu.VMEM((rows, model), F32)), name="dnorm",
        )
        keep, got = finish_scatter(keep, send, "head")
        fresh += [
            product(orders[0], Far(nb), [dxb[:, : inner // 2]], []),
            product(orders[1], Far(nb), [dxb[:, inner // 2 :]], []),
        ]
        cot, gains[l] = run(
            k_norm_back, [quarter_rows, ((1, model), F32)],
            resid, keep, got, norm_gain[l : l + 1], cot, flops=1000000, name="normback",
        )
        for pending in fresh[:2] + waiting[1:]:
            pending.advance([cot])
        for slot in range(len(waiting)):
            final[slot][l + 1] = waiting[slot].result()
        waiting = fresh
        narrow_in[l] = (Far(nb), dbb, dd)
        small[l] = (gcw, gcb, gbw, gbb, gdtb, galog, gskip, ggain)
    for slot in range(len(waiting)):
        final[slot][0] = waiting[slot].result()
    (grad_in,) = run(
        k_place, [((rows, model), F32)], *gather_pieces(cot, "head"), small=[place],
        flops=1000000, name="place",
    )

    narrow = jnp.stack(
        [product(orders[1], n[0], n[1:], [], "dwn").result() for n in narrow_in]
    )

    def reduced(flat, order):
        sizes = [part.size for part in flat]
        pack = jnp.concatenate([part.reshape(-1) for part in flat])
        pack = jnp.pad(pack, (0, -pack.size % 1024)).reshape(-1, 128)
        pack = seq_sum(pack, order).reshape(-1)
        pieces, start = [], 0
        for count in sizes:
            pieces.append(pack[start : start + count])
            start += count
        return pieces

    pieces = reduced([part for l in range(layers) for part in small[l]], orders[0])
    count = len(small[0])

    def both(slot):
        return jnp.stack([pieces[l * count + slot].reshape(small[l][slot].shape) for l in range(layers)])

    wide = jnp.concatenate(
        [seq_sum(jnp.concatenate(gains, 0), orders[0]).reshape(-1), both(2).reshape(-1),
         both(3).reshape(-1)]
    )
    wide = head_sum(wide.reshape(-1, 128)).reshape(-1)
    stop = layers * model
    grad_gain = wide[:stop].reshape(layers, model)
    grad_gain = lax.dynamic_slice_in_dim(grad_gain, lax.axis_index("seq") * share, share, 1)
    bc_w = wide[stop : stop + layers * taps * state2].reshape(layers, taps, state2)
    bc_b = wide[stop + layers * taps * state2 :].reshape(layers, state2)
    bc_parts = gather_back(narrow[:, :, :quarter], "head", 2)
    return (
        hidden_out,
        grad_in,
        grad_gain,
        jnp.stack(final[1]),
        jnp.stack([jnp.concatenate(pair, 1) for pair in zip(final[2], final[3])]),
        bc_parts,
        narrow[:, :, quarter:],
        both(0),
        both(1)[:, 0],
        bc_w,
        bc_b,
        both(4)[:, 0],
        both(5)[:, 0],
        both(6)[:, 0],
        both(7)[:, 0],
        jnp.stack([part.T for part in final[0]]),
    )


def solution(mesh):
    return jax.shard_map(
        local,
        mesh=mesh,
        in_specs=(
            P("seq", None),
            P(),
            P(),
            P(None, None, "head"),
            P(None, None, "head"),
            P(),
            P(None, None, "head"),
            P(None, None, "head"),
            P(None, "head"),
            P(),
            P(),
            P(None, "head"),
            P(None, "head"),
            P(None, "head"),
            P(None, "head"),
            P(None, "head", None),
            P("seq", None),
        ),
        out_specs=(
            P("seq", None),
            P("seq", None),
            P(None, "seq"),
            P(None, "seq", "head"),
            P(None, "seq", "head"),
            P(None, "seq", None),
            P(None, "seq", "head"),
            P(None, None, "head"),
            P(None, "head"),
            P(),
            P(),
            P(None, "head"),
            P(None, "head"),
            P(None, "head"),
            P(None, "head"),
            P(None, "head", "seq"),
        ),
        check_vma=False,
    )
```

```python
import functools

import jax
import jax.numpy as jnp
from jax import lax
from jax.experimental import pallas as pl
from jax.experimental.pallas import tpu as pltpu
from jax.sharding import PartitionSpec as P

eps = 1e-05
F32, BF = jnp.float32, jnp.bfloat16
NN, NT, TN = ((1,), (0,)), ((1,), (1,)), ((0,), (0,))
HALO = 8
GRANT = 16 << 20


def swap(value, axis, mask):
    count = lax.axis_size(axis)
    return lax.ppermute(value, axis, [(i, i ^ mask) for i in range(count)])


def rotate(value, axis, steps):
    count = lax.axis_size(axis)
    return lax.ppermute(value, axis, [(i, (i + steps) % count) for i in range(count)])


def bit_of(axis, bit):
    return (lax.axis_index(axis) >> bit) & 1


def bits_of(axis):
    return lax.axis_size(axis).bit_length() - 1


def reverse_bits(value, count):
    result = 0
    for bit in range(count):
        result = result | (((value >> bit) & 1) << (count - 1 - bit))
    return result


def relative_order(count):
    return [reverse_bits(i, count) for i in range(1 << count)]


def finish_scatter(keep, send, axis):
    for bit in range(bits_of(axis)):
        got = swap(send, axis, 1 << bit)
        half = keep.shape[0] // 2
        if bit + 1 < bits_of(axis):
            send = keep[half:] + got[half:]
            keep = keep[:half] + got[:half]
    return keep, got


def scatter_cols(value, axis):
    for bit in range(bits_of(axis)):
        half = value.shape[1] // 2
        which = bit_of(axis, bit)
        keep = lax.dynamic_slice_in_dim(value, which * half, half, 1)
        send = lax.dynamic_slice_in_dim(value, (1 - which) * half, half, 1)
        value = keep + swap(send, axis, 1 << bit)
    return value


def gather_pieces(mine, axis):
    pieces = [mine]
    for bit in reversed(range(bits_of(axis))):
        pieces = pieces + [swap(piece, axis, 1 << bit) for piece in pieces]
    return pieces


def gather_back(value, axis, dim):
    for bit in reversed(range(bits_of(axis))):
        other = swap(value, axis, 1 << bit)
        first = bit_of(axis, bit) == 0
        value = jnp.where(
            first,
            jnp.concatenate([value, other], dim),
            jnp.concatenate([other, value], dim),
        )
    return value


def own_piece(value, axis, dim):
    for bit in range(bits_of(axis)):
        half = value.shape[dim] // 2
        value = lax.dynamic_slice_in_dim(value, bit_of(axis, bit) * half, half, dim)
    return value


def mask_of(bit):
    return 1 << bit


def seq_places(order, share):
    count = len(order)
    me = lax.axis_index("seq")
    starts = []
    for piece in range(1 << count):
        mask = 0
        for step, bit in enumerate(order):
            if (piece >> (count - 1 - step)) & 1:
                mask ^= mask_of(bit)
        starts.append((me ^ mask) * share)
    return jnp.stack(starts).astype(jnp.int32)


class SeqScatter:
    def __init__(self, order, keep, send):
        self.order, self.keep, self.step = order, keep, 0
        self.got = swap(send, "seq", mask_of(order[0]))

    def advance(self, after=()):
        self.step += 1
        if self.step == len(self.order):
            self.keep = self.keep + self.got
        elif self.step < len(self.order):
            rows, cols = self.keep.shape
            half = ((rows // 2, cols), F32)
            self.keep, send = run(
                k_add, [half, half], self.keep, self.got, after=after, flops=rows * cols, name="add"
            )
            self.got = swap(send, "seq", mask_of(self.order[self.step]))

    def result(self, after=()):
        while self.step < len(self.order):
            self.advance(after)
        return self.keep


def seq_sum(value, order):
    for bit in order:
        value = value + swap(value, "seq", mask_of(bit))
    return value


def head_sum(value):
    for bit in range(bits_of("head")):
        value = value + swap(value, "head", 1 << bit)
    return value


def carried(message, heads, reverse):
    count = bits_of("seq")
    shape = [(message.shape, F32)]
    flags = [
        ((1 - bit_of("seq", bit)) if reverse else bit_of("seq", bit)).reshape(1).astype(jnp.int32)
        for bit in range(count)
    ]
    ahead, stages = None, []
    for bit in range(count - 1):
        got = swap(message, "seq", mask_of(bit))
        if ahead is None:
            ahead, message = run(
                functools.partial(k_scan_first, heads), shape * 2, message, got, small=[flags[bit]],
                flops=1000000, name="scan",
            )
        else:
            ahead, message = run(
                functools.partial(k_scan, heads), shape * 2, message, ahead, got,
                small=[flags[bit]], flops=1000000, name="scan",
            )
        stages.append(ahead)
    return ahead, swap(message, "seq", mask_of(count - 1)), flags[count - 1], stages


def mm(left, right, dims):
    return lax.dot_general(left, right, (dims, ((), ())), preferred_element_type=F32)


def split2(value):
    high = value.astype(BF)
    return high, (value - high.astype(F32)).astype(BF)


def mm3(left, right, dims):
    lh, ll = split2(left)
    rh, rl = split2(right)
    return mm(lh, rh, dims) + (mm(lh, rl, dims) + mm(ll, rh, dims))


def split3(value):
    high = value.astype(BF)
    rest = value - high.astype(F32)
    mid = rest.astype(BF)
    return high, mid, (rest - mid.astype(F32)).astype(BF)


def sel_right(value, sel, dims):
    return sum(mm(part, sel, dims) for part in split3(value))


def sel_left(sel, value, dims):
    return sum(mm(sel, part, dims) for part in split3(value))


def head_map(heads, inner):
    chan = lax.broadcasted_iota(jnp.int32, (inner, heads), 0)
    head = lax.broadcasted_iota(jnp.int32, (inner, heads), 1)
    return jnp.where(chan // (inner // heads) == head, 1.0, 0.0).astype(BF)


def expand(value, emap):
    return sel_right(value, emap, NT)


def per_head(value, emap):
    return sel_right(value, emap, NN)


def lower(rows):
    row = lax.broadcasted_iota(jnp.int32, (rows, rows), 0)
    col = lax.broadcasted_iota(jnp.int32, (rows, rows), 1)
    return row >= col


def to_column(row_value):
    rows = row_value.shape[1]
    row = lax.broadcasted_iota(jnp.int32, (rows, rows), 0)
    col = lax.broadcasted_iota(jnp.int32, (rows, rows), 1)
    return jnp.sum(jnp.where(row == col, row_value, 0.0), axis=1, keepdims=True)


def row_sums(value):
    ones = jnp.ones((8, value.shape[1]), BF)
    return sel_left(ones, value, NT)[0:1, :]


def sigmoid(value):
    return 1.0 / (1.0 + jnp.exp(-value))


def silu(value):
    return value * sigmoid(value)


def silu_slope(value):
    sig = sigmoid(value)
    return sig * (1.0 + value * (1.0 - sig))


class Far:
    def __init__(self, value, layer):
        self.value, self.layer = value, layer
        self.shape = value.shape[1:]


def run(body, outs, *args, small=(), after=(), scratch=(), flops=2_000_000_000, name=None):
    held = pl.BlockSpec(memory_space=pltpu.VMEM)
    first, second = len(small), len(small) + len(args)
    values = [arg.value if isinstance(arg, Far) else arg for arg in args]
    moved = sum(a.size * a.dtype.itemsize for a in values)

    def inner(*refs):
        given = list(refs[:second])
        for i, arg in enumerate(args):
            if isinstance(arg, Far):
                given[first + i] = given[first + i].at[arg.layer]
        body(*given, *refs[second + len(after) :])

    return pl.pallas_call(
        inner,
        in_specs=[pl.BlockSpec(memory_space=pltpu.SMEM)] * first
        + [held] * len(args)
        + [pl.BlockSpec(memory_space=pl.ANY)] * len(after),
        out_specs=[held] * len(outs),
        out_shape=[jax.ShapeDtypeStruct(shape, kind) for shape, kind in outs],
        scratch_shapes=list(scratch),
        compiler_params=pltpu.CompilerParams(vmem_limit_bytes=GRANT),
        cost_estimate=pl.CostEstimate(flops=flops, bytes_accessed=moved, transcendentals=0),
        name=name,
    )(*small, *values, *after)


def rows_at(place, piece, size):
    return pl.ds(pl.multiple_of(place[piece], size), size)


def norm_rows(value, gain):
    return value * lax.rsqrt(jnp.mean(value * value, axis=1, keepdims=True) + eps) * gain


def k_add(keep, got, first, second):
    half = first.shape[0]
    first[...] = keep[0:half, :] + got[0:half, :]
    second[...] = keep[half:, :] + got[half:, :]


def merge(heads, flag, near, far, state, decay=None):
    rows = near.shape[0] - heads
    per = rows // heads
    use = flag[0] == 1
    for head in range(heads):
        cols = slice(head * per, (head + 1) * per)
        fade = near[rows + head : rows + head + 1, :]
        state[cols, :] = jnp.where(use, fade * far[cols, :] + near[cols, :], near[cols, :])
    if decay is not None:
        fades = near[rows:, :]
        decay[...] = jnp.where(use, fades * far[rows:, :], fades)


def k_scan_first(heads, flag, mine, got, ahead, total):
    rows = mine.shape[0] - heads
    use = flag[0] == 1
    ahead[0:rows, :] = jnp.where(use, got[0:rows, :], 0.0)
    ahead[rows:, :] = jnp.where(use, got[rows:, :], 1.0)
    join(heads, use, mine, got, total)


def join(heads, use, mine, got, total):
    rows = mine.shape[0] - heads
    per = rows // heads
    for head in range(heads):
        cols = slice(head * per, (head + 1) * per)
        own, other = mine[cols, :], got[cols, :]
        own_fade = mine[rows + head : rows + head + 1, :]
        got_fade = got[rows + head : rows + head + 1, :]
        total[cols, :] = jnp.where(use, own_fade * other + own, got_fade * own + other)
    total[rows:, :] = mine[rows:, :] * got[rows:, :]


def k_scan(heads, flag, mine, ahead, got, ahead_out, total):
    rows = mine.shape[0] - heads
    merge(heads, flag, ahead, got, ahead_out, ahead_out.at[pl.ds(rows, heads), :])
    join(heads, flag[0] == 1, mine, got, total)


def k_join(resid, keep, got, gain, total, normed):
    value = resid[...] + (keep[...] + got[...])
    total[...] = value
    normed[...] = norm_rows(value, gain[...])


def k_place(place, *refs):
    out = refs[-1]
    size = refs[0].shape[0]
    for piece, ref in enumerate(refs[:-1]):
        out[rows_at(place, piece, size), :] = ref[:, : out.shape[1]].astype(out.dtype)


def project(rounded, wz, wx, wbc, wdt, z, x, bc, dt):
    x[...] = mm(rounded, wx[...], NN)
    bc[...] = mm(rounded, wbc[...], NN)
    dt[...] = mm(rounded, wdt[...], NN)
    z[...] = mm(rounded, wz[...], NN)


def k_proj_first(hidden, gain, wz, wx, wbc, wdt, z, x, bc, dt, nb):
    rounded = norm_rows(hidden[...].astype(F32), gain[...]).astype(BF)
    nb[...] = rounded
    project(rounded, wz, wx, wbc, wdt, z, x, bc, dt)


def k_proj(place, *refs):
    pieces, (wz, wx, wbc, wdt, z, x, bc, dt, nb) = refs[:-9], refs[-9:]
    k_place(place, *pieces, nb)
    project(nb[...], wz, wx, wbc, wdt, z, x, bc, dt)


def conv_rows(ext, halo_rows, rows, weights, bias, aux):
    total = jnp.broadcast_to(bias, (rows, weights.shape[1]))
    taps = weights.shape[0]
    for tap in range(taps):
        part = ext[pl.ds(halo_rows - taps + 1 + tap, rows), :] * weights[tap : tap + 1, :]
        total = total + (part * aux[:, tap : tap + 1] if tap < taps - 1 else part)
    return total


def k_front(layer, x, bc, dt, edge, aux, cxw, cxb, cbw, cbb, dtb, alog,
            ux, ubc, dts, cum, cumt, msg, ext_x, ext_b):
    rows, inner = x.shape
    heads = dt.shape[1]
    width = bc.shape[1] // 2
    ext_x[0:HALO, :] = edge[:, :inner]
    ext_x[HALO:, :] = x[...]
    ext_b[0:HALO, :] = edge[:, inner:]
    ext_b[HALO:, :] = bc[...]
    masks = aux[...]
    conv_x = conv_rows(ext_x, HALO, rows, cxw[...], cxb[layer : layer + 1, :], masks)
    conv_b = conv_rows(ext_b, HALO, rows, cbw[...], cbb[layer : layer + 1, :], masks)
    ux[...] = conv_x
    ubc[...] = conv_b
    b_mat = silu(conv_b[:, :width])
    raw = dt[...] + dtb[layer : layer + 1, :]
    step = jnp.maximum(raw, 0.0) + jnp.log1p(jnp.exp(-jnp.abs(raw)))
    dts[...] = step
    decay = -step * jnp.exp(alog[layer : layer + 1, :])
    tri = jnp.where(lower(rows), 1.0, 0.0).astype(BF)
    total = sel_left(tri, decay, NN)
    total_t = sum(mm(part, tri, ((0,), (1,))) for part in split3(decay))
    cum[...] = total
    cumt[...] = total_t
    emap = head_map(heads, inner)
    to_end = jnp.exp(total[rows - 1 : rows, :] - total) * masks[:, 3:4] * step
    msg[0:inner, :] = mm3(silu(conv_x) * expand(to_end, emap), b_mat, TN)
    msg[inner:, :] = jnp.broadcast_to(
        jnp.exp(total_t[:, rows - 1 : rows]) * masks[rows - 1 : rows, 4:5], (heads, width)
    )


def head_kernel(cum, cumt, allowed, head):
    gap = cum[:, head : head + 1] - cumt[head : head + 1, :]
    return jnp.exp(jnp.where(allowed, gap, -1e30))


def k_intra(layer, ux, ubc, dts, cum, cumt, segc, segr, dskip, yp):
    rows, inner = ux.shape
    heads = dts.shape[1]
    width = ubc.shape[1] // 2
    per = inner // heads
    emap = head_map(heads, inner)
    x_conv = silu(ux[...])
    bc = silu(ubc[...])
    gram = mm3(bc[:, width:], bc[:, :width], NT)
    allowed = jnp.logical_and(segc[...] == segr[...], lower(rows))
    scaled = x_conv * expand(dts[...], emap)
    skip = x_conv * expand(jnp.broadcast_to(dskip[layer : layer + 1, :], (8, heads)), emap)[0:1, :]
    total, total_t = cum[...], cumt[...]
    group = max(1, 128 // per)
    for first in range(0, heads, group):
        cols = slice(first * per, (first + group) * per)
        sh, sl = split2(scaled[:, cols])
        lane = lax.broadcasted_iota(jnp.int32, (rows, group * per), 1)
        result = skip[:, cols]
        for head in range(first, first + group):
            gh, gl = split2(gram * head_kernel(total, total_t, allowed, head))
            part = mm(gh, sh, NN) + (mm(gh, sl, NN) + mm(gl, sh, NN))
            result = result + jnp.where(lane // per == head - first, part, 0.0)
        yp[:, cols] = result


def k_gate(flag, yp, ubc, cum, aux, z, near, far, mixed, gated, ss, inc):
    inner = yp.shape[1]
    heads = cum.shape[1]
    merge(heads, flag, near, far, inc)
    width = ubc.shape[1] // 2
    emap = head_map(heads, inner)
    c_mat = silu(ubc[:, width:])
    into = jnp.exp(cum[...]) * aux[:, 4:5]
    mix = yp[...] + mm3(c_mat, inc[...], NT) * expand(into, emap)
    mixed[...] = mix
    gate = mix * silu(z[...])
    gated[...] = gate
    ss[...] = row_sums(gate * gate)


def to_relative(place, source, target):
    pieces = place.shape[0]
    size = source.shape[0] // pieces
    for piece in range(pieces):
        target[piece * size : (piece + 1) * size, :] = source[rows_at(place, piece, size), :]


def k_out(layer, total, place, gated, ss, gain, wout, gn, keep, send, moved):
    scale = to_column(lax.rsqrt(ss[...] * (1.0 / total) + eps))
    normed = (gated[...] * scale * gain[layer : layer + 1, :]).astype(BF)
    gn[...] = normed
    to_relative(place, gn, moved)
    half = keep.shape[0]
    part = mm(moved[...], wout[...], NN)
    keep[...] = part[:half, :]
    send[...] = part[half:, :]


def k_b1_top(layer, total, cot, wout, gated, ss, gain, cb, dgn, cross, ggain):
    cb[...] = cot[...].astype(BF)
    back_out(layer, total, wout, gated, ss, gain, cb, dgn, cross, ggain)


def k_b1(layer, total, place, *refs):
    pieces, (wout, gated, ss, gain, cb, dgn, cross, ggain) = refs[:-8], refs[-8:]
    k_place(place, *pieces, cb)
    back_out(layer, total, wout, gated, ss, gain, cb, dgn, cross, ggain)


def back_out(layer, total, wout, gated, ss, gain, cb, dgn, cross, ggain):
    grad = mm(cb[...], wout[...], NT)
    dgn[...] = grad
    scale = to_column(lax.rsqrt(ss[...] * (1.0 / total) + eps))
    both = grad * gated[...]
    cross[...] = row_sums(both * gain[layer : layer + 1, :])
    ggain[...] = jnp.sum(both * scale, axis=0, keepdims=True)


def k_b2(layer, total, dgn, gated, mixed, z, ss, cross, gain, ubc, cum, cumt, aux, dm, dz, msg):
    rows, inner = dgn.shape
    heads = cum.shape[1]
    width = ubc.shape[1] // 2
    emap = head_map(heads, inner)
    scale_row = lax.rsqrt(ss[...] * (1.0 / total) + eps)
    scale = to_column(scale_row)
    pull = to_column(scale_row * scale_row * scale_row * cross[...] * (1.0 / total))
    d_gated = scale * gain[layer : layer + 1, :] * dgn[...] - gated[...] * pull
    zv = z[...]
    grad = d_gated * silu(zv)
    dm[...] = grad
    dz[...] = (d_gated * mixed[...] * silu_slope(zv)).astype(BF)
    masks = aux[...]
    into = jnp.exp(cum[...]) * masks[:, 4:5]
    msg[0:inner, :] = mm3(grad * expand(into, emap), silu(ubc[:, width:]), TN)
    msg[inner:, :] = jnp.broadcast_to(
        jnp.exp(cumt[:, rows - 1 : rows]) * masks[rows - 1 : rows, 4:5], (heads, width)
    )


def k_b3(layer, dm, ux, ubc, dts, cum, cumt, segc, segr, mixed, inc, aux, dskip,
         dx, dbc, dcum, ddt, gskip):
    rows, inner = ux.shape
    heads = dts.shape[1]
    width = ubc.shape[1] // 2
    per = inner // heads
    emap = head_map(heads, inner)
    x_conv = silu(ux[...])
    bc = silu(ubc[...])
    b_mat, c_mat = bc[:, :width], bc[:, width:]
    gram = mm3(c_mat, b_mat, NT)
    allowed = jnp.logical_and(segc[...] == segr[...], lower(rows))
    step = dts[...]
    step_e = expand(step, emap)
    scaled = x_conv * step_e
    grad = dm[...]
    total, total_t = cum[...], cumt[...]
    skip_row = dskip[layer : layer + 1, :]
    skip_e = expand(jnp.broadcast_to(skip_row, (8, heads)), emap)[0:1, :]
    d_gram = jnp.zeros((rows, rows), F32)
    group = max(1, 128 // per)
    plain = []
    for first in range(0, heads, group):
        cols = slice(first * per, (first + group) * per)
        sh, sl = split2(scaled[:, cols])
        lane = lax.broadcasted_iota(jnp.int32, (rows, group * per), 1)
        g_cols = grad[:, cols]
        ch, cl = split2(g_cols)
        result = jnp.zeros((rows, group * per), F32)
        for head in range(first, first + group):
            mine = lane // per == head - first
            fall = head_kernel(total, total_t, allowed, head)
            gh, gl = split2(gram * fall)
            part = mm(gh, ch, TN) + (mm(gh, cl, TN) + mm(gl, ch, TN))
            result = result + jnp.where(mine, part, 0.0)
            mh = jnp.where(mine, ch, jnp.zeros_like(ch))
            ml = jnp.where(mine, cl, jnp.zeros_like(cl))
            outer = mm(mh, sh, NT) + (mm(mh, sl, NT) + mm(ml, sh, NT))
            d_gram = d_gram + outer * fall
        plain.append(result)
    plain = jnp.concatenate(plain, axis=1)
    dx[...] = plain * step_e + grad * skip_e
    into = jnp.exp(total) * aux[:, 4:5]
    dbc[:, :width] = mm3(d_gram, c_mat, TN)
    dbc[:, width:] = mm3(d_gram, b_mat, NN) + mm3(grad * expand(into, emap), inc[...], NN)
    by_col = per_head(x_conv * plain, emap)
    skip_dot = per_head(grad * x_conv, emap)
    ddt[...] = by_col
    dcum[...] = per_head(grad * mixed[...], emap) - skip_row * skip_dot - step * by_col
    gskip[...] = jnp.sum(skip_dot, axis=0, keepdims=True)


def k_b4(layer, flag, ux, ubc, dts, dtp, cum, aux, dx, dbc, dcum, ddt, near, far, inc, dtb, alog,
         du, dbo, dd, gdtb, galog, edge, df):
    rows, inner = ux.shape
    heads = dts.shape[1]
    width = ubc.shape[1] // 2
    merge(heads, flag, near, far, df)
    emap = head_map(heads, inner)
    conv = ux[...]
    x_conv = silu(conv)
    b_mat = silu(ubc[:, :width])
    total, step, masks = cum[...], dts[...], aux[...]
    fin = df[...]
    spread = mm3(b_mat, fin, NT)
    bare = jnp.exp(total[rows - 1 : rows, :] - total) * masks[:, 3:4]
    to_end = bare * step
    to_end_e = expand(to_end, emap)
    dot = per_head(x_conv * spread, emap)
    du[...] = (dx[...] + to_end_e * spread) * silu_slope(conv)
    slope = silu_slope(ubc[...])
    dbo[:, :width] = (dbc[:, :width] + mm3(x_conv * to_end_e, fin, NN)) * slope[:, :width]
    dbo[:, width:] = dbc[:, width:] * slope[:, width:]
    edge[:, :inner] = du[0:HALO, :]
    edge[:, inner:] = dbo[0:HALO, :]
    used = to_end * dot
    d_cum = dcum[...] - used
    through = per_head(row_sums(fin * inc[...]) + jnp.zeros((8, inner), F32), emap)[0:1, :]
    last = jnp.sum(used, axis=0, keepdims=True) + through * (
        jnp.exp(total[rows - 1 : rows, :]) * masks[rows - 1 : rows, 4:5]
    )
    tri = jnp.where(lower(rows), 1.0, 0.0).astype(BF)
    d_decay = sel_left(tri, d_cum, TN) + last
    rate = jnp.exp(alog[layer : layer + 1, :])
    galog[...] = jnp.sum(-step * rate * d_decay, axis=0, keepdims=True)
    d_raw = (ddt[...] + bare * dot - rate * d_decay) * sigmoid(dtp[...] + dtb[layer : layer + 1, :])
    gdtb[...] = jnp.sum(d_raw, axis=0, keepdims=True)
    dd[...] = d_raw.astype(BF)


def k_conv_back(du, halo, proj, edge, aux, weights, grad, gw, gb, ext_d, ext_p):
    rows = du.shape[0]
    ext_d[0:rows, :] = du[...]
    ext_d[rows:, :] = halo[...]
    conv_back(proj, edge, aux, weights, grad, gw, gb, ext_d, ext_p)


def k_conv_back_b(which, du, proj, edge, aux, weights, grad, gw, gb, part, ext_d, ext_p):
    quarter = du.shape[1]
    for slot in range(ext_d.shape[1] // quarter):
        cols = slice(slot * quarter, (slot + 1) * quarter)
        ext_d[:, cols] = jnp.where(which[0] == slot, du[...], 0.0)
    wide = conv_back(proj, edge, aux, weights, grad, gw, gb, ext_d, ext_p)
    part[...] = sum(
        wide[:, slot * quarter : (slot + 1) * quarter] for slot in range(ext_d.shape[1] // quarter)
    ).astype(BF)


def conv_back(proj, edge, aux, weights, grad, gw, gb, ext_d, ext_p):
    rows = proj.shape[0]
    taps = weights.shape[0]
    ext_p[0:HALO, :] = edge[...]
    ext_p[HALO:, :] = proj[...]
    masks = aux[...]
    value = ext_d[0:rows, :]
    total = jnp.zeros_like(value)
    for tap in range(taps):
        back = ext_d[pl.ds(taps - 1 - tap, rows), :] * weights[tap : tap + 1, :]
        seen = ext_p[pl.ds(HALO - taps + 1 + tap, rows), :] * value
        if tap < taps - 1:
            back = back * masks[:, 5 + tap : 6 + tap]
            seen = seen * masks[:, tap : tap + 1]
        total = total + back
        gw[tap : tap + 1, :] = jnp.sum(seen, axis=0, keepdims=True)
    gb[...] = jnp.sum(value, axis=0, keepdims=True)
    grad[...] = total.astype(BF)
    return total


def k_dnorm(place, dz, dxb, dd, dbq, wz, wx, wdt, wbq, keep, send, own, moved):
    own[...] = (
        mm(dz[...], wz[...], NT)
        + mm(dxb[...], wx[...], NT)
        + mm(dd[...], wdt[...], NT)
        + mm(dbq[...], wbq[...], NT)
    )
    to_relative(place, own, moved)
    half = keep.shape[0]
    keep[...] = moved[0:half, :]
    send[...] = moved[half:, :]


def k_norm_back(resid, keep, got, gain, cot, out, g_gain):
    grad = keep[...] + got[...]
    value = resid[...]
    inv = lax.rsqrt(jnp.mean(value * value, axis=1, keepdims=True) + eps)
    unit = value * inv
    g_gain[...] = jnp.sum(grad * unit, axis=0, keepdims=True)
    scaled = grad * gain[...]
    mean = jnp.mean(scaled * unit, axis=1, keepdims=True)
    out[...] = cot[...] + inv * (scaled - unit * mean)


def k_dw(place, left, *refs):
    rights, (keep, send, moved, full) = refs[:-4], refs[-4:]
    pieces = place.shape[0]
    size = left.shape[1] // pieces
    half = keep.shape[0]
    aligned = size % 128 == 0
    if aligned:
        for piece in range(pieces):
            moved[:, piece * size : (piece + 1) * size] = left[:, rows_at(place, piece, size)]
    start = 0
    for right in rights:
        cols = slice(start, start + right.shape[1])
        start += right.shape[1]
        if aligned:
            keep[:, cols] = mm(moved[:, :half], right[...], TN)
            send[:, cols] = mm(moved[:, half:], right[...], TN)
        else:
            full[:, cols] = mm(left[...], right[...], TN)
    if not aligned:
        for piece in range(pieces):
            target, row = (keep, piece) if piece < pieces // 2 else (send, piece - pieces // 2)
            target[row * size : (row + 1) * size, :] = full[rows_at(place, piece, size), :]


def local(hidden_in, seg_ids, norm_gain, w_z, w_x, w_bc, w_dt, conv_x_w, conv_x_b, conv_bc_w,
          conv_bc_b, dt_bias, a_log, d_skip, gate_gain, w_out, out_cot):
    rows, model = hidden_in.shape
    layers = w_z.shape[0]
    heads = w_dt.shape[2]
    inner = w_z.shape[2]
    state2 = w_bc.shape[2]
    width = state2 // 2
    taps = conv_x_w.shape[1]
    inner_total = inner * lax.axis_size("head")
    seq_bits = bits_of("seq")
    spare = list(range(3, seq_bits))
    orders = [
        [bit for bit in base if bit < seq_bits] + spare
        for base in ([0, 1, 2], [1, 0, 2])
    ]
    share = model // lax.axis_size("seq")
    head_bits = bits_of("head")
    size = rows // lax.axis_size("head")
    place = jnp.stack(
        [
            reverse_bits(lax.axis_index("head") ^ mask, head_bits) * size
            for mask in relative_order(head_bits)
        ]
    ).astype(jnp.int32)

    padded = jnp.concatenate(
        [jnp.full((taps - 1,), -1, jnp.int32), seg_ids, jnp.full((taps - 1,), -1, jnp.int32)]
    )
    around = lax.dynamic_slice_in_dim(
        padded, lax.axis_index("seq") * rows, rows + 2 * (taps - 1)
    )
    own = around[taps - 1 : taps - 1 + rows]
    seg_before = around[taps - 2]
    columns = [around[k : k + rows] == own for k in range(taps - 1)]
    columns += [own == own[rows - 1], own == seg_before]
    columns += [around[2 * (taps - 1) - k : 2 * (taps - 1) - k + rows] == own for k in range(taps - 1)]
    aux = jnp.stack(columns, axis=1).astype(F32)
    segc, segr = own[:, None], own[None, :]

    own_quarter = reverse_bits(lax.axis_index("head"), head_bits).reshape(1).astype(jnp.int32)
    half_rows = ((rows // 2, model), F32)
    quarter_rows = ((size, model), F32)
    proj_outs = [((rows, inner), F32), ((rows, inner), F32), ((rows, state2), F32),
                 ((rows, heads), F32), ((rows, model), BF)]
    message = ((inner + heads, width), F32)

    resid = own_piece(hidden_in, "head", 0).astype(F32)
    normed = None
    saved = []
    for l in range(layers):
        weights = (Far(w_z, l), Far(w_x, l), Far(w_bc, l), Far(w_dt, l))
        if l == 0:
            z, x, bc, dtp, nb = run(
                k_proj_first, proj_outs, hidden_in, norm_gain[l : l + 1], *weights, name="proj"
            )
        else:
            z, x, bc, dtp, nb = run(
                k_proj, proj_outs, *gather_pieces(normed, "head"), *weights, small=[place],
                name="proj",
            )
        edge = rotate(jnp.concatenate([x[rows - HALO :], bc[rows - HALO :]], 1), "seq", 1)
        ux, ubc, dts, cum, cumt, msg = run(
            functools.partial(k_front, l),
            [((rows, inner), F32), ((rows, state2), F32), ((rows, heads), F32),
             ((rows, heads), F32), ((heads, rows), F32), message],
            x, bc, dtp, edge, aux, conv_x_w[l], conv_x_b, conv_bc_w[l], conv_bc_b, dt_bias, a_log,
            scratch=(pltpu.VMEM((rows + HALO, inner), F32), pltpu.VMEM((rows + HALO, state2), F32)),
            name="front",
        )
        near, far, flag, _ = carried(msg, heads, False)
        (yp,) = run(
            functools.partial(k_intra, l), [((rows, inner), F32)],
            ux, ubc, dts, cum, cumt, segc, segr, d_skip, name="intra",
        )
        mixed, gated, ss, inc = run(
            k_gate,
            [((rows, inner), F32), ((rows, inner), F32), ((1, rows), F32), ((inner, width), F32)],
            yp, ubc, cum, aux, z, near, far, small=[flag], name="gate",
        )
        ss = lax.psum(ss, "head")
        gn, keep, send = run(
            functools.partial(k_out, l, inner_total),
            [((rows, inner), BF), half_rows, half_rows],
            gated, ss, gate_gain, Far(w_out, l), small=[place],
            scratch=(pltpu.VMEM((rows, inner), BF),), name="out",
        )
        keep, got = finish_scatter(keep, send, "head")
        saved.append((resid, z, x, bc, dtp, nb, edge, ux, ubc, dts, cum, cumt, inc, mixed, gated,
                      ss, gn))
        last = l + 1 == layers
        resid, normed = run(
            k_join, [quarter_rows, quarter_rows], resid, keep, got,
            norm_gain[0 if last else l + 1][None, :], flops=1000000, name="join",
        )
    (hidden_out,) = run(
        k_place, [((rows, model), BF)], *gather_pieces(resid, "head"), small=[place],
        flops=1000000, name="round",
    )

    def dw_scratch(cols):
        aligned = share % 128 == 0
        return (
            pltpu.VMEM((rows, model if aligned else 128), BF),
            pltpu.VMEM((8 if aligned else model, cols), F32),
        )

    cot = own_piece(out_cot, "head", 0)
    final = [[None] * layers for _ in range(4)]

    def product(order, left, rights, after, name="dw", bare=False):
        cols = sum(right.shape[1] for right in rights)
        keep, send = run(
            k_dw, [((model // 2, cols), F32)] * 2, left, *rights, small=[seq_places(order, share)],
            after=after, scratch=dw_scratch(cols), name=name,
        )
        return (keep, send) if bare else SeqScatter(order, keep, send)

    narrow_in = [None] * layers
    small = [None] * layers
    gains = [None] * layers
    waiting = []
    for l in reversed(range(layers)):
        (resid, z, x, bc, dtp, nb, edge, ux, ubc, dts, cum, cumt, inc, mixed, gated, ss,
         gn) = saved[l]
        b1_outs = [((rows, model), BF), ((rows, inner), F32), ((1, rows), F32), ((1, inner), F32)]
        if l + 1 == layers:
            cb, dgn, cross, ggain = run(
                functools.partial(k_b1_top, l, inner_total), b1_outs,
                out_cot, Far(w_out, l), gated, ss, gate_gain, name="b1",
            )
        else:
            cb, dgn, cross, ggain = run(
                functools.partial(k_b1, l, inner_total), b1_outs,
                *gather_pieces(cot, "head"), Far(w_out, l), gated, ss, gate_gain,
                small=[place], name="b1",
            )
        cross = lax.psum(cross, "head")
        dm, dz, msg = run(
            functools.partial(k_b2, l, inner_total),
            [((rows, inner), F32), ((rows, inner), BF), message],
            dgn, gated, mixed, z, ss, cross, gate_gain, ubc, cum, cumt, aux,
            name="b2",
        )
        near, far, flag, stages = carried(msg, heads, True)
        fresh = [
            product(orders[0], cb, [gn], stages[:1]),
            product(orders[1], nb, [dz], stages[1:2]),
        ]
        dx, dbc, dcum, ddt, gskip = run(
            functools.partial(k_b3, l),
            [((rows, inner), F32), ((rows, state2), F32), ((rows, heads), F32),
             ((rows, heads), F32), ((1, heads), F32)],
            dm, ux, ubc, dts, cum, cumt, segc, segr, mixed, inc, aux,
            d_skip, after=[fresh[0].keep], name="b3",
        )
        du, dub, dd, gdtb, galog, first_rows = run(
            functools.partial(k_b4, l),
            [((rows, inner), F32), ((rows, state2), F32), ((rows, heads), BF),
             ((1, heads), F32), ((1, heads), F32), ((HALO, inner + state2), F32)],
            ux, ubc, dts, dtp, cum, aux, dx, dbc, dcum, ddt, near, far,
            inc, dt_bias, a_log,
            small=[flag], after=[fresh[1].keep], scratch=(pltpu.VMEM((inner, width), F32),),
            name="b4",
        )
        halo = rotate(first_rows, "seq", -1)
        for pending in waiting[2:] + fresh:
            pending.advance([halo])
        dub = scatter_cols(jnp.concatenate([dub, halo[:, inner:]], 0), "head")
        quarter = dub.shape[1]
        dxb, gcw, gcb = run(
            k_conv_back,
            [((rows, inner), BF), ((taps, inner), F32), ((1, inner), F32)],
            du, halo[:, :inner], x, edge[:, :inner], aux, conv_x_w[l],
            scratch=(pltpu.VMEM((rows + HALO, inner), F32), pltpu.VMEM((rows + HALO, inner), F32)),
            name="convx",
        )
        dbw, gbw, gbb, dbb = run(
            k_conv_back_b,
            [((rows, state2), BF), ((taps, state2), F32), ((1, state2), F32), ((rows, quarter), BF)],
            dub, bc, edge[:, inner:], aux, conv_bc_w[l], small=[own_quarter],
            scratch=(pltpu.VMEM((rows + HALO, state2), F32),
                     pltpu.VMEM((rows + HALO, state2), F32)),
            name="convb",
        )
        keep, send = run(
            k_dnorm, [half_rows, half_rows],
            dz, dxb, dd, dbw, Far(w_z, l), Far(w_x, l), Far(w_dt, l), Far(w_bc, l), small=[place],
            scratch=(pltpu.VMEM((rows, model), F32), pltpu.VMEM((rows, model), F32)), name="dnorm",
        )
        keep, got = finish_scatter(keep, send, "head")
        fresh += [
            product(orders[0], nb, [dxb[:, : inner // 2]], []),
            product(orders[1], nb, [dxb[:, inner // 2 :]], []),
        ]
        cot, gains[l] = run(
            k_norm_back, [quarter_rows, ((1, model), F32)],
            resid, keep, got, norm_gain[l : l + 1], cot,
            after=[pending.keep for pending in fresh[2:]], flops=1000000, name="normback",
        )
        for pending in fresh:
            pending.advance([cot])
        for slot in range(len(waiting)):
            final[slot][l + 1] = waiting[slot].result()
        waiting = fresh
        narrow_in[l] = (nb, dbb, dd)
        small[l] = (gcw, gcb, gbw, gbb, gdtb, galog, gskip, ggain)
    for pending in waiting[2:]:
        pending.advance([cot])
    for slot in range(len(waiting)):
        final[slot][0] = waiting[slot].result()
    (grad_in,) = run(
        k_place, [((rows, model), F32)], *gather_pieces(cot, "head"), small=[place],
        flops=1000000, name="place",
    )

    late = [seq_bits - 1] + list(range(seq_bits - 1))
    pairs = [product(late, n[0], n[1:], [cot], "dwn", True) for n in narrow_in]
    narrow = SeqScatter(
        late,
        jnp.concatenate([pair[0] for pair in pairs], 1),
        jnp.concatenate([pair[1] for pair in pairs], 1),
    ).result()
    narrow = jnp.stack(jnp.split(narrow, layers, 1))

    def reduced(flat, order):
        sizes = [part.size for part in flat]
        pack = jnp.concatenate([part.reshape(-1) for part in flat])
        pack = jnp.pad(pack, (0, -pack.size % 1024)).reshape(-1, 128)
        pack = seq_sum(pack, order).reshape(-1)
        pieces, start = [], 0
        for count in sizes:
            pieces.append(pack[start : start + count])
            start += count
        return pieces

    pieces = reduced([part for l in range(layers) for part in small[l]] + gains, late)
    count = len(small[0])

    def both(slot):
        return jnp.stack([pieces[l * count + slot].reshape(small[l][slot].shape) for l in range(layers)])

    wide = jnp.concatenate(
        pieces[layers * count :] + [both(2).reshape(-1), both(3).reshape(-1)]
    )
    wide = head_sum(wide.reshape(-1, 128)).reshape(-1)
    stop = layers * model
    grad_gain = wide[:stop].reshape(layers, model)
    grad_gain = lax.dynamic_slice_in_dim(grad_gain, lax.axis_index("seq") * share, share, 1)
    bc_w = wide[stop : stop + layers * taps * state2].reshape(layers, taps, state2)
    bc_b = wide[stop + layers * taps * state2 :].reshape(layers, state2)
    bc_parts = gather_back(narrow[:, :, :quarter], "head", 2)
    return (
        hidden_out,
        grad_in,
        grad_gain,
        jnp.stack(final[1]),
        jnp.stack([jnp.concatenate(pair, 1) for pair in zip(final[2], final[3])]),
        bc_parts,
        narrow[:, :, quarter:],
        both(0),
        both(1)[:, 0],
        bc_w,
        bc_b,
        both(4)[:, 0],
        both(5)[:, 0],
        both(6)[:, 0],
        both(7)[:, 0],
        jnp.stack([part.T for part in final[0]]),
    )


def solution(mesh):
    return jax.shard_map(
        local,
        mesh=mesh,
        in_specs=(
            P("seq", None),
            P(),
            P(),
            P(None, None, "head"),
            P(None, None, "head"),
            P(),
            P(None, None, "head"),
            P(None, None, "head"),
            P(None, "head"),
            P(),
            P(),
            P(None, "head"),
            P(None, "head"),
            P(None, "head"),
            P(None, "head"),
            P(None, "head", None),
            P("seq", None),
        ),
        out_specs=(
            P("seq", None),
            P("seq", None),
            P(None, "seq"),
            P(None, "seq", "head"),
            P(None, "seq", "head"),
            P(None, "seq", None),
            P(None, "seq", "head"),
            P(None, None, "head"),
            P(None, "head"),
            P(),
            P(),
            P(None, "head"),
            P(None, "head"),
            P(None, "head"),
            P(None, "head"),
            P(None, "head", "seq"),
        ),
        check_vma=False,
    )
```

```python
import functools

import jax
import jax.numpy as jnp
from jax import lax
from jax.experimental import pallas as pl
from jax.experimental.pallas import tpu as pltpu
from jax.sharding import PartitionSpec as P

eps = 1e-05
F32, BF = jnp.float32, jnp.bfloat16
NN, NT, TN = ((1,), (0,)), ((1,), (1,)), ((0,), (0,))
HALO = 8
GRANT = 16 << 20


def swap(value, axis, mask):
    count = lax.axis_size(axis)
    return lax.ppermute(value, axis, [(i, i ^ mask) for i in range(count)])


def rotate(value, axis, steps):
    count = lax.axis_size(axis)
    return lax.ppermute(value, axis, [(i, (i + steps) % count) for i in range(count)])


def bit_of(axis, bit):
    return (lax.axis_index(axis) >> bit) & 1


def bits_of(axis):
    return lax.axis_size(axis).bit_length() - 1


def reverse_bits(value, count):
    result = 0
    for bit in range(count):
        result = result | (((value >> bit) & 1) << (count - 1 - bit))
    return result


def relative_order(count):
    return [reverse_bits(i, count) for i in range(1 << count)]


def finish_scatter(keep, send, axis):
    for bit in range(bits_of(axis)):
        got = swap(send, axis, 1 << bit)
        half = keep.shape[0] // 2
        if bit + 1 < bits_of(axis):
            send = keep[half:] + got[half:]
            keep = keep[:half] + got[:half]
    return keep, got


def scatter_cols(value, axis):
    for bit in range(bits_of(axis)):
        half = value.shape[1] // 2
        which = bit_of(axis, bit)
        keep = lax.dynamic_slice_in_dim(value, which * half, half, 1)
        send = lax.dynamic_slice_in_dim(value, (1 - which) * half, half, 1)
        value = keep + swap(send, axis, 1 << bit)
    return value


def gather_pieces(mine, axis):
    pieces = [mine]
    for bit in reversed(range(bits_of(axis))):
        pieces = pieces + [swap(piece, axis, 1 << bit) for piece in pieces]
    return pieces


def gather_back(value, axis, dim):
    for bit in reversed(range(bits_of(axis))):
        other = swap(value, axis, 1 << bit)
        first = bit_of(axis, bit) == 0
        value = jnp.where(
            first,
            jnp.concatenate([value, other], dim),
            jnp.concatenate([other, value], dim),
        )
    return value


def own_piece(value, axis, dim):
    for bit in range(bits_of(axis)):
        half = value.shape[dim] // 2
        value = lax.dynamic_slice_in_dim(value, bit_of(axis, bit) * half, half, dim)
    return value


def mask_of(bit):
    return 1 << bit


def seq_places(order, share):
    count = len(order)
    me = lax.axis_index("seq")
    starts = []
    for piece in range(1 << count):
        mask = 0
        for step, bit in enumerate(order):
            if (piece >> (count - 1 - step)) & 1:
                mask ^= mask_of(bit)
        starts.append((me ^ mask) * share)
    return jnp.stack(starts).astype(jnp.int32)


class SeqScatter:
    def __init__(self, order, keep, send):
        self.order, self.keep, self.step = order, keep, 0
        self.got = swap(send, "seq", mask_of(order[0]))

    def advance(self, after=()):
        self.step += 1
        if self.step == len(self.order):
            self.keep = self.keep + self.got
        elif self.step < len(self.order):
            rows, cols = self.keep.shape
            half = ((rows // 2, cols), F32)
            self.keep, send = run(
                k_add, [half, half], self.keep, self.got, after=after, flops=rows * cols, name="add"
            )
            self.got = swap(send, "seq", mask_of(self.order[self.step]))

    def result(self, after=()):
        while self.step < len(self.order):
            self.advance(after)
        return self.keep


def seq_sum(value, order):
    for bit in order:
        value = value + swap(value, "seq", mask_of(bit))
    return value


def head_sum(value):
    for bit in range(bits_of("head")):
        value = value + swap(value, "head", 1 << bit)
    return value


def carried(message, heads, reverse):
    count = bits_of("seq")
    shape = [(message.shape, F32)]
    flags = [
        ((1 - bit_of("seq", bit)) if reverse else bit_of("seq", bit)).reshape(1).astype(jnp.int32)
        for bit in range(count)
    ]
    ahead, stages = None, []
    for bit in range(count - 1):
        got = swap(message, "seq", mask_of(bit))
        if ahead is None:
            ahead, message = run(
                functools.partial(k_scan_first, heads), shape * 2, message, got, small=[flags[bit]],
                flops=1000000, name="scan",
            )
        else:
            ahead, message = run(
                functools.partial(k_scan, heads), shape * 2, message, ahead, got,
                small=[flags[bit]], flops=1000000, name="scan",
            )
        stages.append(ahead)
    return ahead, swap(message, "seq", mask_of(count - 1)), flags[count - 1], stages


def mm(left, right, dims):
    return lax.dot_general(left, right, (dims, ((), ())), preferred_element_type=F32)


def split2(value):
    high = value.astype(BF)
    return high, (value - high.astype(F32)).astype(BF)


def mm3(left, right, dims):
    lh, ll = split2(left)
    rh, rl = split2(right)
    return mm(lh, rh, dims) + (mm(lh, rl, dims) + mm(ll, rh, dims))


def split3(value):
    high = value.astype(BF)
    rest = value - high.astype(F32)
    mid = rest.astype(BF)
    return high, mid, (rest - mid.astype(F32)).astype(BF)


def sel_right(value, sel, dims):
    return sum(mm(part, sel, dims) for part in split3(value))


def sel_left(sel, value, dims):
    return sum(mm(sel, part, dims) for part in split3(value))


def head_map(heads, inner):
    chan = lax.broadcasted_iota(jnp.int32, (inner, heads), 0)
    head = lax.broadcasted_iota(jnp.int32, (inner, heads), 1)
    return jnp.where(chan // (inner // heads) == head, 1.0, 0.0).astype(BF)


def expand(value, emap):
    return sel_right(value, emap, NT)


def per_head(value, emap):
    return sel_right(value, emap, NN)


def lower(rows):
    row = lax.broadcasted_iota(jnp.int32, (rows, rows), 0)
    col = lax.broadcasted_iota(jnp.int32, (rows, rows), 1)
    return row >= col


def to_column(row_value):
    rows = row_value.shape[1]
    row = lax.broadcasted_iota(jnp.int32, (rows, rows), 0)
    col = lax.broadcasted_iota(jnp.int32, (rows, rows), 1)
    return jnp.sum(jnp.where(row == col, row_value, 0.0), axis=1, keepdims=True)


def row_sums(value):
    ones = jnp.ones((8, value.shape[1]), BF)
    return sel_left(ones, value, NT)[0:1, :]


def sigmoid(value):
    return 1.0 / (1.0 + jnp.exp(-value))


def silu(value):
    return value * sigmoid(value)


def silu_slope(value):
    sig = sigmoid(value)
    return sig * (1.0 + value * (1.0 - sig))


class Far:
    def __init__(self, value, layer):
        self.value, self.layer = value, layer
        self.shape = value.shape[1:]


def run(body, outs, *args, small=(), after=(), scratch=(), flops=2_000_000_000, name=None):
    held = pl.BlockSpec(memory_space=pltpu.VMEM)
    first, second = len(small), len(small) + len(args)
    values = [arg.value if isinstance(arg, Far) else arg for arg in args]
    moved = sum(a.size * a.dtype.itemsize for a in values)

    def inner(*refs):
        given = list(refs[:second])
        for i, arg in enumerate(args):
            if isinstance(arg, Far):
                given[first + i] = given[first + i].at[arg.layer]
        body(*given, *refs[second + len(after) :])

    return pl.pallas_call(
        inner,
        in_specs=[pl.BlockSpec(memory_space=pltpu.SMEM)] * first
        + [held] * len(args)
        + [pl.BlockSpec(memory_space=pl.ANY)] * len(after),
        out_specs=[held] * len(outs),
        out_shape=[jax.ShapeDtypeStruct(shape, kind) for shape, kind in outs],
        scratch_shapes=list(scratch),
        compiler_params=pltpu.CompilerParams(vmem_limit_bytes=GRANT),
        cost_estimate=pl.CostEstimate(flops=flops, bytes_accessed=moved, transcendentals=0),
        name=name,
    )(*small, *values, *after)


def rows_at(place, piece, size):
    return pl.ds(pl.multiple_of(place[piece], size), size)


def norm_rows(value, gain):
    return value * lax.rsqrt(jnp.mean(value * value, axis=1, keepdims=True) + eps) * gain


def k_add(keep, got, first, second):
    half = first.shape[0]
    first[...] = keep[0:half, :] + got[0:half, :]
    second[...] = keep[half:, :] + got[half:, :]


def merge(heads, flag, near, far, state, decay=None):
    rows = near.shape[0] - heads
    per = rows // heads
    use = flag[0] == 1
    for head in range(heads):
        cols = slice(head * per, (head + 1) * per)
        fade = near[rows + head : rows + head + 1, :]
        state[cols, :] = jnp.where(use, fade * far[cols, :] + near[cols, :], near[cols, :])
    if decay is not None:
        fades = near[rows:, :]
        decay[...] = jnp.where(use, fades * far[rows:, :], fades)


def k_scan_first(heads, flag, mine, got, ahead, total):
    rows = mine.shape[0] - heads
    use = flag[0] == 1
    ahead[0:rows, :] = jnp.where(use, got[0:rows, :], 0.0)
    ahead[rows:, :] = jnp.where(use, got[rows:, :], 1.0)
    join(heads, use, mine, got, total)


def join(heads, use, mine, got, total):
    rows = mine.shape[0] - heads
    per = rows // heads
    for head in range(heads):
        cols = slice(head * per, (head + 1) * per)
        own, other = mine[cols, :], got[cols, :]
        own_fade = mine[rows + head : rows + head + 1, :]
        got_fade = got[rows + head : rows + head + 1, :]
        total[cols, :] = jnp.where(use, own_fade * other + own, got_fade * own + other)
    total[rows:, :] = mine[rows:, :] * got[rows:, :]


def k_scan(heads, flag, mine, ahead, got, ahead_out, total):
    rows = mine.shape[0] - heads
    merge(heads, flag, ahead, got, ahead_out, ahead_out.at[pl.ds(rows, heads), :])
    join(heads, flag[0] == 1, mine, got, total)


def k_join(resid, keep, got, gain, total, normed):
    value = resid[...] + (keep[...] + got[...])
    total[...] = value
    normed[...] = norm_rows(value, gain[...])


def k_place(place, *refs):
    out = refs[-1]
    size = refs[0].shape[0]
    for piece, ref in enumerate(refs[:-1]):
        out[rows_at(place, piece, size), :] = ref[:, : out.shape[1]].astype(out.dtype)


def project(rounded, wz, wx, wbc, wdt, z, x, bc, dt):
    x[...] = mm(rounded, wx[...], NN)
    bc[...] = mm(rounded, wbc[...], NN)
    dt[...] = mm(rounded, wdt[...], NN)
    z[...] = mm(rounded, wz[...], NN)


def k_proj_first(hidden, gain, wz, wx, wbc, wdt, z, x, bc, dt, nb):
    rounded = norm_rows(hidden[...].astype(F32), gain[...]).astype(BF)
    nb[...] = rounded
    project(rounded, wz, wx, wbc, wdt, z, x, bc, dt)


def k_proj(place, *refs):
    pieces, (wz, wx, wbc, wdt, z, x, bc, dt, nb) = refs[:-9], refs[-9:]
    k_place(place, *pieces, nb)
    project(nb[...], wz, wx, wbc, wdt, z, x, bc, dt)


def conv_rows(ext, halo_rows, rows, weights, bias, aux):
    total = jnp.broadcast_to(bias, (rows, weights.shape[1]))
    taps = weights.shape[0]
    for tap in range(taps):
        part = ext[pl.ds(halo_rows - taps + 1 + tap, rows), :] * weights[tap : tap + 1, :]
        total = total + (part * aux[:, tap : tap + 1] if tap < taps - 1 else part)
    return total


def k_front(layer, x, bc, dt, edge, aux, cxw, cxb, cbw, cbb, dtb, alog,
            ux, ubc, dts, cum, cumt, msg, ext_x, ext_b):
    rows, inner = x.shape
    heads = dt.shape[1]
    width = bc.shape[1] // 2
    ext_x[0:HALO, :] = edge[:, :inner]
    ext_x[HALO:, :] = x[...]
    ext_b[0:HALO, :] = edge[:, inner:]
    ext_b[HALO:, :] = bc[...]
    masks = aux[...]
    conv_x = conv_rows(ext_x, HALO, rows, cxw[...], cxb[layer : layer + 1, :], masks)
    conv_b = conv_rows(ext_b, HALO, rows, cbw[...], cbb[layer : layer + 1, :], masks)
    ux[...] = conv_x
    ubc[...] = conv_b
    b_mat = silu(conv_b[:, :width])
    raw = dt[...] + dtb[layer : layer + 1, :]
    step = jnp.maximum(raw, 0.0) + jnp.log1p(jnp.exp(-jnp.abs(raw)))
    dts[...] = step
    decay = -step * jnp.exp(alog[layer : layer + 1, :])
    tri = jnp.where(lower(rows), 1.0, 0.0).astype(BF)
    total = sel_left(tri, decay, NN)
    total_t = sum(mm(part, tri, ((0,), (1,))) for part in split3(decay))
    cum[...] = total
    cumt[...] = total_t
    emap = head_map(heads, inner)
    to_end = jnp.exp(total[rows - 1 : rows, :] - total) * masks[:, 3:4] * step
    msg[0:inner, :] = mm3(silu(conv_x) * expand(to_end, emap), b_mat, TN)
    msg[inner:, :] = jnp.broadcast_to(
        jnp.exp(total_t[:, rows - 1 : rows]) * masks[rows - 1 : rows, 4:5], (heads, width)
    )


def head_kernel(cum, cumt, allowed, head):
    gap = cum[:, head : head + 1] - cumt[head : head + 1, :]
    return jnp.exp(jnp.where(allowed, gap, -1e30))


def k_intra(layer, ux, ubc, dts, cum, cumt, segc, segr, dskip, yp):
    rows, inner = ux.shape
    heads = dts.shape[1]
    width = ubc.shape[1] // 2
    per = inner // heads
    emap = head_map(heads, inner)
    x_conv = silu(ux[...])
    bc = silu(ubc[...])
    gram = mm3(bc[:, width:], bc[:, :width], NT)
    allowed = jnp.logical_and(segc[...] == segr[...], lower(rows))
    scaled = x_conv * expand(dts[...], emap)
    skip = x_conv * expand(jnp.broadcast_to(dskip[layer : layer + 1, :], (8, heads)), emap)[0:1, :]
    total, total_t = cum[...], cumt[...]
    group = max(1, 128 // per)
    for first in range(0, heads, group):
        cols = slice(first * per, (first + group) * per)
        sh, sl = split2(scaled[:, cols])
        lane = lax.broadcasted_iota(jnp.int32, (rows, group * per), 1)
        result = skip[:, cols]
        for head in range(first, first + group):
            gh, gl = split2(gram * head_kernel(total, total_t, allowed, head))
            part = mm(gh, sh, NN) + (mm(gh, sl, NN) + mm(gl, sh, NN))
            result = result + jnp.where(lane // per == head - first, part, 0.0)
        yp[:, cols] = result


def k_gate(flag, yp, ubc, cum, aux, z, near, far, mixed, gated, ss, inc):
    inner = yp.shape[1]
    heads = cum.shape[1]
    merge(heads, flag, near, far, inc)
    width = ubc.shape[1] // 2
    emap = head_map(heads, inner)
    c_mat = silu(ubc[:, width:])
    into = jnp.exp(cum[...]) * aux[:, 4:5]
    mix = yp[...] + mm3(c_mat, inc[...], NT) * expand(into, emap)
    mixed[...] = mix
    gate = mix * silu(z[...])
    gated[...] = gate
    ss[...] = row_sums(gate * gate)


def to_relative(place, source, target):
    pieces = place.shape[0]
    size = source.shape[0] // pieces
    for piece in range(pieces):
        target[piece * size : (piece + 1) * size, :] = source[rows_at(place, piece, size), :]


def k_out(layer, total, place, gated, ss, gain, wout, gn, keep, send, moved):
    scale = to_column(lax.rsqrt(ss[...] * (1.0 / total) + eps))
    normed = (gated[...] * scale * gain[layer : layer + 1, :]).astype(BF)
    gn[...] = normed
    to_relative(place, gn, moved)
    half = keep.shape[0]
    part = mm(moved[...], wout[...], NN)
    keep[...] = part[:half, :]
    send[...] = part[half:, :]


def k_b1_top(layer, total, cot, wout, gated, ss, gain, cb, dgn, cross, ggain):
    cb[...] = cot[...].astype(BF)
    back_out(layer, total, wout, gated, ss, gain, cb, dgn, cross, ggain)


def k_b1(layer, total, place, *refs):
    pieces, (wout, gated, ss, gain, cb, dgn, cross, ggain) = refs[:-8], refs[-8:]
    k_place(place, *pieces, cb)
    back_out(layer, total, wout, gated, ss, gain, cb, dgn, cross, ggain)


def back_out(layer, total, wout, gated, ss, gain, cb, dgn, cross, ggain):
    grad = mm(cb[...], wout[...], NT)
    dgn[...] = grad
    scale = to_column(lax.rsqrt(ss[...] * (1.0 / total) + eps))
    both = grad * gated[...]
    cross[...] = row_sums(both * gain[layer : layer + 1, :])
    ggain[...] = jnp.sum(both * scale, axis=0, keepdims=True)


def k_b2(layer, total, dgn, gated, mixed, z, ss, cross, gain, ubc, cum, cumt, aux, dm, dz, msg):
    rows, inner = dgn.shape
    heads = cum.shape[1]
    width = ubc.shape[1] // 2
    emap = head_map(heads, inner)
    scale_row = lax.rsqrt(ss[...] * (1.0 / total) + eps)
    scale = to_column(scale_row)
    pull = to_column(scale_row * scale_row * scale_row * cross[...] * (1.0 / total))
    d_gated = scale * gain[layer : layer + 1, :] * dgn[...] - gated[...] * pull
    zv = z[...]
    grad = d_gated * silu(zv)
    dm[...] = grad
    dz[...] = (d_gated * mixed[...] * silu_slope(zv)).astype(BF)
    masks = aux[...]
    into = jnp.exp(cum[...]) * masks[:, 4:5]
    msg[0:inner, :] = mm3(grad * expand(into, emap), silu(ubc[:, width:]), TN)
    msg[inner:, :] = jnp.broadcast_to(
        jnp.exp(cumt[:, rows - 1 : rows]) * masks[rows - 1 : rows, 4:5], (heads, width)
    )


def k_b3(layer, dm, ux, ubc, dts, cum, cumt, segc, segr, mixed, inc, aux, dskip,
         dx, dbc, dcum, ddt, gskip):
    rows, inner = ux.shape
    heads = dts.shape[1]
    width = ubc.shape[1] // 2
    per = inner // heads
    emap = head_map(heads, inner)
    x_conv = silu(ux[...])
    bc = silu(ubc[...])
    b_mat, c_mat = bc[:, :width], bc[:, width:]
    gram = mm3(c_mat, b_mat, NT)
    allowed = jnp.logical_and(segc[...] == segr[...], lower(rows))
    step = dts[...]
    step_e = expand(step, emap)
    scaled = x_conv * step_e
    grad = dm[...]
    total, total_t = cum[...], cumt[...]
    skip_row = dskip[layer : layer + 1, :]
    skip_e = expand(jnp.broadcast_to(skip_row, (8, heads)), emap)[0:1, :]
    d_gram = jnp.zeros((rows, rows), F32)
    group = max(1, 128 // per)
    plain = []
    for first in range(0, heads, group):
        cols = slice(first * per, (first + group) * per)
        sh, sl = split2(scaled[:, cols])
        lane = lax.broadcasted_iota(jnp.int32, (rows, group * per), 1)
        g_cols = grad[:, cols]
        ch, cl = split2(g_cols)
        result = jnp.zeros((rows, group * per), F32)
        for head in range(first, first + group):
            mine = lane // per == head - first
            fall = head_kernel(total, total_t, allowed, head)
            gh, gl = split2(gram * fall)
            part = mm(gh, ch, TN) + (mm(gh, cl, TN) + mm(gl, ch, TN))
            result = result + jnp.where(mine, part, 0.0)
            mh = jnp.where(mine, ch, jnp.zeros_like(ch))
            ml = jnp.where(mine, cl, jnp.zeros_like(cl))
            outer = mm(mh, sh, NT) + (mm(mh, sl, NT) + mm(ml, sh, NT))
            d_gram = d_gram + outer * fall
        plain.append(result)
    plain = jnp.concatenate(plain, axis=1)
    dx[...] = plain * step_e + grad * skip_e
    into = jnp.exp(total) * aux[:, 4:5]
    dbc[:, :width] = mm3(d_gram, c_mat, TN)
    dbc[:, width:] = mm3(d_gram, b_mat, NN) + mm3(grad * expand(into, emap), inc[...], NN)
    by_col = per_head(x_conv * plain, emap)
    skip_dot = per_head(grad * x_conv, emap)
    ddt[...] = by_col
    dcum[...] = per_head(grad * mixed[...], emap) - skip_row * skip_dot - step * by_col
    gskip[...] = jnp.sum(skip_dot, axis=0, keepdims=True)


def k_b4(layer, flag, ux, ubc, dts, dtp, cum, aux, dx, dbc, dcum, ddt, near, far, inc, dtb, alog,
         du, dbo, dd, gdtb, galog, edge, df):
    rows, inner = ux.shape
    heads = dts.shape[1]
    width = ubc.shape[1] // 2
    merge(heads, flag, near, far, df)
    emap = head_map(heads, inner)
    conv = ux[...]
    x_conv = silu(conv)
    b_mat = silu(ubc[:, :width])
    total, step, masks = cum[...], dts[...], aux[...]
    fin = df[...]
    spread = mm3(b_mat, fin, NT)
    bare = jnp.exp(total[rows - 1 : rows, :] - total) * masks[:, 3:4]
    to_end = bare * step
    to_end_e = expand(to_end, emap)
    dot = per_head(x_conv * spread, emap)
    du[...] = (dx[...] + to_end_e * spread) * silu_slope(conv)
    slope = silu_slope(ubc[...])
    dbo[:, :width] = (dbc[:, :width] + mm3(x_conv * to_end_e, fin, NN)) * slope[:, :width]
    dbo[:, width:] = dbc[:, width:] * slope[:, width:]
    edge[:, :inner] = du[0:HALO, :]
    edge[:, inner:] = dbo[0:HALO, :]
    used = to_end * dot
    d_cum = dcum[...] - used
    through = per_head(row_sums(fin * inc[...]) + jnp.zeros((8, inner), F32), emap)[0:1, :]
    last = jnp.sum(used, axis=0, keepdims=True) + through * (
        jnp.exp(total[rows - 1 : rows, :]) * masks[rows - 1 : rows, 4:5]
    )
    tri = jnp.where(lower(rows), 1.0, 0.0).astype(BF)
    d_decay = sel_left(tri, d_cum, TN) + last
    rate = jnp.exp(alog[layer : layer + 1, :])
    galog[...] = jnp.sum(-step * rate * d_decay, axis=0, keepdims=True)
    d_raw = (ddt[...] + bare * dot - rate * d_decay) * sigmoid(dtp[...] + dtb[layer : layer + 1, :])
    gdtb[...] = jnp.sum(d_raw, axis=0, keepdims=True)
    dd[...] = d_raw.astype(BF)


def k_conv_back(du, halo, proj, edge, aux, weights, grad, gw, gb, ext_d, ext_p):
    rows = du.shape[0]
    ext_d[0:rows, :] = du[...]
    ext_d[rows:, :] = halo[...]
    conv_back(proj, edge, aux, weights, grad, gw, gb, ext_d, ext_p)


def k_conv_back_b(which, du, proj, edge, aux, weights, grad, gw, gb, part, ext_d, ext_p):
    quarter = du.shape[1]
    for slot in range(ext_d.shape[1] // quarter):
        cols = slice(slot * quarter, (slot + 1) * quarter)
        ext_d[:, cols] = jnp.where(which[0] == slot, du[...], 0.0)
    wide = conv_back(proj, edge, aux, weights, grad, gw, gb, ext_d, ext_p)
    part[...] = sum(
        wide[:, slot * quarter : (slot + 1) * quarter] for slot in range(ext_d.shape[1] // quarter)
    ).astype(BF)


def conv_back(proj, edge, aux, weights, grad, gw, gb, ext_d, ext_p):
    rows = proj.shape[0]
    taps = weights.shape[0]
    ext_p[0:HALO, :] = edge[...]
    ext_p[HALO:, :] = proj[...]
    masks = aux[...]
    value = ext_d[0:rows, :]
    total = jnp.zeros_like(value)
    for tap in range(taps):
        back = ext_d[pl.ds(taps - 1 - tap, rows), :] * weights[tap : tap + 1, :]
        seen = ext_p[pl.ds(HALO - taps + 1 + tap, rows), :] * value
        if tap < taps - 1:
            back = back * masks[:, 5 + tap : 6 + tap]
            seen = seen * masks[:, tap : tap + 1]
        total = total + back
        gw[tap : tap + 1, :] = jnp.sum(seen, axis=0, keepdims=True)
    gb[...] = jnp.sum(value, axis=0, keepdims=True)
    grad[...] = total.astype(BF)
    return total


def k_dnorm(place, dz, dxb, dd, dbq, wz, wx, wdt, wbq, keep, send, own, moved):
    own[...] = (
        mm(dz[...], wz[...], NT)
        + mm(dxb[...], wx[...], NT)
        + mm(dd[...], wdt[...], NT)
        + mm(dbq[...], wbq[...], NT)
    )
    to_relative(place, own, moved)
    half = keep.shape[0]
    keep[...] = moved[0:half, :]
    send[...] = moved[half:, :]


def k_norm_back(resid, keep, got, gain, cot, out, g_gain):
    grad = keep[...] + got[...]
    value = resid[...]
    inv = lax.rsqrt(jnp.mean(value * value, axis=1, keepdims=True) + eps)
    unit = value * inv
    g_gain[...] = jnp.sum(grad * unit, axis=0, keepdims=True)
    scaled = grad * gain[...]
    mean = jnp.mean(scaled * unit, axis=1, keepdims=True)
    out[...] = cot[...] + inv * (scaled - unit * mean)


def k_dw(place, left, *refs):
    rights, (keep, send, moved, full) = refs[:-4], refs[-4:]
    pieces = place.shape[0]
    size = left.shape[1] // pieces
    half = keep.shape[0]
    aligned = size % 128 == 0
    if aligned:
        for piece in range(pieces):
            moved[:, piece * size : (piece + 1) * size] = left[:, rows_at(place, piece, size)]
    start = 0
    for right in rights:
        cols = slice(start, start + right.shape[1])
        start += right.shape[1]
        if aligned:
            keep[:, cols] = mm(moved[:, :half], right[...], TN)
            send[:, cols] = mm(moved[:, half:], right[...], TN)
        else:
            full[:, cols] = mm(left[...], right[...], TN)
    if not aligned:
        for piece in range(pieces):
            target, row = (keep, piece) if piece < pieces // 2 else (send, piece - pieces // 2)
            target[row * size : (row + 1) * size, :] = full[rows_at(place, piece, size), :]


def local(hidden_in, seg_ids, norm_gain, w_z, w_x, w_bc, w_dt, conv_x_w, conv_x_b, conv_bc_w,
          conv_bc_b, dt_bias, a_log, d_skip, gate_gain, w_out, out_cot):
    rows, model = hidden_in.shape
    layers = w_z.shape[0]
    heads = w_dt.shape[2]
    inner = w_z.shape[2]
    state2 = w_bc.shape[2]
    width = state2 // 2
    taps = conv_x_w.shape[1]
    inner_total = inner * lax.axis_size("head")
    seq_bits = bits_of("seq")
    spare = list(range(3, seq_bits))
    orders = [
        [bit for bit in base if bit < seq_bits] + spare
        for base in ([0, 1, 2], [1, 0, 2])
    ]
    share = model // lax.axis_size("seq")
    head_bits = bits_of("head")
    size = rows // lax.axis_size("head")
    place = jnp.stack(
        [
            reverse_bits(lax.axis_index("head") ^ mask, head_bits) * size
            for mask in relative_order(head_bits)
        ]
    ).astype(jnp.int32)

    padded = jnp.concatenate(
        [jnp.full((taps - 1,), -1, jnp.int32), seg_ids, jnp.full((taps - 1,), -1, jnp.int32)]
    )
    around = lax.dynamic_slice_in_dim(
        padded, lax.axis_index("seq") * rows, rows + 2 * (taps - 1)
    )
    own = around[taps - 1 : taps - 1 + rows]
    seg_before = around[taps - 2]
    columns = [around[k : k + rows] == own for k in range(taps - 1)]
    columns += [own == own[rows - 1], own == seg_before]
    columns += [around[2 * (taps - 1) - k : 2 * (taps - 1) - k + rows] == own for k in range(taps - 1)]
    aux = jnp.stack(columns, axis=1).astype(F32)
    segc, segr = own[:, None], own[None, :]

    own_quarter = reverse_bits(lax.axis_index("head"), head_bits).reshape(1).astype(jnp.int32)
    half_rows = ((rows // 2, model), F32)
    quarter_rows = ((size, model), F32)
    proj_outs = [((rows, inner), F32), ((rows, inner), F32), ((rows, state2), F32),
                 ((rows, heads), F32), ((rows, model), BF)]
    message = ((inner + heads, width), F32)

    resid = own_piece(hidden_in, "head", 0).astype(F32)
    normed = None
    saved = []
    for l in range(layers):
        weights = (Far(w_z, l), Far(w_x, l), Far(w_bc, l), Far(w_dt, l))
        if l == 0:
            z, x, bc, dtp, nb = run(
                k_proj_first, proj_outs, hidden_in, norm_gain[l : l + 1], *weights, name="proj"
            )
        else:
            z, x, bc, dtp, nb = run(
                k_proj, proj_outs, *gather_pieces(normed, "head"), *weights, small=[place],
                name="proj",
            )
        edge = rotate(jnp.concatenate([x[rows - HALO :], bc[rows - HALO :]], 1), "seq", 1)
        ux, ubc, dts, cum, cumt, msg = run(
            functools.partial(k_front, l),
            [((rows, inner), F32), ((rows, state2), F32), ((rows, heads), F32),
             ((rows, heads), F32), ((heads, rows), F32), message],
            x, bc, dtp, edge, aux, conv_x_w[l], conv_x_b, conv_bc_w[l], conv_bc_b, dt_bias, a_log,
            scratch=(pltpu.VMEM((rows + HALO, inner), F32), pltpu.VMEM((rows + HALO, state2), F32)),
            name="front",
        )
        near, far, flag, _ = carried(msg, heads, False)
        (yp,) = run(
            functools.partial(k_intra, l), [((rows, inner), F32)],
            ux, ubc, dts, cum, cumt, segc, segr, d_skip, name="intra",
        )
        mixed, gated, ss, inc = run(
            k_gate,
            [((rows, inner), F32), ((rows, inner), F32), ((1, rows), F32), ((inner, width), F32)],
            yp, ubc, cum, aux, z, near, far, small=[flag], name="gate",
        )
        ss = lax.psum(ss, "head")
        gn, keep, send = run(
            functools.partial(k_out, l, inner_total),
            [((rows, inner), BF), half_rows, half_rows],
            gated, ss, gate_gain, Far(w_out, l), small=[place],
            scratch=(pltpu.VMEM((rows, inner), BF),), name="out",
        )
        keep, got = finish_scatter(keep, send, "head")
        saved.append((resid, z, x, bc, dtp, nb, edge, ux, ubc, dts, cum, cumt, inc, mixed, gated,
                      ss, gn))
        last = l + 1 == layers
        resid, normed = run(
            k_join, [quarter_rows, quarter_rows], resid, keep, got,
            norm_gain[0 if last else l + 1][None, :], flops=1000000, name="join",
        )
    (hidden_out,) = run(
        k_place, [((rows, model), BF)], *gather_pieces(resid, "head"), small=[place],
        flops=1000000, name="round",
    )

    def dw_scratch(cols):
        aligned = share % 128 == 0
        return (
            pltpu.VMEM((rows, model if aligned else 128), BF),
            pltpu.VMEM((8 if aligned else model, cols), F32),
        )

    cot = own_piece(out_cot, "head", 0)
    final = [[None] * layers for _ in range(4)]

    def product(order, left, rights, after, name="dw", bare=False):
        cols = sum(right.shape[1] for right in rights)
        keep, send = run(
            k_dw, [((model // 2, cols), F32)] * 2, left, *rights, small=[seq_places(order, share)],
            after=after, scratch=dw_scratch(cols), name=name,
        )
        return (keep, send) if bare else SeqScatter(order, keep, send)

    narrow_in = [None] * layers
    small = [None] * layers
    gains = [None] * layers
    waiting = []
    for l in reversed(range(layers)):
        (resid, z, x, bc, dtp, nb, edge, ux, ubc, dts, cum, cumt, inc, mixed, gated, ss,
         gn) = saved[l]
        b1_outs = [((rows, model), BF), ((rows, inner), F32), ((1, rows), F32), ((1, inner), F32)]
        if l + 1 == layers:
            cb, dgn, cross, ggain = run(
                functools.partial(k_b1_top, l, inner_total), b1_outs,
                out_cot, Far(w_out, l), gated, ss, gate_gain, name="b1",
            )
        else:
            cb, dgn, cross, ggain = run(
                functools.partial(k_b1, l, inner_total), b1_outs,
                *gather_pieces(cot, "head"), Far(w_out, l), gated, ss, gate_gain,
                small=[place], name="b1",
            )
        cross = lax.psum(cross, "head")
        dm, dz, msg = run(
            functools.partial(k_b2, l, inner_total),
            [((rows, inner), F32), ((rows, inner), BF), message],
            dgn, gated, mixed, z, ss, cross, gate_gain, ubc, cum, cumt, aux,
            name="b2",
        )
        near, far, flag, stages = carried(msg, heads, True)
        fresh = [
            product(orders[0], cb, [gn], stages[:1]),
            product(orders[1], nb, [dz], stages[1:2]),
        ]
        dx, dbc, dcum, ddt, gskip = run(
            functools.partial(k_b3, l),
            [((rows, inner), F32), ((rows, state2), F32), ((rows, heads), F32),
             ((rows, heads), F32), ((1, heads), F32)],
            dm, ux, ubc, dts, cum, cumt, segc, segr, mixed, inc, aux,
            d_skip, after=[fresh[0].keep], name="b3",
        )
        du, dub, dd, gdtb, galog, first_rows = run(
            functools.partial(k_b4, l),
            [((rows, inner), F32), ((rows, state2), F32), ((rows, heads), BF),
             ((1, heads), F32), ((1, heads), F32), ((HALO, inner + state2), F32)],
            ux, ubc, dts, dtp, cum, aux, dx, dbc, dcum, ddt, near, far,
            inc, dt_bias, a_log,
            small=[flag], after=[fresh[1].keep], scratch=(pltpu.VMEM((inner, width), F32),),
            name="b4",
        )
        halo = rotate(first_rows, "seq", -1)
        for pending in waiting[2:] + fresh:
            pending.advance([halo])
        dub = scatter_cols(jnp.concatenate([dub, halo[:, inner:]], 0), "head")
        quarter = dub.shape[1]
        dxb, gcw, gcb = run(
            k_conv_back,
            [((rows, inner), BF), ((taps, inner), F32), ((1, inner), F32)],
            du, halo[:, :inner], x, edge[:, :inner], aux, conv_x_w[l],
            scratch=(pltpu.VMEM((rows + HALO, inner), F32), pltpu.VMEM((rows + HALO, inner), F32)),
            name="convx",
        )
        dbw, gbw, gbb, dbb = run(
            k_conv_back_b,
            [((rows, state2), BF), ((taps, state2), F32), ((1, state2), F32), ((rows, quarter), BF)],
            dub, bc, edge[:, inner:], aux, conv_bc_w[l], small=[own_quarter],
            scratch=(pltpu.VMEM((rows + HALO, state2), F32),
                     pltpu.VMEM((rows + HALO, state2), F32)),
            name="convb",
        )
        keep, send = run(
            k_dnorm, [half_rows, half_rows],
            dz, dxb, dd, dbw, Far(w_z, l), Far(w_x, l), Far(w_dt, l), Far(w_bc, l), small=[place],
            scratch=(pltpu.VMEM((rows, model), F32), pltpu.VMEM((rows, model), F32)), name="dnorm",
        )
        ready = keep
        keep, got = finish_scatter(keep, send, "head")
        fresh += [
            product(orders[0], nb, [dxb[:, : inner // 2]], []),
            product(orders[1], nb, [dxb[:, inner // 2 :]], []),
        ]
        cot, gains[l] = run(
            k_norm_back, [quarter_rows, ((1, model), F32)],
            resid, keep, got, norm_gain[l : l + 1], cot,
            after=[pending.keep for pending in fresh[2:]], flops=1000000, name="normback",
        )
        for pending in fresh:
            pending.advance([cot])
        for slot in range(len(waiting)):
            final[slot][l + 1] = waiting[slot].result()
        waiting = fresh
        narrow_in[l] = (nb, dbb, dd)
        small[l] = (gcw, gcb, gbw, gbb, gdtb, galog, gskip, ggain)
    for pending in waiting[2:]:
        pending.advance([cot])
    for slot in range(len(waiting)):
        final[slot][0] = waiting[slot].result()
    (grad_in,) = run(
        k_place, [((rows, model), F32)], *gather_pieces(cot, "head"), small=[place],
        flops=1000000, name="place",
    )

    late = [seq_bits - 1] + list(range(seq_bits - 1))
    pairs = [product(late, n[0], n[1:], [ready], "dwn", True) for n in narrow_in]
    narrow = SeqScatter(
        late,
        jnp.concatenate([pair[0] for pair in pairs], 1),
        jnp.concatenate([pair[1] for pair in pairs], 1),
    ).result()
    narrow = jnp.stack(jnp.split(narrow, layers, 1))

    def reduced(flat, order):
        sizes = [part.size for part in flat]
        pack = jnp.concatenate([part.reshape(-1) for part in flat])
        pack = jnp.pad(pack, (0, -pack.size % 1024)).reshape(-1, 128)
        pack = seq_sum(pack, order).reshape(-1)
        pieces, start = [], 0
        for count in sizes:
            pieces.append(pack[start : start + count])
            start += count
        return pieces

    pieces = reduced([part for l in range(layers) for part in small[l]] + gains, late)
    count = len(small[0])

    def both(slot):
        return jnp.stack([pieces[l * count + slot].reshape(small[l][slot].shape) for l in range(layers)])

    wide = jnp.concatenate(
        pieces[layers * count :] + [both(2).reshape(-1), both(3).reshape(-1)]
    )
    wide = head_sum(wide.reshape(-1, 128)).reshape(-1)
    stop = layers * model
    grad_gain = wide[:stop].reshape(layers, model)
    grad_gain = lax.dynamic_slice_in_dim(grad_gain, lax.axis_index("seq") * share, share, 1)
    bc_w = wide[stop : stop + layers * taps * state2].reshape(layers, taps, state2)
    bc_b = wide[stop + layers * taps * state2 :].reshape(layers, state2)
    bc_parts = gather_back(narrow[:, :, :quarter], "head", 2)
    return (
        hidden_out,
        grad_in,
        grad_gain,
        jnp.stack(final[1]),
        jnp.stack([jnp.concatenate(pair, 1) for pair in zip(final[2], final[3])]),
        bc_parts,
        narrow[:, :, quarter:],
        both(0),
        both(1)[:, 0],
        bc_w,
        bc_b,
        both(4)[:, 0],
        both(5)[:, 0],
        both(6)[:, 0],
        both(7)[:, 0],
        jnp.stack([part.T for part in final[0]]),
    )


def solution(mesh):
    return jax.shard_map(
        local,
        mesh=mesh,
        in_specs=(
            P("seq", None),
            P(),
            P(),
            P(None, None, "head"),
            P(None, None, "head"),
            P(),
            P(None, None, "head"),
            P(None, None, "head"),
            P(None, "head"),
            P(),
            P(),
            P(None, "head"),
            P(None, "head"),
            P(None, "head"),
            P(None, "head"),
            P(None, "head", None),
            P("seq", None),
        ),
        out_specs=(
            P("seq", None),
            P("seq", None),
            P(None, "seq"),
            P(None, "seq", "head"),
            P(None, "seq", "head"),
            P(None, "seq", None),
            P(None, "seq", "head"),
            P(None, None, "head"),
            P(None, "head"),
            P(),
            P(),
            P(None, "head"),
            P(None, "head"),
            P(None, "head"),
            P(None, "head"),
            P(None, "head", "seq"),
        ),
        check_vma=False,
    )
```
